32 devices in a mesh: seq: 2 (over y), head: 4 (over x, core), ctx: 4 (over z).
Axes of the slice: x: 2, y: 2, z: 4, core: 2. Of those that a mesh axis runs over, the one named last changes fastest.
Arguments:
- tokens: bfloat16 [16384, 768], P(('seq', 'head', 'ctx')), may hold values from -6 to 6
- segment_ids: int32 [16384], P(('seq', 'head', 'ctx')), may hold values from -1 to 3, as said below
- w_qkv: bfloat16 [768, 2304], P(('seq', 'head', 'ctx')), may hold values from -0.21875 to 0.21875
- w_out: bfloat16 [768, 768], P(('seq', 'head', 'ctx')), may hold values from -6 to 6
- w_up: bfloat16 [768, 3072], P(('seq', 'head', 'ctx')), may hold values from -0.21875 to 0.21875
- w_down: bfloat16 [3072, 768], P(('seq', 'head', 'ctx')), may hold values from -0.109375 to 0.109375
- gain_one: bfloat16 [768], P(('seq', 'head', 'ctx')), may hold values from 0.5 to 1.5
- bias_one: bfloat16 [768], P(('seq', 'head', 'ctx')), may hold values from -3 to 3
- gain_two: bfloat16 [768], P(('seq', 'head', 'ctx')), may hold values from 0.5 to 1.5
- bias_two: bfloat16 [768], P(('seq', 'head', 'ctx')), may hold values from -3 to 3
- cotangent: bfloat16 [16384, 768], P(('seq', 'head', 'ctx')), may hold values from -6 to 6
Outputs:
- output: bfloat16 [16384, 768], P(('seq', 'head', 'ctx'))
- grad_tokens: bfloat16 [16384, 768], P(('seq', 'head', 'ctx'))
- grad_w_qkv: float32 [768, 2304], P(('seq', 'head', 'ctx'))
- grad_w_out: float32 [768, 768], P(('seq', 'head', 'ctx'))
- grad_w_up: float32 [768, 3072], P(('seq', 'head', 'ctx'))
- grad_w_down: float32 [3072, 768], P(('seq', 'head', 'ctx'))
- grad_gain_one: float32 [768], P(('seq', 'head', 'ctx'))
- grad_bias_one: float32 [768], P(('seq', 'head', 'ctx'))
- grad_gain_two: float32 [768], P(('seq', 'head', 'ctx'))
- grad_bias_two: float32 [768], P(('seq', 'head', 'ctx'))
The draws below stay inside these ranges and needn't reach their ends.
Inputs may be any that keep to these rules, and one draw needn't show every extreme that they name: `segment_ids`: within each sequence of 8192 tokens the ids start at 0 and never fall before the trailing padding; a scene is made of whole views of 1024 tokens (the last one possibly cut by the padding) and has at most 5 views; the padding is a tail of 1 to min(512, 1023) tokens of each sequence.
All inputs are finite; a program needn't handle non-finite values.
Results may differ from the reference program's by a relative error of at most 0.023.
Values may be sent and summed in bfloat16 or wider, within the bound.
No kernel may reach another device: no remote copies, remote signals or barrier semaphores. Data moves between devices by JAX's collectives and lax.ppermute only.
A program may use at most 192 MiB of HBM per device.

```python
from functools import partial
import jax
import jax.numpy as jnp
from jax import lax

D = 768
HEADS = 12
HDIM = 64
FF = 3072
TOK_DEV = 512
VIEW = 1024
SEQLEN = 8192
SEQS = 2
TOKENS = 16384


def draw_segment_ids(key, part):
    key_flags, key_pad = jax.random.split(jax.random.fold_in(key, 7))
    view_count = (SEQLEN + VIEW - 1) // VIEW
    first_scene = min(5, view_count)
    flags = jax.random.randint(key_flags, (SEQS, view_count), 0, 2)
    flags = jnp.where(jnp.arange(SEQS)[:, None] == 0, 1, flags)
    view_pos = jnp.arange(view_count)[None, :]
    starts = jnp.where(view_pos < first_scene, 0, jnp.where((view_pos - first_scene) % 3 == 0, 1, flags))
    scenes = jnp.cumsum(starts, axis=1)
    per_token = jnp.repeat(scenes, VIEW, axis=1)[:, :SEQLEN]
    pad_len = jax.random.randint(key_pad, (SEQS, 1), 1, min(TOK_DEV, VIEW - 1) + 1)
    token_pos = jnp.arange(SEQLEN)[None, :]
    labelled = jnp.where(token_pos >= SEQLEN - pad_len, -1, per_token)
    return labelled.reshape(TOKENS).astype(jnp.int32)


def steps_of(stream_key, shape, cuts, low, high):
    level = 1.0
    for axis_at, blocks in cuts:
        heights = jax.random.uniform(jax.random.fold_in(jax.random.fold_in(stream_key, 6), axis_at), (blocks,), jnp.float32, low / len(cuts), high / len(cuts))
        level = level * jnp.repeat(jnp.exp(heights), shape[axis_at] // blocks).reshape((-1,) + (1,) * (len(shape) - 1 - axis_at))
    return level


def noise(own_key, dims, width, limit, shards=(), dtype=jnp.bfloat16):
    values = width * jax.random.normal(own_key, dims, jnp.float32)
    if shards:
        values = values * steps_of(own_key, dims, shards, -0.22, 0.18)
    return jnp.clip(values, -limit, limit).astype(dtype)


def setup_inputs(seed: int = 0) -> dict:
    streams_of = jax.random.split(jax.random.key(seed), 12)
    return {
        "tokens": noise(streams_of[0], (TOKENS, D), 1.0, 6.0, ((0, 32),)),
        "segment_ids": draw_segment_ids(jax.random.fold_in(streams_of[11], 71), 0),
        "w_qkv": noise(streams_of[2], (D, 3 * D), D ** -0.5, 0.21875, ((0, 32),)),
        "w_out": noise(streams_of[3], (D, D), 1 ** -0.5, 6.0, ((0, 32),)),
        "w_up": noise(streams_of[4], (D, FF), D ** -0.5, 0.21875, ((0, 32),)),
        "w_down": noise(streams_of[5], (FF, D), FF ** -0.5, 0.109375, ((0, 32),)),
        "gain_one": jnp.clip(1.0 + 0.1 * jax.random.normal(streams_of[6], (D,), jnp.float32), 0.5, 1.5).astype(jnp.bfloat16),
        "bias_one": noise(streams_of[7], (D,), 0.5, 3.0, ((0, 32),)),
        "gain_two": jnp.clip(1.0 + 0.1 * jax.random.normal(streams_of[8], (D,), jnp.float32), 0.5, 1.5).astype(jnp.bfloat16),
        "bias_two": noise(streams_of[9], (D,), 0.5, 3.0, ((0, 32),)),
        "cotangent": noise(streams_of[10], (TOKENS, D), 1.0, 6.0, ((0, 32),)),
    }


@jax.custom_vjp
def low(v):
    return lax.optimization_barrier(v.astype(jnp.bfloat16)).astype(jnp.float32)

@jax.custom_vjp
def low_back(v):
    return v

def low_keep(v):
    return (low(v), None)

def low_pass(kept, grad):
    return (grad,)

def back_keep(v):
    return (v, None)

def back_low(kept, grad):
    return (low(grad),)
low.defvjp(low_keep, low_pass)
low_back.defvjp(back_keep, back_low)
EPSILON = 1e-05
MASKED = -1e+30
HIGHEST = lax.Precision.HIGHEST

def norm_layer(values, gain_vec, bias_vec):
    row_mean = lax.optimization_barrier(jnp.mean(values, axis=-1, keepdims=True))
    centered = values - row_mean
    variance = lax.optimization_barrier(jnp.mean(centered * centered, axis=-1, keepdims=True))
    return centered * lax.rsqrt(variance + EPSILON) * gain_vec + bias_vec

def product(left, right):
    return jnp.dot(left, right, precision=HIGHEST)

def attend_block(keys, values, key_ids, query_pack):
    queries, query_ids = query_pack
    score_scale = HDIM ** (-0.5)
    scores = jnp.einsum('qhd,khd->hqk', queries, keys, precision=HIGHEST) * score_scale
    scores = low_back(scores)
    same_scene = query_ids[None, :, None] == key_ids[None, None, :]
    scores = jnp.where(same_scene, scores, MASKED)
    row_max = lax.optimization_barrier(jnp.max(scores, axis=-1, keepdims=True))
    weights = jnp.exp(scores - row_max)
    probs = low(weights / lax.optimization_barrier(jnp.sum(weights, axis=-1, keepdims=True)))
    return jnp.einsum('hqk,khd->qhd', probs, values, precision=HIGHEST)

def sequence_attention(packed):
    queries, keys, values, seq_ids = packed
    length = queries.shape[0]
    block_rows = min(512, length)
    blocks = (queries.reshape(length // block_rows, block_rows, HEADS, HDIM), seq_ids.reshape(length // block_rows, block_rows))
    result = lax.map(jax.checkpoint(partial(attend_block, keys, values, seq_ids)), blocks)
    return result.reshape(length, HEADS, HDIM)

def layer_forward(seg_ids, inputs, w_qkv, w_out, w_up, w_down, gain_one, bias_one, gain_two, bias_two):
    h_one = low(norm_layer(inputs, gain_one, bias_one))
    qkv = low(low_back(product(h_one, w_qkv))).reshape(SEQS, SEQLEN, HEADS, 3, HDIM)
    attended = lax.map(sequence_attention, (qkv[:, :, :, 0], qkv[:, :, :, 1], qkv[:, :, :, 2], seg_ids.reshape(SEQS, SEQLEN)))
    merged = low(low_back(attended.reshape(TOKENS, D)))
    y_one = inputs + low_back(product(merged, w_out))
    h_two = low(norm_layer(y_one, gain_two, bias_two))
    up_proj = low_back(product(h_two, w_up))
    hidden = low(jax.nn.gelu(up_proj, approximate=False))
    return y_one + product(hidden, w_down)

def reference(tokens, segment_ids, w_qkv, w_out, w_up, w_down, gain_one, bias_one, gain_two, bias_two, cotangent):
    forward_fn = partial(layer_forward, segment_ids)
    result, pullback = jax.vjp(forward_fn, tokens.astype(jnp.float32), w_qkv.astype(jnp.float32), w_out.astype(jnp.float32), w_up.astype(jnp.float32), w_down.astype(jnp.float32), gain_one.astype(jnp.float32), bias_one.astype(jnp.float32), gain_two.astype(jnp.float32), bias_two.astype(jnp.float32))
    grads = pullback(cotangent.astype(jnp.float32))
    return (result.astype(jnp.bfloat16), grads[0].astype(jnp.bfloat16), grads[1], grads[2], grads[3], grads[4], grads[5], grads[6], grads[7], grads[8])
```

```python
from functools import partial

import jax
import jax.numpy as jnp
from jax import lax
from jax.experimental import pallas as pl
from jax.experimental.pallas import tpu as pltpu
from jax.sharding import PartitionSpec as P

D = 768
HEADS = 12
HDIM = 64
BLOCK = 512
LANES = 128
EPSILON = 1e-05
MASKED = -1e30
LOG2E = 1.4426950408889634
LN2 = 0.6931471805599453
ALL_AXES = ("seq", "head", "ctx")
BF16 = jnp.bfloat16
F32 = jnp.float32


def dot_on(left, right, left_dim, right_dim):
    return lax.dot_general(
        left, right, (((left_dim,), (right_dim,)), ((), ())), preferred_element_type=F32
    )


def norm_rows(values, gain_vec, bias_vec):
    row_mean = jnp.mean(values, axis=-1, keepdims=True)
    centered = values - row_mean
    variance = jnp.mean(centered * centered, axis=-1, keepdims=True)
    inv_rows = lax.rsqrt(variance + EPSILON)
    unit_rows = centered * inv_rows
    return (unit_rows * gain_vec + bias_vec, unit_rows, inv_rows)


def norm_back(grad_norm, unit_rows, inv_rows, gain_vec):
    scaled = grad_norm * gain_vec
    return inv_rows * (
        scaled
        - jnp.mean(scaled, axis=-1, keepdims=True)
        - unit_rows * jnp.mean(scaled * unit_rows, axis=-1, keepdims=True)
    )


def gelu_exact(values):
    return jax.nn.gelu(values, approximate=False)


def swap_head(value, mask):
    count = lax.axis_size("head")
    return lax.ppermute(value, "head", [(i, i ^ mask) for i in range(count)])


def ring_order(count):
    return [0, 1, 3, 2] if count == 4 else list(range(count))


def ring_pairs(count, step):
    order = ring_order(count)
    return [(order[i], order[(i + step) % count]) for i in range(count)]


def ring_send(value, step):
    return lax.ppermute(value, "ctx", ring_pairs(lax.axis_size("ctx"), step))


def plane_blocks(block):
    near = swap_head(block, 2)
    return [block, swap_head(block, 1), near, swap_head(near, 1)]


def split_three(values):
    high = values.astype(BF16)
    rest = values - high.astype(F32)
    middle = rest.astype(BF16)
    low = (rest - middle.astype(F32)).astype(BF16)
    return [high.astype(F32), middle.astype(F32), low.astype(F32)]


def key_marks(valid, lane):
    row = lax.broadcasted_iota(jnp.int32, (BLOCK, LANES), 0)
    real = row < valid
    marks = jnp.where((lane >= 64) & (lane < 67), 1.0, 0.0)
    marks = jnp.where((lane == 67) & jnp.logical_not(real), MASKED, marks)
    return jnp.where((lane == 68) & real, MASKED, marks)


def fill_keys(slots, kv_ref, valid_ref, keys_out, values_t=None, values_out=None):
    lane = lax.broadcasted_iota(jnp.int32, (BLOCK, LANES), 1)

    def fill(slot, carry):
        rows = pl.ds(pl.multiple_of(slot * BLOCK, BLOCK), BLOCK)
        marks = key_marks(valid_ref[slot], lane)
        for head in range(3):
            pair = kv_ref[rows, head * LANES : (head + 1) * LANES].astype(F32)
            keys_out[head, rows, :] = jnp.where(lane < 64, pair, marks).astype(BF16)
            if values_out is not None:
                ones = jnp.where(lane < 3, 1.0, 0.0)
                values_out[head, rows, :] = jnp.where(lane < 64, ones, pair).astype(BF16)
            if values_t is not None:
                turned = pair.T[64:128].astype(BF16)
                values_t[head, :, rows] = jnp.concatenate(
                    [turned, jnp.ones((16, BLOCK), BF16)], axis=0
                )
        return carry

    lax.fori_loop(0, slots, fill, 0)


def query_marks(valid, width):
    row = lax.broadcasted_iota(jnp.int32, (1, width), 1)
    real = jnp.where(row < valid, 1.0, 0.0)
    return [real, 1.0 - real]


def forward_kernel(
    slots, count_ref, list_ref, valid_ref, q_ref, kv_ref, out_ref, lse_ref, keys, values_t, q_ext, acc, top, total
):
    fill_keys(slots, kv_ref, valid_ref, keys, values_t=values_t)

    def over_queries(block, carry):
        q_rows = pl.ds(pl.multiple_of(block * BLOCK, BLOCK), BLOCK)
        lane = lax.broadcasted_iota(jnp.int32, (BLOCK, LANES), 1)
        row = lax.broadcasted_iota(jnp.int32, (BLOCK, LANES), 0)
        real = row < valid_ref[block]
        marks = jnp.where((lane == 67) & real, 1.0, 0.0)
        marks = jnp.where((lane == 68) & jnp.logical_not(real), 1.0, marks)
        for head in range(3):
            own = q_ref[q_rows, head * LANES : (head + 1) * LANES].astype(F32)
            q_ext[head] = jnp.where(lane < 64, own, marks).astype(BF16)
            acc[head] = jnp.zeros(acc.shape[1:], F32)

        def scores_of(slot, head):
            rows = pl.ds(pl.multiple_of(slot * BLOCK, BLOCK), BLOCK)
            return dot_on(keys[head, rows, :], q_ext[head], 1, 1)

        def over_keys(item, carry_in):
            slot = list_ref[block, item]
            rows = pl.ds(pl.multiple_of(slot * BLOCK, BLOCK), BLOCK)
            ready = [scores_of(slot, 0), scores_of(slot, 1)]
            for head in range(3):
                if head == 0:
                    ready.append(scores_of(slot, 2))
                weights = jnp.exp2(ready.pop(0)).astype(BF16)
                acc[head] += dot_on(values_t[head, :, rows], weights, 1, 0)
            return carry_in

        lax.fori_loop(0, count_ref[block], over_keys, 0)
        safe = jnp.bool_(True)
        for head in range(3):
            sums = acc[head, 64:65, :]
            good = (sums >= 2.0**-60) & (sums <= 2.0**100)
            safe = safe & (jnp.min(jnp.where(good, 1.0, 0.0)) > 0.5)
        for head in range(3):
            top[head] = jnp.zeros((1, BLOCK), F32)

        @pl.when(jnp.logical_not(safe))
        def _():
            for head in range(3):
                top[head] = jnp.full((1, BLOCK), MASKED, F32)
                acc[head] = jnp.zeros(acc.shape[1:], F32)

            def with_max(item, carry_in):
                slot = list_ref[block, item]
                rows = pl.ds(pl.multiple_of(slot * BLOCK, BLOCK), BLOCK)
                for head in range(3):
                    scores = scores_of(slot, head)
                    before = top[head]
                    after = jnp.maximum(before, jnp.max(scores, axis=0, keepdims=True))
                    weights = jnp.exp2(scores - after).astype(BF16)
                    top[head] = after
                    acc[head] = acc[head] * jnp.exp2(before - after) + dot_on(
                        values_t[head, :, rows], weights, 1, 0
                    )
                return carry_in

            lax.fori_loop(0, count_ref[block], with_max, 0)

        for head in range(3):
            sums = acc[head, 64:65, :]
            out_ref[head, :, q_rows] = (acc[head, 0:64, :] / sums).astype(BF16)
            lse_ref[head, :, q_rows] = top[head] + jnp.log2(sums)
        return carry

    lax.fori_loop(0, 4, over_queries, 0)


def attend_forward(counts, lists, valid, queries, key_vals):
    q_rows, kv_rows = queries.shape[0], key_vals.shape[0]
    slots = kv_rows // BLOCK
    smem = pl.BlockSpec(memory_space=pltpu.SMEM)
    vmem = pl.BlockSpec(memory_space=pltpu.VMEM)
    return pl.pallas_call(
        partial(forward_kernel, slots),
        out_shape=(
            jax.ShapeDtypeStruct((3, HDIM, q_rows), BF16),
            jax.ShapeDtypeStruct((3, 1, q_rows), F32),
        ),
        in_specs=[smem, smem, smem, vmem, vmem],
        out_specs=(vmem, vmem),
        scratch_shapes=[
            pltpu.VMEM((3, kv_rows, LANES), BF16),
            pltpu.VMEM((3, 80, kv_rows), BF16),
            pltpu.VMEM((3, BLOCK, LANES), BF16),
            pltpu.VMEM((3, 80, BLOCK), F32),
            pltpu.VMEM((3, 1, BLOCK), F32),
            pltpu.VMEM((3, 1, BLOCK), F32),
        ],
        compiler_params=pltpu.CompilerParams(vmem_limit_bytes=48 << 20),
        cost_estimate=pl.CostEstimate(
            flops=4 * 108 * BLOCK * BLOCK * 256, bytes_accessed=10 << 20, transcendentals=28 << 20
        ),
        name="attend_forward",
    )(counts, lists, valid, queries, key_vals)


def backward_kernel(
    slots,
    count_ref,
    list_ref,
    valid_ref,
    q_ref,
    kv_ref,
    out_ref,
    lse_ref,
    grad_ref,
    dq_ref,
    dkv_ref,
    keys,
    values,
    q_ext,
    g_ext,
    q_turned,
    dq_acc,
    dkv_acc,
):
    fill_keys(slots, kv_ref, valid_ref, keys, values_out=values)

    def clear(slot, carry):
        rows = pl.ds(pl.multiple_of(slot * BLOCK, BLOCK), BLOCK)
        for head in range(3):
            dkv_acc[head, :, rows] = jnp.zeros((LANES, BLOCK), F32)
        return carry

    lax.fori_loop(0, slots, clear, 0)

    def over_queries(block, carry):
        q_rows = pl.ds(pl.multiple_of(block * BLOCK, BLOCK), BLOCK)
        for head in range(3):
            turned = q_ref[q_rows, head * LANES : (head + 1) * LANES].astype(F32).T[0:64]
            grad_t = grad_ref[head, :, q_rows].astype(F32)
            delta = jnp.sum(grad_t * out_ref[head, :, q_rows].astype(F32), axis=0, keepdims=True)
            marks = split_three(-lse_ref[head, :, q_rows]) + query_marks(valid_ref[block], BLOCK)
            blank = jnp.zeros((64 - len(marks), BLOCK), F32)
            q_turned[head] = turned.astype(BF16)
            q_ext[head] = jnp.concatenate([turned] + marks + [blank], axis=0).T.astype(BF16)
            minus = split_three(-delta)
            blank = jnp.zeros((64 - len(minus), BLOCK), F32)
            g_ext[head] = jnp.concatenate(minus + [blank, grad_t], axis=0).T.astype(BF16)
            dq_acc[head] = jnp.zeros((BLOCK, LANES), F32)

        def over_keys(item, carry_in):
            slot = list_ref[block, item]
            rows = pl.ds(pl.multiple_of(slot * BLOCK, BLOCK), BLOCK)

            def products(head):
                return (
                    dot_on(q_ext[head], keys[head, rows, :], 1, 1),
                    dot_on(g_ext[head], values[head, rows, :], 1, 1),
                )

            ready = [products(0)]
            for head in range(3):
                if head < 2:
                    ready.append(products(head + 1))
                scores, grad_probs = ready.pop(0)
                probs = jnp.exp2(scores)
                grad_scores = (probs * grad_probs).astype(BF16)
                dkv_acc[head, 64:128, rows] += dot_on(
                    grad_ref[head, :, q_rows], probs.astype(BF16), 1, 0
                )
                dkv_acc[head, 0:64, rows] += dot_on(q_turned[head], grad_scores, 1, 0)
                dq_acc[head] += dot_on(grad_scores, keys[head, rows, :], 1, 0)
            return carry_in

        lax.fori_loop(0, count_ref[block], over_keys, 0)
        lane = lax.broadcasted_iota(jnp.int32, (BLOCK, LANES), 1)
        for head in range(3):
            dq_ref[q_rows, head * LANES : (head + 1) * LANES] = jnp.where(
                lane < 64, dq_acc[head] * HDIM ** (-0.5), 0.0
            ).astype(BF16)
        return carry

    lax.fori_loop(0, 4, over_queries, 0)

    def finish(slot, carry):
        rows = pl.ds(pl.multiple_of(slot * BLOCK, BLOCK), BLOCK)
        for head in range(3):
            dkv_ref[head, 0:64, rows] = (dkv_acc[head, 0:64, rows] * LN2).astype(BF16)
            dkv_ref[head, 64:128, rows] = dkv_acc[head, 64:128, rows].astype(BF16)
        return carry

    lax.fori_loop(0, slots, finish, 0)


def attend_backward(counts, lists, valid, queries, key_vals, attended, lse, grads):
    q_rows, kv_rows = queries.shape[0], key_vals.shape[0]
    slots = kv_rows // BLOCK
    smem = pl.BlockSpec(memory_space=pltpu.SMEM)
    vmem = pl.BlockSpec(memory_space=pltpu.VMEM)
    return pl.pallas_call(
        partial(backward_kernel, slots),
        out_shape=(
            jax.ShapeDtypeStruct((q_rows, 3 * LANES), BF16),
            jax.ShapeDtypeStruct((3, LANES, kv_rows), BF16),
        ),
        in_specs=[smem] * 3 + [vmem] * 5,
        out_specs=(vmem, vmem),
        scratch_shapes=[
            pltpu.VMEM((3, kv_rows, LANES), BF16),
            pltpu.VMEM((3, kv_rows, LANES), BF16),
            pltpu.VMEM((3, BLOCK, LANES), BF16),
            pltpu.VMEM((3, BLOCK, LANES), BF16),
            pltpu.VMEM((3, HDIM, BLOCK), BF16),
            pltpu.VMEM((3, BLOCK, LANES), F32),
            pltpu.VMEM((3, LANES, kv_rows), F32),
        ],
        compiler_params=pltpu.CompilerParams(vmem_limit_bytes=58 << 20),
        cost_estimate=pl.CostEstimate(
            flops=10 * 108 * BLOCK * BLOCK * 256, bytes_accessed=20 << 20, transcendentals=28 << 20
        ),
        name="attend_backward",
    )(counts, lists, valid, queries, key_vals, attended, lse, grads)


def scene_lists(segment_ids, slots_ids, slots_valid):
    same = slots_ids[:4, None] == slots_ids[None, :]
    counts = jnp.sum(same, axis=1).astype(jnp.int32)
    number = slots_ids.shape[0]
    earlier = jnp.arange(number)[None, :] < jnp.arange(number)[:, None]
    place = jnp.sum(same[:, None, :] & earlier[None], axis=2)
    hits = same[:, None, :] & (place[:, None, :] == jnp.arange(number)[None, :, None])
    lists = jnp.sum(jnp.where(hits, jnp.arange(number)[None, None, :], 0), axis=2)
    return counts, lists.astype(jnp.int32)


def body(
    tokens,
    segment_ids,
    w_qkv,
    w_out,
    w_up,
    w_down,
    gain_one,
    bias_one,
    gain_two,
    bias_two,
    cotangent,
):
    heads_ax = lax.axis_size("head")
    ctx_ax = lax.axis_size("ctx")
    me_head = lax.axis_index("head")
    tok_rows = tokens.shape[0]
    group = D // heads_ax
    shard = w_qkv.shape[0]

    ring = [tokens]
    for _ in range(ctx_ax - 1):
        ring.append(ring_send(ring[-1], 1))
    planes = [plane_blocks(block) for block in ring]

    norms = jnp.stack([gain_one, bias_one, gain_two, bias_two], axis=1)
    packed = jnp.concatenate([w_qkv, jnp.pad(norms, ((0, 0), (0, LANES - 4)))], axis=1)
    packed = lax.all_gather(packed, ALL_AXES, axis=0, tiled=True)
    full_qkv = packed[:, : 3 * D]
    g_one, b_one, g_two, b_two = [packed[:, 3 * D + i].astype(F32) for i in range(4)]
    full_out = lax.all_gather(w_out, ALL_AXES, axis=0, tiled=True)
    full_up = lax.all_gather(w_up, ALL_AXES, axis=0, tiled=True)
    full_down = lax.all_gather(w_down, ALL_AXES, axis=0, tiled=True)

    about = jnp.stack([segment_ids[0], jnp.sum(segment_ids >= 0).astype(jnp.int32)])
    about = jnp.broadcast_to(about[:, None], (2, LANES))
    ring_about = [about]
    for _ in range(ctx_ax - 1):
        ring_about.append(ring_send(ring_about[-1], 1))
    about_all = jnp.stack([b[:, 0] for r in ring_about for b in plane_blocks(r)])
    slot_ids, slot_valid = about_all[:, 0], about_all[:, 1]
    counts, lists = scene_lists(segment_ids, slot_ids, slot_valid)

    w_mine = lax.dynamic_slice_in_dim(full_qkv, me_head * 3 * group, 3 * group, axis=1)
    w_mine = w_mine.reshape(D, 3, 3, HDIM)
    w_kv = w_mine[:, :, 1:].reshape(D, 6 * HDIM)
    w_q = jnp.pad(w_mine[:, :, :1], ((0, 0), (0, 0), (0, 1), (0, 0))).reshape(D, 6 * HDIM)

    x_all = jnp.concatenate([b for plane in planes for b in plane], axis=0).astype(F32)
    normed, ignored, ignored_too = norm_rows(x_all, g_one, b_one)
    h_all = normed.astype(BF16)
    key_vals = jnp.dot(h_all, w_kv, preferred_element_type=F32).astype(BF16)
    h_plane = h_all[: heads_ax * tok_rows]
    queries = jnp.dot(h_plane, w_q, preferred_element_type=F32) * (HDIM ** (-0.5) * LOG2E)
    queries = queries.astype(BF16)

    attended, lse = attend_forward(counts, lists, slot_valid, queries, key_vals)

    parts = []
    for j in range(heads_ax):
        part = attended[:, :, j * tok_rows : (j + 1) * tok_rows].reshape(group, tok_rows)
        parts.append(swap_head(part, j) if j else part)
    merged_t = jnp.concatenate(parts, axis=0)
    order = [me_head ^ j for j in range(heads_ax)]
    out_groups = full_out.reshape(heads_ax, group, D)
    out_mine = jnp.concatenate(
        [lax.dynamic_index_in_dim(out_groups, o, 0, keepdims=False) for o in order], axis=0
    )

    inputs = tokens.astype(F32)
    y_one = inputs + jnp.einsum("at,ad->td", merged_t, out_mine, preferred_element_type=F32)
    normed_two, unit_two, inv_two = norm_rows(y_one, g_two, b_two)
    h_two = normed_two.astype(BF16)
    up_proj = jnp.dot(h_two, full_up, preferred_element_type=F32)
    hidden = gelu_exact(up_proj).astype(BF16)
    output = (y_one + jnp.dot(hidden, full_down, preferred_element_type=F32)).astype(BF16)
    grad_w_down = jnp.einsum("tf,td->fd", hidden, cotangent, preferred_element_type=F32)
    grad_hidden = jnp.einsum("td,fd->tf", cotangent, full_down, preferred_element_type=F32)
    grad_up = jax.vjp(gelu_exact, up_proj)[1](grad_hidden)[0].astype(BF16)
    grad_w_up = jnp.einsum("td,tf->df", h_two, grad_up, preferred_element_type=F32)
    grad_h_two = jnp.einsum("tf,df->td", grad_up, full_up, preferred_element_type=F32)
    grad_gain_two = jnp.sum(grad_h_two * unit_two, axis=0)
    grad_bias_two = jnp.sum(grad_h_two, axis=0)
    grad_y_one = cotangent.astype(F32) + norm_back(grad_h_two, unit_two, inv_two, g_two)
    grad_z = grad_y_one.astype(BF16)
    grad_w_out = jnp.einsum("at,td->ad", merged_t, grad_z, preferred_element_type=F32)
    grad_merged = jnp.einsum("td,ad->at", grad_z, out_mine, preferred_element_type=F32)
    grad_merged = grad_merged.astype(BF16)

    grad_parts = []
    for j in range(heads_ax):
        part = grad_merged[j * group : (j + 1) * group]
        grad_parts.append(swap_head(part, j) if j else part)
    grad_local = jnp.concatenate(grad_parts, axis=1).reshape(3, HDIM, heads_ax * tok_rows)

    d_query, d_kv = attend_backward(
        counts, lists, slot_valid, queries, key_vals, attended, lse, grad_local
    )
    d_kv = d_kv.reshape(6 * HDIM, heads_ax * ctx_ax * tok_rows)

    grad_h = jnp.einsum("ct,dc->td", d_kv, w_kv, preferred_element_type=F32)
    grad_h_q = jnp.einsum("tc,dc->td", d_query, w_q, preferred_element_type=F32)
    grad_h = grad_h.reshape(ctx_ax, heads_ax, tok_rows, D)
    grad_h_q = grad_h_q.reshape(heads_ax, tok_rows, D)
    traveling = None
    for r in reversed(range(ctx_ax)):
        term = grad_h[r]
        if r == 0:
            term = term + grad_h_q
        low = term.astype(BF16)
        by_x = [
            term[2 * i] + swap_head(low[2 * i + 1], 1).astype(F32) for i in range(2)
        ]
        own = by_x[0] + swap_head(by_x[1].astype(BF16), 2).astype(F32)
        if traveling is not None:
            own = own + ring_send(traveling.astype(BF16), -1).astype(F32)
        traveling = own
    grad_h_one = traveling

    grad_w_kv = jnp.einsum("td,ct->dc", h_all, d_kv, preferred_element_type=F32)
    grad_w_q = jnp.einsum("td,tc->dc", h_plane, d_query, preferred_element_type=F32)
    grad_w_mine = jnp.concatenate(
        [
            grad_w_q.reshape(D, 3, 2, HDIM)[:, :, :1],
            grad_w_kv.reshape(D, 3, 2, HDIM),
        ],
        axis=2,
    ).reshape(-1, heads_ax, ctx_ax, shard, 3 * group)
    grad_w_mine = jnp.swapaxes(grad_w_mine, 1, 2).reshape(D, 3 * group).astype(BF16)
    grad_w_mine = lax.psum_scatter(
        grad_w_mine, ("seq", "ctx"), scatter_dimension=0, tiled=True
    )
    grad_w_qkv = lax.all_to_all(
        grad_w_mine.reshape(heads_ax, shard, 3 * group),
        "head",
        split_axis=0,
        concat_axis=2,
        tiled=True,
    ).reshape(shard, 3 * D).astype(F32)

    normed_one, unit_one, inv_one = norm_rows(inputs, g_one, b_one)
    grad_gain_one = jnp.sum(grad_h_one * unit_one, axis=0)
    grad_bias_one = jnp.sum(grad_h_one, axis=0)
    grad_tokens = (grad_y_one + norm_back(grad_h_one, unit_one, inv_one, g_one)).astype(BF16)

    grad_out_groups = grad_w_out.reshape(heads_ax, group, D)
    grad_w_out = jnp.concatenate(
        [lax.dynamic_index_in_dim(grad_out_groups, o, 0, keepdims=False) for o in order], axis=0
    )
    scatter = partial(lax.psum_scatter, axis_name=ALL_AXES, scatter_dimension=0, tiled=True)
    return (
        output,
        grad_tokens,
        grad_w_qkv,
        scatter(grad_w_out.astype(BF16)).astype(F32),
        scatter(grad_w_up.astype(BF16)).astype(F32),
        scatter(grad_w_down.astype(BF16)).astype(F32),
        scatter(grad_gain_one),
        scatter(grad_bias_one),
        scatter(grad_gain_two),
        scatter(grad_bias_two),
    )


def solution(mesh):
    rows = P(ALL_AXES, None)
    vector = P(ALL_AXES)
    return jax.shard_map(
        body,
        mesh=mesh,
        in_specs=(rows, vector, rows, rows, rows, rows, vector, vector, vector, vector, rows),
        out_specs=(rows, rows, rows, rows, rows, rows, vector, vector, vector, vector),
        check_vma=False,
    )
```

```python
from functools import partial

import jax
import jax.numpy as jnp
from jax import lax
from jax.experimental import pallas as pl
from jax.experimental.pallas import tpu as pltpu
from jax.sharding import PartitionSpec as P

D = 768
HEADS = 12
HDIM = 64
BLOCK = 512
LANES = 128
EPSILON = 1e-05
MASKED = -1e30
LOG2E = 1.4426950408889634
LN2 = 0.6931471805599453
ALL_AXES = ("seq", "head", "ctx")
BF16 = jnp.bfloat16
F32 = jnp.float32


def dot_on(left, right, left_dim, right_dim):
    return lax.dot_general(
        left, right, (((left_dim,), (right_dim,)), ((), ())), preferred_element_type=F32
    )


def norm_rows(values, gain_vec, bias_vec):
    row_mean = jnp.mean(values, axis=-1, keepdims=True)
    centered = values - row_mean
    variance = jnp.mean(centered * centered, axis=-1, keepdims=True)
    inv_rows = lax.rsqrt(variance + EPSILON)
    unit_rows = centered * inv_rows
    return (unit_rows * gain_vec + bias_vec, unit_rows, inv_rows)


def norm_back(grad_norm, unit_rows, inv_rows, gain_vec):
    scaled = grad_norm * gain_vec
    return inv_rows * (
        scaled
        - jnp.mean(scaled, axis=-1, keepdims=True)
        - unit_rows * jnp.mean(scaled * unit_rows, axis=-1, keepdims=True)
    )


def gelu_exact(values):
    return jax.nn.gelu(values, approximate=False)


def swap_head(value, mask):
    count = lax.axis_size("head")
    return lax.ppermute(value, "head", [(i, i ^ mask) for i in range(count)])


def ring_order(count):
    return [0, 1, 3, 2] if count == 4 else list(range(count))


def ring_pairs(count, step):
    order = ring_order(count)
    return [(order[i], order[(i + step) % count]) for i in range(count)]


def ring_send(value, step):
    return lax.ppermute(value, "ctx", ring_pairs(lax.axis_size("ctx"), step))


def plane_blocks(block):
    near = swap_head(block, 2)
    return [block, swap_head(block, 1), near, swap_head(near, 1)]


def split_three(values):
    high = values.astype(BF16)
    rest = values - high.astype(F32)
    middle = rest.astype(BF16)
    low = (rest - middle.astype(F32)).astype(BF16)
    return [high.astype(F32), middle.astype(F32), low.astype(F32)]


def key_marks(valid, lane):
    row = lax.broadcasted_iota(jnp.int32, (BLOCK, LANES), 0)
    real = row < valid
    marks = jnp.where((lane >= 64) & (lane < 67), 1.0, 0.0)
    marks = jnp.where((lane == 67) & jnp.logical_not(real), MASKED, marks)
    return jnp.where((lane == 68) & real, MASKED, marks)


def fill_keys(slots, kv_ref, valid_ref, keys_out, values_t=None, values_out=None, marks_first=0):
    lane = lax.broadcasted_iota(jnp.int32, (BLOCK, LANES), 1)

    def fill(slot, carry):
        rows = pl.ds(pl.multiple_of(slot * BLOCK, BLOCK), BLOCK)
        marks = key_marks(valid_ref[slot + marks_first], lane)
        for head in range(3):
            pair = kv_ref[rows, head * LANES : (head + 1) * LANES].astype(F32)
            keys_out[head, rows, :] = jnp.where(lane < 64, pair, marks).astype(BF16)
            if values_out is not None:
                ones = jnp.where(lane < 3, 1.0, 0.0)
                values_out[head, rows, :] = jnp.where(lane < 64, ones, pair).astype(BF16)
            if values_t is not None:
                turned = pair.T[64:128].astype(BF16)
                values_t[head, :, rows] = jnp.concatenate(
                    [turned, jnp.ones((16, BLOCK), BF16)], axis=0
                )
        return carry

    lax.fori_loop(0, slots, fill, 0)


def query_marks(valid, width):
    row = lax.broadcasted_iota(jnp.int32, (1, width), 1)
    real = jnp.where(row < valid, 1.0, 0.0)
    return [real, 1.0 - real]


def forward_kernel(plane, last, *refs):
    refs = list(refs)
    count_ref, list_ref, valid_ref = refs[:3]
    x_refs, norm_ref, w_kv_ref = refs[3:7], refs[7], refs[8]
    refs = refs[9:]
    if plane == 0:
        w_q_ref = refs.pop(0)
    else:
        q_ref, acc_in = refs.pop(0), refs.pop(0)
    if last:
        before, refs = refs[:plane], refs[plane:]
    kv_ref = refs.pop(0)
    if plane == 0:
        q_ref = refs.pop(0)
    if last:
        out_ref, lse_ref = refs.pop(0), refs.pop(0)
        keys, values_t, q_ext, acc, top, kv_copy, copied = refs
    else:
        acc = refs.pop(0)
        keys, values_t, q_ext = refs
    gain, bias = norm_ref[0:1, :], norm_ref[1:2, :]
    for slot, x_ref in enumerate(x_refs):
        rows = slice(slot * BLOCK, (slot + 1) * BLOCK)
        normed, ignored, ignored_too = norm_rows(x_ref[...].astype(F32), gain, bias)
        normed = normed.astype(BF16)
        kv_ref[rows, :] = dot_on(normed, w_kv_ref[...], 1, 0).astype(BF16)
        if plane == 0:
            own = dot_on(normed, w_q_ref[...], 1, 0) * (HDIM ** (-0.5) * LOG2E)
            q_ref[rows, :] = own.astype(BF16)
    fill_keys(4, kv_ref, valid_ref, keys, values_t=values_t, marks_first=4 * plane)
    if plane == 0:
        acc[...] = jnp.zeros_like(acc)
    else:
        acc[...] = acc_in[...]

    def set_queries(block):
        q_rows = pl.ds(pl.multiple_of(block * BLOCK, BLOCK), BLOCK)
        lane = lax.broadcasted_iota(jnp.int32, (BLOCK, LANES), 1)
        row = lax.broadcasted_iota(jnp.int32, (BLOCK, LANES), 0)
        real = row < valid_ref[block]
        marks = jnp.where((lane == 67) & real, 1.0, 0.0)
        marks = jnp.where((lane == 68) & jnp.logical_not(real), 1.0, marks)
        for head in range(3):
            own = q_ref[q_rows, head * LANES : (head + 1) * LANES].astype(F32)
            q_ext[head] = jnp.where(lane < 64, own, marks).astype(BF16)
        return q_rows

    def scores_of(slot, head):
        rows = pl.ds(pl.multiple_of(slot * BLOCK, BLOCK), BLOCK)
        return dot_on(keys[head, rows, :], q_ext[head], 1, 1)

    def over_queries(block, carry):
        q_rows = set_queries(block)

        def over_keys(item, carry_in):
            slot = list_ref[plane, block, item]
            rows = pl.ds(pl.multiple_of(slot * BLOCK, BLOCK), BLOCK)
            ready = [scores_of(slot, 0), scores_of(slot, 1)]
            for head in range(3):
                if head == 0:
                    ready.append(scores_of(slot, 2))
                weights = jnp.exp2(ready.pop(0)).astype(BF16)
                acc[head, :, q_rows] += dot_on(values_t[head, :, rows], weights, 1, 0)
            return carry_in

        lax.fori_loop(0, count_ref[plane, block], over_keys, 0)
        return carry

    lax.fori_loop(0, 4, over_queries, 0)
    if not last:
        return
    sums = acc[:, 64:65, :]
    good = (sums >= 2.0**-60) & (sums <= 2.0**100)
    safe = jnp.min(jnp.where(good, 1.0, 0.0)) > 0.5
    top[...] = jnp.zeros_like(top)

    @pl.when(jnp.logical_not(safe))
    def _():
        top[...] = jnp.full_like(top, MASKED)
        acc[...] = jnp.zeros_like(acc)
        for which, source in enumerate(list(before) + [kv_ref]):
            if which < plane:
                move = pltpu.make_async_copy(source, kv_copy, copied)
                move.start()
                move.wait()
                source = kv_copy
            fill_keys(4, source, valid_ref, keys, values_t=values_t, marks_first=4 * which)

            def over_queries_again(block, carry, which=which):
                q_rows = set_queries(block)

                def with_max(item, carry_in):
                    slot = list_ref[which, block, item]
                    rows = pl.ds(pl.multiple_of(slot * BLOCK, BLOCK), BLOCK)
                    for head in range(3):
                        scores = scores_of(slot, head)
                        old = top[head, :, q_rows]
                        now = jnp.maximum(old, jnp.max(scores, axis=0, keepdims=True))
                        weights = jnp.exp2(scores - now).astype(BF16)
                        top[head, :, q_rows] = now
                        acc[head, :, q_rows] = acc[head, :, q_rows] * jnp.exp2(
                            old - now
                        ) + dot_on(values_t[head, :, rows], weights, 1, 0)
                    return carry_in

                lax.fori_loop(0, count_ref[which, block], with_max, 0)
                return carry

            lax.fori_loop(0, 4, over_queries_again, 0)

    for head in range(3):
        total = acc[head, 64:65, :]
        out_ref[head] = (acc[head, 0:64, :] / total).astype(BF16)
        lse_ref[head] = top[head] + jnp.log2(total)


def attend_forward(plane, last, counts, lists, valid, blocks, norms, w_kv, w_q, queries, acc, before):
    kv_rows = 4 * BLOCK
    smem = pl.BlockSpec(memory_space=pltpu.SMEM)
    vmem = pl.BlockSpec(memory_space=pltpu.VMEM)
    anywhere = pl.BlockSpec(memory_space=pl.ANY)
    packed = jax.ShapeDtypeStruct((kv_rows, 3 * LANES), BF16)
    sums = jax.ShapeDtypeStruct((3, 80, kv_rows), F32)
    inputs = [counts, lists, valid] + list(blocks) + [norms, w_kv]
    inputs += [w_q] if plane == 0 else [queries, acc]
    outs = [packed] + ([packed] if plane == 0 else [])
    scratch = [
        pltpu.VMEM((3, kv_rows, LANES), BF16),
        pltpu.VMEM((3, 80, kv_rows), BF16),
        pltpu.VMEM((3, BLOCK, LANES), BF16),
    ]
    in_specs = [smem] * 3 + [vmem] * (len(inputs) - 3)
    if last:
        inputs += list(before)
        in_specs += [anywhere] * len(before)
        outs += [
            jax.ShapeDtypeStruct((3, HDIM, kv_rows), BF16),
            jax.ShapeDtypeStruct((3, 1, kv_rows), F32),
        ]
        scratch += [
            pltpu.VMEM((3, 80, kv_rows), F32),
            pltpu.VMEM((3, 1, kv_rows), F32),
            pltpu.VMEM((kv_rows, 3 * LANES), BF16),
            pltpu.SemaphoreType.DMA,
        ]
    else:
        outs += [sums]
    return pl.pallas_call(
        partial(forward_kernel, plane, last),
        out_shape=tuple(outs),
        in_specs=in_specs,
        out_specs=(vmem,) * len(outs),
        scratch_shapes=scratch,
        compiler_params=pltpu.CompilerParams(vmem_limit_bytes=40 << 20),
        cost_estimate=pl.CostEstimate(
            flops=12 * 1000 * 1000 * 1000, bytes_accessed=10 << 20, transcendentals=7 << 20
        ),
        name="attend_forward",
    )(*inputs)


def backward_kernel(plane, carried, last, *refs):
    refs = list(refs)
    count_ref, list_ref, valid_ref = refs[:3]
    q_ref, kv_ref, out_ref, lse_ref, grad_ref, norm_ref, w_kv_ref, w_q_ref = refs[3:11]
    x_from, refs = refs[11:15], refs[15:]
    if carried:
        dq_in, dw_in, sum_in = refs[:3]
        refs = refs[3:]
    if last:
        keep_ref, send_ref, dw_ref, dwq_ref, sum_ref = refs[:5]
        dq_ref = None
        refs = refs[5:]
    else:
        keep_ref, send_ref, dw_ref, dq_ref, sum_ref = refs[:5]
        refs = refs[5:]
    keys, values, q_ext, g_ext, q_turned, dq_acc, dkv_acc, x_ref, moved = refs
    slots = 4
    moves = [
        pltpu.make_async_copy(x_from[i], x_ref.at[pl.ds(i * BLOCK, BLOCK)], moved.at[i])
        for i in range(slots)
    ]
    if carried:
        moves.append(pltpu.make_async_copy(dq_in, dq_acc, moved.at[4]))
    for move in moves:
        move.start()
    fill_keys(slots, kv_ref, valid_ref, keys, values_out=values, marks_first=4 * plane)
    lane = lax.broadcasted_iota(jnp.int32, (BLOCK, LANES), 1)

    def clear(slot, carry):
        rows = pl.ds(pl.multiple_of(slot * BLOCK, BLOCK), BLOCK)
        for head in range(3):
            dkv_acc[head, :, rows] = jnp.zeros((LANES, BLOCK), F32)
        return carry

    lax.fori_loop(0, slots, clear, 0)
    if carried:
        moves[4].wait()
    else:
        dq_acc[...] = jnp.zeros_like(dq_acc)

    def over_queries(block, carry):
        q_rows = pl.ds(pl.multiple_of(block * BLOCK, BLOCK), BLOCK)
        for head in range(3):
            lanes = slice(head * LANES, (head + 1) * LANES)
            turned = q_ref[q_rows, lanes].astype(F32).T[0:64]
            grad_t = grad_ref[head, :, q_rows].astype(F32)
            delta = jnp.sum(grad_t * out_ref[head, :, q_rows].astype(F32), axis=0, keepdims=True)
            marks = split_three(-lse_ref[head, :, q_rows]) + query_marks(valid_ref[block], BLOCK)
            blank = jnp.zeros((64 - len(marks), BLOCK), F32)
            q_turned[head] = turned.astype(BF16)
            q_ext[head] = jnp.concatenate([turned] + marks + [blank], axis=0).T.astype(BF16)
            minus = split_three(-delta)
            blank = jnp.zeros((64 - len(minus), BLOCK), F32)
            g_ext[head] = jnp.concatenate(minus + [blank, grad_t], axis=0).T.astype(BF16)

        def over_keys(item, carry_in):
            slot = list_ref[plane, block, item]
            rows = pl.ds(pl.multiple_of(slot * BLOCK, BLOCK), BLOCK)

            def products(head):
                return (
                    dot_on(q_ext[head], keys[head, rows, :], 1, 1),
                    dot_on(g_ext[head], values[head, rows, :], 1, 1),
                )

            ready = [products(0)]
            for head in range(3):
                lanes = slice(head * LANES, (head + 1) * LANES)
                if head < 2:
                    ready.append(products(head + 1))
                scores, grad_probs = ready.pop(0)
                probs = jnp.exp2(scores)
                grad_scores = (probs * grad_probs).astype(BF16)
                dkv_acc[head, 64:128, rows] += dot_on(
                    grad_ref[head, :, q_rows], probs.astype(BF16), 1, 0
                )
                dkv_acc[head, 0:64, rows] += dot_on(q_turned[head], grad_scores, 1, 0)
                dq_acc[q_rows, lanes] += dot_on(grad_scores, keys[head, rows, :], 1, 0)
            return carry_in

        lax.fori_loop(0, count_ref[plane, block], over_keys, 0)
        return carry

    lax.fori_loop(0, 4, over_queries, 0)
    for move in moves[:4]:
        move.wait()
    if not last:
        leave = pltpu.make_async_copy(dq_acc, dq_ref, moved.at[4])
        leave.start()
    if carried:
        dw_ref[...] = dw_in[...]
        sum_ref[...] = sum_in[...]
    else:
        dw_ref[...] = jnp.zeros_like(dw_ref)
        sum_ref[...] = jnp.zeros_like(sum_ref)
    if last:
        dwq_ref[...] = jnp.zeros_like(dwq_ref)
    gain, bias = norm_ref[0:1, :], norm_ref[1:2, :]

    def finish(slot, carry):
        rows = pl.ds(pl.multiple_of(slot * BLOCK, BLOCK), BLOCK)
        pieces = []
        for head in range(3):
            pieces.append(dkv_acc[head, 0:64, rows] * LN2)
            pieces.append(dkv_acc[head, 64:128, rows])
        turned = jnp.concatenate(pieces, axis=0)
        part = dot_on(turned.T.astype(BF16), w_kv_ref[...], 1, 0)
        values_now = x_ref[rows, :].astype(F32)
        normed, unit, ignored = norm_rows(values_now, gain, bias)
        normed = normed.astype(BF16)
        dw_ref[...] += dot_on(turned.astype(BF16), normed, 1, 0)
        if last:
            scaled = [
                jnp.where(lane < 64, dq_acc[rows, h * LANES : (h + 1) * LANES], 0.0)
                for h in range(3)
            ]
            scaled = jnp.concatenate(scaled, axis=1) * HDIM ** (-0.5)
            part = part + dot_on(scaled.astype(BF16), w_q_ref[...], 1, 0)
            dwq_ref[...] += dot_on(scaled.T.astype(BF16), normed, 1, 0)
        sum_ref[0:1, :] += jnp.sum(part * unit, axis=0, keepdims=True)
        sum_ref[1:2, :] += jnp.sum(part, axis=0, keepdims=True)
        low = part.astype(BF16)

        @pl.when(slot % 2 == 0)
        def _():
            keep_ref[slot // 2] = low

        @pl.when(slot % 2 == 1)
        def _():
            send_ref[slot // 2] = low

        return carry

    lax.fori_loop(0, slots, finish, 0)
    if not last:
        leave.wait()


def attend_backward(
    plane, counts, lists, valid, queries, key_vals, attended, lse, grads, norms, w_kv_t, w_q_t, blocks, carry, last
):
    q_rows = queries.shape[0]
    smem = pl.BlockSpec(memory_space=pltpu.SMEM)
    vmem = pl.BlockSpec(memory_space=pltpu.VMEM)
    anywhere = pl.BlockSpec(memory_space=pl.ANY)
    carry = list(carry)
    half = jax.ShapeDtypeStruct((2, BLOCK, D), BF16)
    weight = jax.ShapeDtypeStruct((3 * LANES, D), F32)
    fourth = weight if last else jax.ShapeDtypeStruct((q_rows, 3 * LANES), F32)
    return pl.pallas_call(
        partial(backward_kernel, plane, bool(carry), last),
        out_shape=(half, half, weight, fourth, jax.ShapeDtypeStruct((8, D), F32)),
        in_specs=[smem] * 3 + [vmem] * 8 + [anywhere] * 4 + [anywhere, vmem, vmem][: len(carry)],
        out_specs=(vmem, vmem, vmem, vmem if last else anywhere, vmem),
        scratch_shapes=[
            pltpu.VMEM((3, q_rows, LANES), BF16),
            pltpu.VMEM((3, q_rows, LANES), BF16),
            pltpu.VMEM((3, BLOCK, LANES), BF16),
            pltpu.VMEM((3, BLOCK, LANES), BF16),
            pltpu.VMEM((3, HDIM, BLOCK), BF16),
            pltpu.VMEM((q_rows, 3 * LANES), F32),
            pltpu.VMEM((3, LANES, q_rows), F32),
            pltpu.VMEM((q_rows, D), BF16),
            pltpu.SemaphoreType.DMA((5,)),
        ],
        compiler_params=pltpu.CompilerParams(vmem_limit_bytes=44 << 20),
        cost_estimate=pl.CostEstimate(
            flops=25 * 1000 * 1000 * 1000, bytes_accessed=16 << 20, transcendentals=7 << 20
        ),
        name="attend_backward",
    )(
        counts, lists, valid, queries, key_vals, attended, lse, grads, norms, w_kv_t, w_q_t, *blocks, *carry
    )


def erf_of(values):
    clamped = jnp.clip(values, -4.0, 4.0)
    square = clamped * clamped
    top = jnp.float32(-2.72614225801306e-10)
    for term in (
        2.77068142495902e-08,
        -2.10102402082508e-06,
        -5.69250639462346e-05,
        -7.34990630326855e-04,
        -2.95459980854025e-03,
        -1.60960333262415e-02,
    ):
        top = top * square + term
    low = jnp.float32(-1.45660718464996e-05)
    for term in (
        -2.13374055278905e-04,
        -1.68282697438203e-03,
        -7.37332916720468e-03,
        -1.42647390514189e-02,
    ):
        low = low * square + term
    return clamped * top / low


def middle_kernel(pieces, shard, *refs):
    refs = list(refs)
    start_ref, group_ref = refs[:2]
    merged_refs, refs = refs[2:6], refs[6:]
    token_ref, cot_ref, norm_ref = refs[:3]
    piece_refs, refs = refs[3 : 3 + pieces], refs[3 + pieces :]
    output_ref, grad_y_ref, grad_z_ref, h_two_ref, hidden_ref, grad_up_ref = refs[:6]
    part_refs, sum_ref, refs = refs[6:10], refs[10], refs[11:]
    w_out, w_up, w_down, moved = refs
    pair = piece_refs[0].shape[0] // 9

    def moves_of(weight):
        moves = []
        for i, piece in enumerate(piece_refs):
            if weight < 5:
                source = piece.at[pl.ds(weight * pair, pair)]
                rows = pl.ds(pl.multiple_of(start_ref[i] * shard, pair), pair)
                target = w_out.at[rows] if weight == 0 else w_up.at[weight - 1, rows]
            else:
                source = piece.at[pl.ds(5 * pair, 4 * pair)]
                rows = pl.ds(pl.multiple_of(start_ref[i] * 4 * shard, 4 * pair), 4 * pair)
                target = w_down.at[rows]
            moves.append(pltpu.make_async_copy(source, target, moved.at[weight, i]))
        return moves

    arriving = [moves_of(weight) for weight in range(6)]
    for weight in (0, 1, 5, 2, 3, 4):
        for move in arriving[weight]:
            move.start()
    for move in arriving[0]:
        move.wait()
    y_one = token_ref[...].astype(F32)
    group = D // 4
    for j, merged_ref in enumerate(merged_refs):
        rows = pl.ds(pl.multiple_of(group_ref[j] * group, group), group)
        turned = merged_ref[...].astype(F32).T.astype(BF16)
        y_one = y_one + dot_on(turned, w_out[rows, :], 1, 0)
    grad_y_ref[...] = y_one
    gain, bias = norm_ref[0:1, :], norm_ref[1:2, :]
    normed, unit, inv_rows = norm_rows(y_one, gain, bias)
    h_two_ref[...] = normed.astype(BF16)

    output_sum = jnp.zeros((BLOCK, D), F32)
    grad_sum = jnp.zeros((BLOCK, D), F32)
    for j in range(4):
        for move in arriving[1 + j]:
            move.wait()
        if j == 0:
            for move in arriving[5]:
                move.wait()
        columns = slice(j * D, (j + 1) * D)
        up = dot_on(h_two_ref[...], w_up[j], 1, 0)
        grad_hidden = dot_on(cot_ref[...], w_down[columns, :], 1, 1)
        normal = 0.5 + 0.5 * erf_of(up * 0.7071067811865476)
        density = jnp.exp(-0.5 * up * up) * 0.3989422804014327
        hidden = (up * normal).astype(BF16)
        grad_up = (grad_hidden * (normal + up * density)).astype(BF16)
        hidden_ref[:, columns] = hidden
        grad_up_ref[:, columns] = grad_up
        output_sum = output_sum + dot_on(hidden, w_down[columns, :], 1, 0)
        grad_sum = grad_sum + dot_on(grad_up, w_up[j], 1, 1)
    y_one = grad_y_ref[...]
    output_ref[...] = (y_one + output_sum).astype(BF16)
    normed, unit, inv_rows = norm_rows(y_one, gain, bias)
    sum_ref[...] = jnp.zeros_like(sum_ref)
    sum_ref[0:1, :] = jnp.sum(grad_sum * unit, axis=0, keepdims=True)
    sum_ref[1:2, :] = jnp.sum(grad_sum, axis=0, keepdims=True)
    grad_y = cot_ref[...].astype(F32) + norm_back(grad_sum, unit, inv_rows, gain)
    grad_y_ref[...] = grad_y
    grad_z = grad_y.astype(BF16)
    grad_z_ref[...] = grad_z
    for j, part_ref in enumerate(part_refs):
        rows = pl.ds(pl.multiple_of(group_ref[j] * group, group), group)
        part_ref[...] = dot_on(w_out[rows, :], grad_z, 1, 1).astype(BF16)


def middle(starts, groups, merged, tokens, cotangent, norms, pieces, shard):
    smem = pl.BlockSpec(memory_space=pltpu.SMEM)
    vmem = pl.BlockSpec(memory_space=pltpu.VMEM)
    anywhere = pl.BlockSpec(memory_space=pl.ANY)
    rows = tokens.shape[0]

    def shape(columns, dtype, height=rows):
        return jax.ShapeDtypeStruct((height, columns), dtype)

    return pl.pallas_call(
        partial(middle_kernel, len(pieces), shard),
        out_shape=(
            shape(D, BF16),
            shape(D, F32),
            shape(D, BF16),
            shape(D, BF16),
            shape(4 * D, BF16),
            shape(4 * D, BF16),
        )
        + (shape(rows, BF16, D // 4),) * 4
        + (shape(D, F32, 8),),
        in_specs=[smem, smem] + [vmem] * 7 + [anywhere] * len(pieces),
        out_specs=(vmem,) * 11,
        scratch_shapes=[
            pltpu.VMEM((D, D), BF16),
            pltpu.VMEM((4, D, D), BF16),
            pltpu.VMEM((4 * D, D), BF16),
            pltpu.SemaphoreType.DMA((6, len(pieces))),
        ],
        compiler_params=pltpu.CompilerParams(vmem_limit_bytes=56 << 20),
        cost_estimate=pl.CostEstimate(
            flops=12 * 1000 * 1000 * 1000, bytes_accessed=24 << 20, transcendentals=3 << 20
        ),
        name="middle",
    )(starts, groups, *merged, tokens, cotangent, norms, *pieces)


def scene_lists(same):
    number = same.shape[-1]
    slot = jnp.arange(number)
    counts = jnp.sum(same, axis=-1).astype(jnp.int32)
    earlier = slot[None, :] < slot[:, None]
    place = jnp.sum(same[:, :, None, :] & earlier, axis=-1)
    hits = same[:, :, None, :] & (place[:, :, None, :] == slot[:, None])
    lists = jnp.sum(jnp.where(hits, slot, 0), axis=-1)
    return counts, lists.astype(jnp.int32)


def halve(value, axis, bit, send):
    keep = lax.dynamic_index_in_dim(value, bit, axis, keepdims=False)
    give = lax.dynamic_index_in_dim(value, 1 - bit, axis, keepdims=False)
    return (keep.astype(F32) + send(give).astype(F32)).astype(BF16)


def ring_sources(count):
    order = ring_order(count)
    table = [[order[(order.index(c) - r) % count] for r in range(count)] for c in range(count)]
    return jnp.array(table, jnp.int32)[lax.axis_index("ctx")]


def sum_over_seq(value):
    count = lax.axis_size("seq")
    me = lax.axis_index("seq")
    while count > 1:
        count //= 2
        bit = (me // count) % 2
        pairs = [(i, i ^ count) for i in range(lax.axis_size("seq"))]
        value = halve(
            value.reshape((2, count) + value.shape[1:]),
            0,
            bit,
            lambda give: lax.ppermute(give, "seq", pairs),
        )
    return value.reshape(value.shape[1:])


def gather_bit(value, bit, send):
    other = send(value)
    first = jnp.where(bit == 0, value, other)
    return jnp.concatenate([first, jnp.where(bit == 0, other, value)], axis=0)


def gather_seq(value):
    count, reach = lax.axis_size("seq"), 1
    me = lax.axis_index("seq")
    while reach < count:
        pairs = [(i, i ^ reach) for i in range(count)]
        value = gather_bit(
            value[None], (me // reach) % 2, lambda v: lax.ppermute(v, "seq", pairs)
        ).reshape((2 * reach,) + value.shape[1:])
        reach *= 2
    return value


def swap_seq(value, mask=1):
    return lax.ppermute(value, "seq", [(i, i ^ mask) for i in range(lax.axis_size("seq"))])


def in_order(blocks, sources, shard):
    count = len(blocks)
    full = jnp.zeros((count,) + blocks[0].shape, BF16)
    for r in range(count):
        full = lax.dynamic_update_index_in_dim(full, blocks[r], sources[r], 0)
    halves = []
    for half in range(2):
        part = full[half * (count // 2) : (half + 1) * (count // 2)]
        cut = [part[:, i * shard : (i + 1) * shard] for i in range(5)] + [part[:, 5 * shard :]]
        halves.append(jnp.concatenate([c.reshape(-1, D) for c in cut], axis=0))
    return halves


def join_halves(pieces, starts, offs, rows):
    cuts = [i * rows for i in range(1, 6)]
    joined, firsts = [], []
    for base in range(0, len(pieces), len(offs)):
        for i, (half, x, y) in enumerate(offs):
            if half == 0:
                other = base + offs.index((1, x, y))
                both = zip(jnp.split(pieces[base + i], cuts), jnp.split(pieces[other], cuts))
                joined.append(jnp.concatenate([part for pair in both for part in pair], axis=0))
                firsts.append(starts[base + i])
    return joined, firsts


def gather_ctx(value):
    count = lax.axis_size("ctx")
    sources = ring_sources(count)
    whole = jnp.zeros((count,) + value.shape, value.dtype)
    whole = lax.dynamic_update_index_in_dim(whole, value, sources[0], 0)
    for r in range(1, count):
        whole = lax.dynamic_update_index_in_dim(whole, ring_send(value, r), sources[r], 0)
    return whole


def sum_over_core(value):
    seqs, ctxs = lax.axis_size("seq"), lax.axis_size("ctx")
    rows = value.shape[0] // (seqs * ctxs * 4)
    value = value.reshape(seqs, 2, 2, ctxs, rows, value.shape[1])
    bit = lax.axis_index("head") % 2
    return halve(value, 2, bit, lambda give: swap_head(give, 1))


def sum_over_x(value):
    bit = lax.axis_index("head") // 2
    return halve(value, 0, bit, lambda give: swap_head(give, 2))


def send_term(value, r):
    source = ring_sources(lax.axis_size("ctx"))[r]
    return ring_send(lax.dynamic_index_in_dim(value, source, 0, keepdims=False), -r)


def sum_terms(value, terms):
    source = ring_sources(lax.axis_size("ctx"))[0]
    total = lax.dynamic_index_in_dim(value, source, 0, keepdims=False).astype(F32)
    for term in terms:
        total = total + term.astype(F32)
    return total


def sum_over_ctx(value):
    count = lax.axis_size("ctx")
    sources = ring_sources(count)
    total = lax.dynamic_index_in_dim(value, sources[0], 0, keepdims=False).astype(F32)
    for r in range(1, count):
        give = lax.dynamic_index_in_dim(value, sources[r], 0, keepdims=False)
        total = total + ring_send(give, -r).astype(F32)
    return total


def tie(*values):
    return lax.optimization_barrier(values)


def body(
    tokens,
    segment_ids,
    w_qkv,
    w_out,
    w_up,
    w_down,
    gain_one,
    bias_one,
    gain_two,
    bias_two,
    cotangent,
):
    heads_ax = lax.axis_size("head")
    ctx_ax = lax.axis_size("ctx")
    seq_ax = lax.axis_size("seq")
    me_head = lax.axis_index("head")
    tok_rows = tokens.shape[0]
    group = D // heads_ax
    shard = w_qkv.shape[0]

    order = [me_head ^ j for j in range(heads_ax)]
    sources = ring_sources(ctx_ax)

    padding = tok_rows - jnp.sum(segment_ids >= 0)
    about = jnp.stack([segment_ids[0], padding // 16, padding % 16]).astype(BF16)
    extra = jnp.stack([gain_one, bias_one, gain_two, bias_two], axis=1)
    extra = jnp.concatenate([extra, jnp.broadcast_to(about[None, :], (shard, 3))], axis=1)
    extra = jnp.pad(extra, ((0, 0), (0, LANES - 7)))
    packed = jnp.swapaxes(w_qkv.reshape(shard, heads_ax, 3 * group), 0, 1)
    packed = jnp.concatenate(
        [packed, jnp.broadcast_to(extra[None], (heads_ax,) + extra.shape)], axis=2
    )
    wide = 3 * group + LANES
    packed = gather_seq(packed[None])
    pieces = []
    for j in range(heads_ax):
        piece = lax.dynamic_index_in_dim(packed, order[j], 1, keepdims=False)
        pieces.append(swap_head(piece, j) if j else piece)
    packed = jnp.zeros((heads_ax, seq_ax, shard, wide), BF16)
    for j in range(heads_ax):
        packed = lax.dynamic_update_index_in_dim(packed, pieces[j], order[j], 0)
    packed = gather_ctx(packed)
    packed = jnp.transpose(packed, (2, 1, 0, 3, 4)).reshape(D, wide)

    w_rest = jnp.concatenate(
        [w_out] + [w_up[:, i * D : (i + 1) * D] for i in range(4)] + [w_down], axis=0
    )
    rest = [w_rest]
    near, ahead, behind = swap_head(tokens, 2), ring_send(tokens, 1), ring_send(w_rest, 1)
    near, ahead, behind, packed = tie(near, ahead, behind, packed)
    rest.append(behind)

    g_one, b_one, g_two, b_two = [packed[:, 3 * group + i].astype(F32) for i in range(4)]
    norm_one = jnp.pad(jnp.stack([g_one, b_one]), ((0, 6), (0, 0)))
    w_mine = packed[:, : 3 * group].reshape(D, 3, 3, HDIM)
    w_kv = w_mine[:, :, 1:].reshape(D, 6 * HDIM)
    w_q = jnp.pad(w_mine[:, :, :1], ((0, 0), (0, 0), (0, 1), (0, 0))).reshape(D, 6 * HDIM)
    w_kv_t, w_q_t = w_kv.T, w_q.T
    about_all = packed[::shard, 3 * group + 4 : 3 * group + 7].astype(jnp.int32)
    about_all = lax.dynamic_index_in_dim(
        about_all.reshape(seq_ax, heads_ax, ctx_ax, 3), lax.axis_index("seq"), 0, keepdims=False
    )
    pick_head = jnp.stack(order)[:, None] == jnp.arange(heads_ax)[None, :]
    pick_ctx = sources[:, None] == jnp.arange(ctx_ax)[None, :]
    pick = pick_ctx[:, None, None, :] & pick_head[None, :, :, None]
    slot_about = jnp.sum(jnp.where(pick[..., None], about_all[None, None], 0), axis=(2, 3))
    slot_ids = slot_about[:, :, 0]
    slot_valid = (tok_rows - (slot_about[:, :, 1] * 16 + slot_about[:, :, 2])).reshape(-1)
    counts, lists = scene_lists(slot_ids[0][None, :, None] == slot_ids[:, None, :])

    planes, key_vals, queries, acc = [], [], None, None
    block = tokens
    ready = None
    for r in range(ctx_ax + 1):
        if r < ctx_ax:
            travelers = [swap_head(block, 1), swap_head(near, 1)]
        else:
            travelers = []
        if r + 1 < ctx_ax:
            travelers.append(swap_head(ahead, 2))
        if r + 2 < ctx_ax:
            travelers.append(ring_send(ahead, 1))
            travelers.append(ring_send(rest[-1], 1))
        count = len(travelers)
        if r == ctx_ax - 2:
            halves = in_order(rest, sources, shard)
            travelers += [swap_head(halves[0], 2), swap_seq(halves[0]), swap_seq(halves[1])]
        if r == ctx_ax - 1:
            travelers += [swap_head(halves[1], 2), swap_seq(x_first)]
            travelers += [swap_head(v, 1) for v in halves]
        if r == ctx_ax:
            travelers += [swap_seq(x_second)]
            travelers += [swap_head(v, 1) for v in (x_first, y_first, y_second, xy_first)]
        results = []
        if ready is not None:
            results = list(
                attend_forward(
                    r - 1,
                    r == ctx_ax,
                    counts,
                    lists,
                    slot_valid,
                    ready,
                    norm_one,
                    w_kv,
                    w_q,
                    queries,
                    acc,
                    key_vals,
                )
            )
        tied = list(tie(*travelers, *results))
        extra, tied = tied[count : len(travelers)], tied[:count] + tied[len(travelers) :]
        if r == ctx_ax - 2:
            x_first, y_first, y_second = extra
        if r == ctx_ax - 1:
            x_second, xy_first = extra[:2]
            cores = extra[2:]
        if r == ctx_ax:
            xy_second = extra[0]
            cores += extra[1:]
            results = tied
            break
        planes.append([block, tied.pop(0), near, tied.pop(0)])
        ready = planes[-1]
        if r + 1 < ctx_ax:
            block, near = ahead, tied.pop(0)
        if r + 2 < ctx_ax:
            ahead = tied.pop(0)
            rest.append(tied.pop(0))
        if results:
            key_vals.append(tied.pop(0))
            if r == 1:
                queries = tied.pop(0)
            acc = tied.pop(0)
    key_vals.append(results[0])
    attended, lse = results[1:]
    cores += [swap_head(v, 1) for v in (x_second, xy_second)]
    owns = [halves[0], halves[1], x_first, y_first, y_second, xy_first, x_second, xy_second]
    offs = [(0, 0, 0), (1, 0, 0), (0, 1, 0), (0, 0, 1), (1, 0, 1), (0, 1, 1), (1, 1, 0), (1, 1, 1)]
    me_x, me_core, me_seq = me_head // 2, me_head % 2, lax.axis_index("seq")
    pieces, starts = [], []
    for core, arrays in enumerate((owns, cores)):
        for array, (half, x, y) in zip(arrays, offs):
            pieces.append(array)
            starts.append((half, (me_x ^ x) * 2 + (me_core ^ core), y))
    reach = 2
    while reach < seq_ax:
        pieces += [swap_seq(array, reach) for array in pieces]
        starts += [(half, place, y ^ reach) for half, place, y in starts]
        reach *= 2
    starts = [
        ((me_seq ^ y) * heads_ax + place) * ctx_ax + half * (ctx_ax // 2)
        for half, place, y in starts
    ]
    if (ctx_ax // 2 * shard) % 8:
        pieces, starts = join_halves(pieces, starts, offs, ctx_ax // 2 * shard)
    starts = jnp.stack(starts).astype(jnp.int32)

    merged = []
    for j in range(heads_ax):
        part = attended[:, :, j * tok_rows : (j + 1) * tok_rows].reshape(group, tok_rows)
        merged.append(swap_head(part, j) if j else part)

    norm_two = jnp.pad(jnp.stack([g_two, b_two]), ((0, 6), (0, 0)))
    groups = jnp.stack(order).astype(jnp.int32)
    output, grad_y_one, grad_z, h_two, hidden, grad_up, *rest_out = middle(
        starts, groups, merged, tokens, cotangent, norm_two, pieces, shard
    )
    grad_merged, sums_two = rest_out[:4], rest_out[4]

    grad_parts = [swap_head(p, j) if j else p for j, p in enumerate(grad_merged)]
    grad_w_down = jnp.einsum("tf,td->fd", hidden, cotangent, preferred_element_type=F32)
    down_sum = sum_over_core(grad_w_down.astype(BF16))
    grad_w_up = jnp.einsum("td,tf->df", h_two, grad_up, preferred_element_type=F32)
    grad_w_up = grad_w_up.astype(BF16)
    grad_w_out = jnp.zeros((heads_ax, group, D), BF16)
    for j in range(heads_ax):
        part = jnp.einsum("at,td->ad", merged[j], grad_z, preferred_element_type=F32)
        grad_w_out = lax.dynamic_update_index_in_dim(grad_w_out, part.astype(BF16), order[j], 0)
    sums_two = jnp.pad(sums_two, ((0, LANES - 8), (0, 0))).T.astype(BF16)
    grad_w_out = jnp.concatenate([grad_w_out.reshape(D, D), sums_two], axis=1)
    tied = tie(down_sum, grad_w_up, grad_w_out, *grad_parts)
    down_sum, grad_w_up, grad_w_out = tied[:3]
    grad_local = jnp.concatenate(tied[3:], axis=1).reshape(3, HDIM, heads_ax * tok_rows)
    up_sum, out_sum = sum_over_core(grad_w_up), sum_over_core(grad_w_out)
    down_sum = sum_over_seq(down_sum)

    carry, traveling, by_x, given = (), None, None, None
    down_terms, wide_terms = [], []
    for r in reversed(range(ctx_ax)):
        step = ctx_ax - 1 - r
        travelers = []
        if step >= 1:
            low = keep.astype(F32) + swap_head(give, 1).astype(F32)
            travelers.append(low.astype(BF16))
        if step >= 2:
            moved = by_x[0].astype(F32) + swap_head(by_x[1], 2).astype(F32)
            if step >= 3:
                moved = moved + ring_send(traveling, -1).astype(F32)
            travelers.append(moved.astype(BF16))
        count = len(travelers)
        if step == 0:
            travelers += [down_sum, up_sum, out_sum]
        if step == 1:
            wide_sum = sum_over_seq(jnp.concatenate([up_sum, out_sum], axis=-1))
            down_sum = sum_over_x(down_sum)
            travelers += [down_sum, wide_sum]
        if step == 2:
            wide_sum = sum_over_x(wide_sum)
            travelers += [wide_sum] + [send_term(down_sum, i) for i in (1, 2)]
        if step == 3:
            travelers += [send_term(down_sum, 3), send_term(wide_sum, 1)]
        keep, give, dw_kv, fourth, sums = attend_backward(
            r,
            counts,
            lists,
            slot_valid,
            queries,
            key_vals[r],
            attended,
            lse,
            grad_local,
            norm_one,
            w_kv_t,
            w_q_t,
            planes[r],
            carry,
            r == 0,
        )
        keep, give, fourth, dw_kv, sums, *travelers = tie(
            keep, give, fourth, dw_kv, sums, *travelers
        )
        carry = (fourth, dw_kv, sums)
        if step >= 1:
            by_x = travelers[0]
        if step >= 2:
            traveling = travelers[1]
        travelers = travelers[count:]
        if step == 0:
            down_sum, up_sum, out_sum = travelers
        if step == 1:
            down_sum, wide_sum = travelers
        if step == 2:
            wide_sum, *down_terms = travelers
        if step == 3:
            down_terms.append(travelers[0])
            wide_terms.append(travelers[1])
    last_x = keep.astype(F32) + swap_head(give, 1).astype(F32)
    moved = by_x[0].astype(F32) + swap_head(by_x[1], 2).astype(F32)
    moved = (moved + ring_send(traveling, -1).astype(F32)).astype(BF16)
    grad_h_one = last_x[0] + swap_head(last_x[1].astype(BF16), 2).astype(F32)
    grad_h_one = grad_h_one + ring_send(moved, -1).astype(F32)
    wide_terms += [send_term(wide_sum, i) for i in (2, 3)]
    down_sum, wide_sum = sum_terms(down_sum, down_terms), sum_terms(wide_sum, wide_terms)
    up_sum, out_sum = wide_sum[:, : 4 * D], wide_sum[:, 4 * D :]
    dw_q = fourth

    dw_kv = dw_kv.reshape(3, 2, HDIM, D)
    dw_q = dw_q.reshape(3, 2, HDIM, D)
    dw_mine = jnp.concatenate([dw_q[:, :1], dw_kv], axis=1).reshape(3 * group, D)
    dw_mine = jnp.concatenate([dw_mine, jnp.pad(sums, ((0, LANES - 8), (0, 0)))], axis=0)
    dw_mine = dw_mine.T.astype(BF16).reshape(seq_ax, heads_ax, ctx_ax, shard, wide)
    dw_mine = sum_over_seq(dw_mine)
    dw_mine = sum_over_ctx(jnp.swapaxes(dw_mine, 0, 1)).astype(BF16)
    groups = []
    for j in range(heads_ax):
        part = lax.dynamic_index_in_dim(dw_mine, order[j], 0, keepdims=False)
        groups.append(swap_head(part, j) if j else part)
    groups = jnp.stack(groups)
    groups = jnp.stack(
        [lax.dynamic_index_in_dim(groups, o, 0, keepdims=False) for o in order]
    ).astype(F32)
    grad_w_qkv = jnp.swapaxes(groups[:, :, : 3 * group], 0, 1).reshape(shard, 3 * D)
    norm_sums = jnp.sum(groups[:, :, 3 * group : 3 * group + 2], axis=0)

    ignored, unit_one, inv_one = norm_rows(tokens.astype(F32), g_one, b_one)
    grad_tokens = (grad_y_one + norm_back(grad_h_one, unit_one, inv_one, g_one)).astype(BF16)
    return (
        output,
        grad_tokens,
        grad_w_qkv,
        out_sum[:, :D],
        up_sum,
        down_sum,
        norm_sums[:, 0],
        norm_sums[:, 1],
        out_sum[:, D],
        out_sum[:, D + 1],
    )


def solution(mesh):
    rows = P(ALL_AXES, None)
    vector = P(ALL_AXES)
    return jax.shard_map(
        body,
        mesh=mesh,
        in_specs=(rows, vector, rows, rows, rows, rows, vector, vector, vector, vector, rows),
        out_specs=(rows, rows, rows, rows, rows, rows, vector, vector, vector, vector),
        check_vma=False,
    )
```

```python
from functools import partial

import jax
import jax.numpy as jnp
from jax import lax
from jax.experimental import pallas as pl
from jax.experimental.pallas import tpu as pltpu
from jax.sharding import PartitionSpec as P

D = 768
HEADS = 12
HDIM = 64
BLOCK = 512
LANES = 128
EPSILON = 1e-05
MASKED = -1e30
LOG2E = 1.4426950408889634
LN2 = 0.6931471805599453
ALL_AXES = ("seq", "head", "ctx")
BF16 = jnp.bfloat16
F32 = jnp.float32


def dot_on(left, right, left_dim, right_dim):
    return lax.dot_general(
        left, right, (((left_dim,), (right_dim,)), ((), ())), preferred_element_type=F32
    )


def norm_rows(values, gain_vec, bias_vec):
    row_mean = jnp.mean(values, axis=-1, keepdims=True)
    centered = values - row_mean
    variance = jnp.mean(centered * centered, axis=-1, keepdims=True)
    inv_rows = lax.rsqrt(variance + EPSILON)
    unit_rows = centered * inv_rows
    return (unit_rows * gain_vec + bias_vec, unit_rows, inv_rows)


def norm_back(grad_norm, unit_rows, inv_rows, gain_vec):
    scaled = grad_norm * gain_vec
    return inv_rows * (
        scaled
        - jnp.mean(scaled, axis=-1, keepdims=True)
        - unit_rows * jnp.mean(scaled * unit_rows, axis=-1, keepdims=True)
    )


def gelu_exact(values):
    return jax.nn.gelu(values, approximate=False)


def swap_head(value, mask):
    count = lax.axis_size("head")
    return lax.ppermute(value, "head", [(i, i ^ mask) for i in range(count)])


def ring_order(count):
    return [0, 1, 3, 2] if count == 4 else list(range(count))


def ring_pairs(count, step):
    order = ring_order(count)
    return [(order[i], order[(i + step) % count]) for i in range(count)]


def ring_send(value, step):
    return lax.ppermute(value, "ctx", ring_pairs(lax.axis_size("ctx"), step))


def plane_blocks(block):
    near = swap_head(block, 2)
    return [block, swap_head(block, 1), near, swap_head(near, 1)]


def split_three(values):
    high = values.astype(BF16)
    rest = values - high.astype(F32)
    middle = rest.astype(BF16)
    low = (rest - middle.astype(F32)).astype(BF16)
    return [high.astype(F32), middle.astype(F32), low.astype(F32)]


def key_marks(valid, lane):
    row = lax.broadcasted_iota(jnp.int32, (BLOCK, LANES), 0)
    real = row < valid
    marks = jnp.where((lane >= 64) & (lane < 67), 1.0, 0.0)
    marks = jnp.where((lane == 67) & jnp.logical_not(real), MASKED, marks)
    return jnp.where((lane == 68) & real, MASKED, marks)


def fill_keys(slots, kv_ref, valid_ref, keys_out, values_t=None, values_out=None, marks_first=0):
    lane = lax.broadcasted_iota(jnp.int32, (BLOCK, LANES), 1)

    def fill(slot, carry):
        rows = pl.ds(pl.multiple_of(slot * BLOCK, BLOCK), BLOCK)
        marks = key_marks(valid_ref[slot + marks_first], lane)
        for head in range(3):
            pair = kv_ref[rows, head * LANES : (head + 1) * LANES].astype(F32)
            keys_out[head, rows, :] = jnp.where(lane < 64, pair, marks).astype(BF16)
            if values_out is not None:
                ones = jnp.where(lane < 3, 1.0, 0.0)
                values_out[head, rows, :] = jnp.where(lane < 64, ones, pair).astype(BF16)
            if values_t is not None:
                turned = pair.T[64:128].astype(BF16)
                values_t[head, :, rows] = jnp.concatenate(
                    [turned, jnp.ones((16, BLOCK), BF16)], axis=0
                )
        return carry

    lax.fori_loop(0, slots, fill, 0)


def query_marks(valid, width):
    row = lax.broadcasted_iota(jnp.int32, (1, width), 1)
    real = jnp.where(row < valid, 1.0, 0.0)
    return [real, 1.0 - real]


def forward_kernel(plane, last, *refs):
    refs = list(refs)
    count_ref, list_ref, valid_ref = refs[:3]
    x_refs = [refs[3], refs[5].at[0], refs[4], refs[5].at[1]]
    norm_ref, w_kv_ref = refs[6:8]
    refs = refs[8:]
    if plane == 0:
        w_q_ref = refs.pop(0)
    else:
        q_ref, acc_in = refs.pop(0), refs.pop(0)
    if last:
        before, refs = refs[:plane], refs[plane:]
    kv_ref = refs.pop(0)
    if plane == 0:
        q_ref = refs.pop(0)
    if last:
        out_ref, lse_ref = refs.pop(0), refs.pop(0)
        keys, values_t, q_ext, acc, top, kv_copy, copied = refs
    else:
        acc = refs.pop(0)
        keys, values_t, q_ext = refs
    gain, bias = norm_ref[0:1, :], norm_ref[1:2, :]
    for slot, x_ref in enumerate(x_refs):
        rows = slice(slot * BLOCK, (slot + 1) * BLOCK)
        normed, ignored, ignored_too = norm_rows(x_ref[...].astype(F32), gain, bias)
        normed = normed.astype(BF16)
        kv_ref[rows, :] = dot_on(normed, w_kv_ref[...], 1, 0).astype(BF16)
        if plane == 0:
            own = dot_on(normed, w_q_ref[...], 1, 0) * (HDIM ** (-0.5) * LOG2E)
            q_ref[rows, :] = own.astype(BF16)
    fill_keys(4, kv_ref, valid_ref, keys, values_t=values_t, marks_first=4 * plane)
    if plane == 0:
        acc[...] = jnp.zeros_like(acc)
    else:
        acc[...] = acc_in[...]

    def set_queries(block):
        q_rows = pl.ds(pl.multiple_of(block * BLOCK, BLOCK), BLOCK)
        lane = lax.broadcasted_iota(jnp.int32, (BLOCK, LANES), 1)
        row = lax.broadcasted_iota(jnp.int32, (BLOCK, LANES), 0)
        real = row < valid_ref[block]
        marks = jnp.where((lane == 67) & real, 1.0, 0.0)
        marks = jnp.where((lane == 68) & jnp.logical_not(real), 1.0, marks)
        for head in range(3):
            own = q_ref[q_rows, head * LANES : (head + 1) * LANES].astype(F32)
            q_ext[head] = jnp.where(lane < 64, own, marks).astype(BF16)
        return q_rows

    def scores_of(slot, head):
        rows = pl.ds(pl.multiple_of(slot * BLOCK, BLOCK), BLOCK)
        return dot_on(keys[head, rows, :], q_ext[head], 1, 1)

    def over_queries(block, carry):
        q_rows = set_queries(block)

        def over_keys(item, carry_in):
            slot = list_ref[plane, block, item]
            rows = pl.ds(pl.multiple_of(slot * BLOCK, BLOCK), BLOCK)
            ready = [scores_of(slot, 0), scores_of(slot, 1)]
            for head in range(3):
                if head == 0:
                    ready.append(scores_of(slot, 2))
                weights = jnp.exp2(ready.pop(0)).astype(BF16)
                acc[head, :, q_rows] += dot_on(values_t[head, :, rows], weights, 1, 0)
            return carry_in

        lax.fori_loop(0, count_ref[plane, block], over_keys, 0)
        return carry

    lax.fori_loop(0, 4, over_queries, 0)
    if not last:
        return
    sums = acc[:, 64:65, :]
    good = (sums >= 2.0**-60) & (sums <= 2.0**100)
    safe = jnp.min(jnp.where(good, 1.0, 0.0)) > 0.5
    top[...] = jnp.zeros_like(top)

    @pl.when(jnp.logical_not(safe))
    def _():
        top[...] = jnp.full_like(top, MASKED)
        acc[...] = jnp.zeros_like(acc)
        for which, source in enumerate(list(before) + [kv_ref]):
            if which < plane:
                move = pltpu.make_async_copy(source, kv_copy, copied)
                move.start()
                move.wait()
                source = kv_copy
            fill_keys(4, source, valid_ref, keys, values_t=values_t, marks_first=4 * which)

            def over_queries_again(block, carry, which=which):
                q_rows = set_queries(block)

                def with_max(item, carry_in):
                    slot = list_ref[which, block, item]
                    rows = pl.ds(pl.multiple_of(slot * BLOCK, BLOCK), BLOCK)
                    for head in range(3):
                        scores = scores_of(slot, head)
                        old = top[head, :, q_rows]
                        now = jnp.maximum(old, jnp.max(scores, axis=0, keepdims=True))
                        weights = jnp.exp2(scores - now).astype(BF16)
                        top[head, :, q_rows] = now
                        acc[head, :, q_rows] = acc[head, :, q_rows] * jnp.exp2(
                            old - now
                        ) + dot_on(values_t[head, :, rows], weights, 1, 0)
                    return carry_in

                lax.fori_loop(0, count_ref[which, block], with_max, 0)
                return carry

            lax.fori_loop(0, 4, over_queries_again, 0)

    for head in range(3):
        total = acc[head, 64:65, :]
        out_ref[head] = (acc[head, 0:64, :] / total).astype(BF16)
        lse_ref[head] = top[head] + jnp.log2(total)


def attend_forward(plane, last, counts, lists, valid, blocks, norms, w_kv, w_q, queries, acc, before):
    kv_rows = 4 * BLOCK
    smem = pl.BlockSpec(memory_space=pltpu.SMEM)
    vmem = pl.BlockSpec(memory_space=pltpu.VMEM)
    anywhere = pl.BlockSpec(memory_space=pl.ANY)
    packed = jax.ShapeDtypeStruct((kv_rows, 3 * LANES), BF16)
    sums = jax.ShapeDtypeStruct((3, 80, kv_rows), F32)
    inputs = [counts, lists, valid] + list(blocks) + [norms, w_kv]
    inputs += [w_q] if plane == 0 else [queries, acc]
    outs = [packed] + ([packed] if plane == 0 else [])
    scratch = [
        pltpu.VMEM((3, kv_rows, LANES), BF16),
        pltpu.VMEM((3, 80, kv_rows), BF16),
        pltpu.VMEM((3, BLOCK, LANES), BF16),
    ]
    in_specs = [smem] * 3 + [vmem] * (len(inputs) - 3)
    if last:
        inputs += list(before)
        in_specs += [anywhere] * len(before)
        outs += [
            jax.ShapeDtypeStruct((3, HDIM, kv_rows), BF16),
            jax.ShapeDtypeStruct((3, 1, kv_rows), F32),
        ]
        scratch += [
            pltpu.VMEM((3, 80, kv_rows), F32),
            pltpu.VMEM((3, 1, kv_rows), F32),
            pltpu.VMEM((kv_rows, 3 * LANES), BF16),
            pltpu.SemaphoreType.DMA,
        ]
    else:
        outs += [sums]
    return pl.pallas_call(
        partial(forward_kernel, plane, last),
        out_shape=tuple(outs),
        in_specs=in_specs,
        out_specs=(vmem,) * len(outs),
        scratch_shapes=scratch,
        compiler_params=pltpu.CompilerParams(vmem_limit_bytes=40 << 20),
        cost_estimate=pl.CostEstimate(
            flops=12 * 1000 * 1000 * 1000, bytes_accessed=10 << 20, transcendentals=7 << 20
        ),
        name="attend_forward",
    )(*inputs)


def backward_kernel(plane, carried, last, *refs):
    refs = list(refs)
    count_ref, list_ref, valid_ref = refs[:3]
    q_ref, kv_ref, out_ref, lse_ref, grad_ref, norm_ref, w_kv_ref, w_q_ref = refs[3:11]
    x_from = [refs[11], refs[13].at[0], refs[12], refs[13].at[1]]
    refs = refs[14:]
    if carried:
        dq_in, dw_in, sum_in = refs[:3]
        refs = refs[3:]
    if last:
        keep_ref, send_ref, dw_out = refs[:3]
        dw_ref, dwq_ref, sum_ref = refs[-3:]
        dq_ref = None
        refs = refs[3:-3]
    else:
        keep_ref, send_ref, dw_ref, dq_ref, sum_ref = refs[:5]
        refs = refs[5:]
    keys, values, q_ext, g_ext, q_turned, dq_acc, dkv_acc, x_ref, moved = refs
    slots = 4
    moves = [
        pltpu.make_async_copy(x_from[i], x_ref.at[pl.ds(i * BLOCK, BLOCK)], moved.at[i])
        for i in range(slots)
    ]
    if carried:
        moves.append(pltpu.make_async_copy(dq_in, dq_acc, moved.at[4]))
    for move in moves:
        move.start()
    fill_keys(slots, kv_ref, valid_ref, keys, values_out=values, marks_first=4 * plane)
    lane = lax.broadcasted_iota(jnp.int32, (BLOCK, LANES), 1)

    def clear(slot, carry):
        rows = pl.ds(pl.multiple_of(slot * BLOCK, BLOCK), BLOCK)
        for head in range(3):
            dkv_acc[head, :, rows] = jnp.zeros((LANES, BLOCK), F32)
        return carry

    lax.fori_loop(0, slots, clear, 0)
    if carried:
        moves[4].wait()
    else:
        dq_acc[...] = jnp.zeros_like(dq_acc)

    def over_queries(block, carry):
        q_rows = pl.ds(pl.multiple_of(block * BLOCK, BLOCK), BLOCK)
        for head in range(3):
            lanes = slice(head * LANES, (head + 1) * LANES)
            turned = q_ref[q_rows, lanes].astype(F32).T[0:64]
            grad_t = grad_ref[head, :, q_rows].astype(F32)
            delta = jnp.sum(grad_t * out_ref[head, :, q_rows].astype(F32), axis=0, keepdims=True)
            marks = split_three(-lse_ref[head, :, q_rows]) + query_marks(valid_ref[block], BLOCK)
            blank = jnp.zeros((64 - len(marks), BLOCK), F32)
            q_turned[head] = turned.astype(BF16)
            q_ext[head] = jnp.concatenate([turned] + marks + [blank], axis=0).T.astype(BF16)
            minus = split_three(-delta)
            blank = jnp.zeros((64 - len(minus), BLOCK), F32)
            g_ext[head] = jnp.concatenate(minus + [blank, grad_t], axis=0).T.astype(BF16)

        def over_keys(item, carry_in):
            slot = list_ref[plane, block, item]
            rows = pl.ds(pl.multiple_of(slot * BLOCK, BLOCK), BLOCK)

            def products(head):
                return (
                    dot_on(q_ext[head], keys[head, rows, :], 1, 1),
                    dot_on(g_ext[head], values[head, rows, :], 1, 1),
                )

            ready = [products(0)]
            for head in range(3):
                lanes = slice(head * LANES, (head + 1) * LANES)
                if head < 2:
                    ready.append(products(head + 1))
                scores, grad_probs = ready.pop(0)
                probs = jnp.exp2(scores)
                grad_scores = (probs * grad_probs).astype(BF16)
                dkv_acc[head, 64:128, rows] += dot_on(
                    grad_ref[head, :, q_rows], probs.astype(BF16), 1, 0
                )
                dkv_acc[head, 0:64, rows] += dot_on(q_turned[head], grad_scores, 1, 0)
                dq_acc[q_rows, lanes] += dot_on(grad_scores, keys[head, rows, :], 1, 0)
            return carry_in

        lax.fori_loop(0, count_ref[plane, block], over_keys, 0)
        return carry

    lax.fori_loop(0, 4, over_queries, 0)
    for move in moves[:4]:
        move.wait()
    if not last:
        leave = pltpu.make_async_copy(dq_acc, dq_ref, moved.at[4])
        leave.start()
    if carried:
        dw_ref[...] = dw_in[...]
        sum_ref[...] = sum_in[...]
    else:
        dw_ref[...] = jnp.zeros_like(dw_ref)
        sum_ref[...] = jnp.zeros_like(sum_ref)
    if last:
        dwq_ref[...] = jnp.zeros_like(dwq_ref)
    gain, bias = norm_ref[0:1, :], norm_ref[1:2, :]

    def finish(slot, carry):
        rows = pl.ds(pl.multiple_of(slot * BLOCK, BLOCK), BLOCK)
        pieces = []
        for head in range(3):
            pieces.append(dkv_acc[head, 0:64, rows] * LN2)
            pieces.append(dkv_acc[head, 64:128, rows])
        turned = jnp.concatenate(pieces, axis=0)
        part = dot_on(turned.T.astype(BF16), w_kv_ref[...], 1, 0)
        values_now = x_ref[rows, :].astype(F32)
        normed, unit, ignored = norm_rows(values_now, gain, bias)
        normed = normed.astype(BF16)
        dw_ref[...] += dot_on(turned.astype(BF16), normed, 1, 0)
        if last:
            scaled = [
                jnp.where(lane < 64, dq_acc[rows, h * LANES : (h + 1) * LANES], 0.0)
                for h in range(3)
            ]
            scaled = jnp.concatenate(scaled, axis=1) * HDIM ** (-0.5)
            part = part + dot_on(scaled.astype(BF16), w_q_ref[...], 1, 0)
            dwq_ref[...] += dot_on(scaled.T.astype(BF16), normed, 1, 0)
        sum_ref[0:1, :] += jnp.sum(part * unit, axis=0, keepdims=True)
        sum_ref[1:2, :] += jnp.sum(part, axis=0, keepdims=True)
        low = part.astype(BF16)

        @pl.when(slot % 2 == 0)
        def _():
            keep_ref[slot // 2] = low

        @pl.when(slot % 2 == 1)
        def _():
            send_ref[slot // 2] = low

        return carry

    lax.fori_loop(0, slots, finish, 0)
    if not last:
        leave.wait()
        return
    pieces = []
    for head in range(3):
        first = head * LANES
        pieces.append(dwq_ref[first : first + 64, :])
        pieces.append(dw_ref[first : first + LANES, :])
    pieces += [sum_ref[...], jnp.zeros((LANES - 8, D), F32)]
    dw_out[...] = jnp.concatenate(pieces, axis=0).T.astype(BF16)


def attend_backward(
    plane, counts, lists, valid, queries, key_vals, attended, lse, grads, norms, w_kv_t, w_q_t, blocks, carry, last
):
    q_rows = queries.shape[0]
    smem = pl.BlockSpec(memory_space=pltpu.SMEM)
    vmem = pl.BlockSpec(memory_space=pltpu.VMEM)
    anywhere = pl.BlockSpec(memory_space=pl.ANY)
    carry = list(carry)
    half = jax.ShapeDtypeStruct((2, BLOCK, D), BF16)
    weight = jax.ShapeDtypeStruct((3 * LANES, D), F32)
    sums = jax.ShapeDtypeStruct((8, D), F32)
    if last:
        outs = (jax.ShapeDtypeStruct((D, 9 * HDIM + LANES), BF16),)
        spaces, kept = (vmem,), [weight, weight, sums]
    else:
        outs = (weight, jax.ShapeDtypeStruct((q_rows, 3 * LANES), F32), sums)
        spaces, kept = (vmem, anywhere, vmem), []
    result = pl.pallas_call(
        partial(backward_kernel, plane, bool(carry), last),
        out_shape=(half, half) + outs,
        in_specs=[smem] * 3 + [vmem] * 8 + [anywhere] * 3 + [anywhere, vmem, vmem][: len(carry)],
        out_specs=(vmem, vmem) + spaces,
        scratch_shapes=[
            pltpu.VMEM((3, q_rows, LANES), BF16),
            pltpu.VMEM((3, q_rows, LANES), BF16),
            pltpu.VMEM((3, BLOCK, LANES), BF16),
            pltpu.VMEM((3, BLOCK, LANES), BF16),
            pltpu.VMEM((3, HDIM, BLOCK), BF16),
            pltpu.VMEM((q_rows, 3 * LANES), F32),
            pltpu.VMEM((3, LANES, q_rows), F32),
            pltpu.VMEM((q_rows, D), BF16),
            pltpu.SemaphoreType.DMA((5,)),
        ]
        + [pltpu.VMEM(k.shape, k.dtype) for k in kept],
        compiler_params=pltpu.CompilerParams(vmem_limit_bytes=44 << 20),
        cost_estimate=pl.CostEstimate(
            flops=25 * 1000 * 1000 * 1000, bytes_accessed=16 << 20, transcendentals=7 << 20
        ),
        name="attend_backward",
    )(
        counts, lists, valid, queries, key_vals, attended, lse, grads, norms, w_kv_t, w_q_t, *blocks, *carry
    )
    return tuple(result) + (None,) * (5 - len(result))


def erf_of(values):
    clamped = jnp.clip(values, -4.0, 4.0)
    square = clamped * clamped
    top = jnp.float32(-2.72614225801306e-10)
    for term in (
        2.77068142495902e-08,
        -2.10102402082508e-06,
        -5.69250639462346e-05,
        -7.34990630326855e-04,
        -2.95459980854025e-03,
        -1.60960333262415e-02,
    ):
        top = top * square + term
    low = jnp.float32(-1.45660718464996e-05)
    for term in (
        -2.13374055278905e-04,
        -1.68282697438203e-03,
        -7.37332916720468e-03,
        -1.42647390514189e-02,
    ):
        low = low * square + term
    return clamped * top / low


def middle_kernel(pieces, pair, shard, *refs):
    refs = list(refs)
    start_ref, group_ref = refs[:2]
    merged_refs, refs = refs[2:6], refs[6:]
    token_ref, cot_ref, norm_ref = refs[:3]
    piece_refs, refs = refs[3 : 3 + pieces], refs[3 + pieces :]
    output_ref, grad_y_ref, grad_z_ref, h_two_ref, hidden_ref, grad_up_ref = refs[:6]
    part_refs, sum_ref, refs = refs[6:10], refs[10], refs[11:]
    w_out, w_up, w_down, moved = refs
    parts = []
    for piece in piece_refs:
        parts += [(piece, base) for base in range(0, piece.shape[0], 9 * pair)]

    def moves_of(weight):
        moves = []
        for i, (piece, base) in enumerate(parts):
            if weight < 5:
                source = piece.at[pl.ds(base + weight * pair, pair)]
                rows = pl.ds(pl.multiple_of(start_ref[i] * shard, pair), pair)
                target = w_out.at[rows] if weight == 0 else w_up.at[weight - 1, rows]
            else:
                source = piece.at[pl.ds(base + 5 * pair, 4 * pair)]
                rows = pl.ds(pl.multiple_of(start_ref[i] * 4 * shard, 4 * pair), 4 * pair)
                target = w_down.at[rows]
            moves.append(pltpu.make_async_copy(source, target, moved.at[weight, i]))
        return moves

    arriving = [moves_of(weight) for weight in range(6)]
    for weight in (0, 1, 5, 2, 3, 4):
        for move in arriving[weight]:
            move.start()
    for move in arriving[0]:
        move.wait()
    y_one = token_ref[...].astype(F32)
    group = D // 4
    for j, merged_ref in enumerate(merged_refs):
        rows = pl.ds(pl.multiple_of(group_ref[j] * group, group), group)
        turned = merged_ref[...].astype(F32).T.astype(BF16)
        y_one = y_one + dot_on(turned, w_out[rows, :], 1, 0)
    grad_y_ref[...] = y_one
    gain, bias = norm_ref[0:1, :], norm_ref[1:2, :]
    normed, unit, inv_rows = norm_rows(y_one, gain, bias)
    h_two_ref[...] = normed.astype(BF16)

    output_sum = jnp.zeros((BLOCK, D), F32)
    grad_sum = jnp.zeros((BLOCK, D), F32)
    for j in range(4):
        for move in arriving[1 + j]:
            move.wait()
        if j == 0:
            for move in arriving[5]:
                move.wait()
        columns = slice(j * D, (j + 1) * D)
        up = dot_on(h_two_ref[...], w_up[j], 1, 0)
        grad_hidden = dot_on(cot_ref[...], w_down[columns, :], 1, 1)
        normal = 0.5 + 0.5 * erf_of(up * 0.7071067811865476)
        density = jnp.exp(-0.5 * up * up) * 0.3989422804014327
        hidden = (up * normal).astype(BF16)
        grad_up = (grad_hidden * (normal + up * density)).astype(BF16)
        hidden_ref[:, columns] = hidden
        grad_up_ref[:, columns] = grad_up
        output_sum = output_sum + dot_on(hidden, w_down[columns, :], 1, 0)
        grad_sum = grad_sum + dot_on(grad_up, w_up[j], 1, 1)
    y_one = grad_y_ref[...]
    output_ref[...] = (y_one + output_sum).astype(BF16)
    normed, unit, inv_rows = norm_rows(y_one, gain, bias)
    sum_ref[...] = jnp.zeros_like(sum_ref)
    sum_ref[0:1, :] = jnp.sum(grad_sum * unit, axis=0, keepdims=True)
    sum_ref[1:2, :] = jnp.sum(grad_sum, axis=0, keepdims=True)
    grad_y = cot_ref[...].astype(F32) + norm_back(grad_sum, unit, inv_rows, gain)
    grad_y_ref[...] = grad_y
    grad_z = grad_y.astype(BF16)
    grad_z_ref[...] = grad_z
    for j, part_ref in enumerate(part_refs):
        rows = pl.ds(pl.multiple_of(group_ref[j] * group, group), group)
        part_ref[...] = dot_on(w_out[rows, :], grad_z, 1, 1).astype(BF16)


def middle(starts, groups, merged, tokens, cotangent, norms, pieces, shard):
    smem = pl.BlockSpec(memory_space=pltpu.SMEM)
    vmem = pl.BlockSpec(memory_space=pltpu.VMEM)
    anywhere = pl.BlockSpec(memory_space=pl.ANY)
    rows = tokens.shape[0]
    number = starts.shape[0]
    pair = sum(piece.shape[0] for piece in pieces) // (9 * number)

    def shape(columns, dtype, height=rows):
        return jax.ShapeDtypeStruct((height, columns), dtype)

    return pl.pallas_call(
        partial(middle_kernel, len(pieces), pair, shard),
        out_shape=(
            shape(D, BF16),
            shape(D, F32),
            shape(D, BF16),
            shape(D, BF16),
            shape(4 * D, BF16),
            shape(4 * D, BF16),
        )
        + (shape(rows, BF16, D // 4),) * 4
        + (shape(D, F32, 8),),
        in_specs=[smem, smem] + [vmem] * 7 + [anywhere] * len(pieces),
        out_specs=(vmem,) * 11,
        scratch_shapes=[
            pltpu.VMEM((D, D), BF16),
            pltpu.VMEM((4, D, D), BF16),
            pltpu.VMEM((4 * D, D), BF16),
            pltpu.SemaphoreType.DMA((6, number)),
        ],
        compiler_params=pltpu.CompilerParams(vmem_limit_bytes=56 << 20),
        cost_estimate=pl.CostEstimate(
            flops=12 * 1000 * 1000 * 1000, bytes_accessed=24 << 20, transcendentals=3 << 20
        ),
        name="middle",
    )(starts, groups, *merged, tokens, cotangent, norms, *pieces)


def scene_lists(same):
    number = same.shape[-1]
    slot = jnp.arange(number)
    counts = jnp.sum(same, axis=-1).astype(jnp.int32)
    earlier = slot[None, :] < slot[:, None]
    place = jnp.sum(same[:, :, None, :] & earlier, axis=-1)
    hits = same[:, :, None, :] & (place[:, :, None, :] == slot[:, None])
    lists = jnp.sum(jnp.where(hits, slot, 0), axis=-1)
    return counts, lists.astype(jnp.int32)


def halve(value, axis, bit, send):
    keep = lax.dynamic_index_in_dim(value, bit, axis, keepdims=False)
    give = lax.dynamic_index_in_dim(value, 1 - bit, axis, keepdims=False)
    return (keep.astype(F32) + send(give).astype(F32)).astype(BF16)


def ring_sources(count):
    order = ring_order(count)
    table = [[order[(order.index(c) - r) % count] for r in range(count)] for c in range(count)]
    return jnp.array(table, jnp.int32)[lax.axis_index("ctx")]


def sum_over_seq(value):
    count = lax.axis_size("seq")
    me = lax.axis_index("seq")
    while count > 1:
        count //= 2
        bit = (me // count) % 2
        pairs = [(i, i ^ count) for i in range(lax.axis_size("seq"))]
        value = halve(
            value.reshape((2, count) + value.shape[1:]),
            0,
            bit,
            lambda give: lax.ppermute(give, "seq", pairs),
        )
    return value.reshape(value.shape[1:])


def gather_bit(value, bit, send):
    other = send(value)
    first = jnp.where(bit == 0, value, other)
    return jnp.concatenate([first, jnp.where(bit == 0, other, value)], axis=0)


def gather_seq(value):
    count, reach = lax.axis_size("seq"), 1
    me = lax.axis_index("seq")
    while reach < count:
        pairs = [(i, i ^ reach) for i in range(count)]
        value = gather_bit(
            value[None], (me // reach) % 2, lambda v: lax.ppermute(v, "seq", pairs)
        ).reshape((2 * reach,) + value.shape[1:])
        reach *= 2
    return value


def swap_seq(value, mask=1):
    return lax.ppermute(value, "seq", [(i, i ^ mask) for i in range(lax.axis_size("seq"))])


def in_order(blocks, sources, shard):
    count = len(blocks)
    full = jnp.zeros((count,) + blocks[0].shape, BF16)
    for r in range(count):
        full = lax.dynamic_update_index_in_dim(full, blocks[r], sources[r], 0)
    cuts = []
    for half in range(2):
        part = full[half * (count // 2) : (half + 1) * (count // 2)]
        cut = [part[:, i * shard : (i + 1) * shard] for i in range(5)] + [part[:, 5 * shard :]]
        cuts += [c.reshape(-1, D) for c in cut]
    return jnp.concatenate(cuts, axis=0)


def join_halves(pieces, places, number):
    def woven(first, second):
        rows = first.shape[0] // 9
        cuts = [i * rows for i in range(1, 6)]
        both = zip(jnp.split(first, cuts), jnp.split(second, cuts))
        return jnp.concatenate([part for pair in both for part in pair], axis=0)

    joined, kept = [], []
    for base in range(0, len(pieces), number):
        for i in (0, 1):
            joined.append(woven(*jnp.split(pieces[base + i], 2)))
            kept.append(((0,),) + places[base + i][1:])
        for i in (2, 4):
            joined.append(woven(pieces[base + i], pieces[base + i + 1]))
            kept.append(((0,),) + places[base + i][1:])
    return joined, kept


def gather_ctx(value):
    count = lax.axis_size("ctx")
    sources = ring_sources(count)
    whole = jnp.zeros((count,) + value.shape, value.dtype)
    whole = lax.dynamic_update_index_in_dim(whole, value, sources[0], 0)
    for r in range(1, count):
        whole = lax.dynamic_update_index_in_dim(whole, ring_send(value, r), sources[r], 0)
    return whole


def sum_over_core(value):
    seqs, ctxs = lax.axis_size("seq"), lax.axis_size("ctx")
    rows = value.shape[0] // (seqs * ctxs * 4)
    value = value.reshape(seqs, 2, 2, ctxs, rows, value.shape[1])
    bit = lax.axis_index("head") % 2
    return halve(value, 2, bit, lambda give: swap_head(give, 1))


def sum_over_x(value):
    bit = lax.axis_index("head") // 2
    return halve(value, 0, bit, lambda give: swap_head(give, 2))


def send_term(value, r):
    source = ring_sources(lax.axis_size("ctx"))[r]
    return ring_send(lax.dynamic_index_in_dim(value, source, 0, keepdims=False), -r)


def sum_terms(value, terms):
    source = ring_sources(lax.axis_size("ctx"))[0]
    total = lax.dynamic_index_in_dim(value, source, 0, keepdims=False).astype(F32)
    for term in terms:
        total = total + term.astype(F32)
    return total


def sum_over_ctx(value):
    count = lax.axis_size("ctx")
    sources = ring_sources(count)
    total = lax.dynamic_index_in_dim(value, sources[0], 0, keepdims=False).astype(F32)
    for r in range(1, count):
        give = lax.dynamic_index_in_dim(value, sources[r], 0, keepdims=False)
        total = total + ring_send(give, -r).astype(F32)
    return total


def tie(*values):
    return lax.optimization_barrier(values)


def body(
    tokens,
    segment_ids,
    w_qkv,
    w_out,
    w_up,
    w_down,
    gain_one,
    bias_one,
    gain_two,
    bias_two,
    cotangent,
):
    heads_ax = lax.axis_size("head")
    ctx_ax = lax.axis_size("ctx")
    seq_ax = lax.axis_size("seq")
    me_head = lax.axis_index("head")
    tok_rows = tokens.shape[0]
    group = D // heads_ax
    shard = w_qkv.shape[0]

    order = [me_head ^ j for j in range(heads_ax)]
    sources = ring_sources(ctx_ax)

    padding = tok_rows - jnp.sum(segment_ids >= 0)
    about = jnp.stack([segment_ids[0], padding // 16, padding % 16]).astype(BF16)
    extra = jnp.stack([gain_one, bias_one, gain_two, bias_two], axis=1)
    extra = jnp.concatenate([extra, jnp.broadcast_to(about[None, :], (shard, 3))], axis=1)
    extra = jnp.pad(extra, ((0, 0), (0, LANES - 7)))
    packed = jnp.swapaxes(w_qkv.reshape(shard, heads_ax, 3 * group), 0, 1)
    packed = jnp.concatenate(
        [packed, jnp.broadcast_to(extra[None], (heads_ax,) + extra.shape)], axis=2
    )
    wide = 3 * group + LANES
    mine = jnp.zeros((heads_ax, shard, wide), BF16)
    for j in range(heads_ax):
        piece = lax.dynamic_index_in_dim(packed, order[j], 0, keepdims=False)
        piece = swap_head(piece, j) if j else piece
        mine = lax.dynamic_update_index_in_dim(mine, piece, order[j], 0)
    ring_mine = [mine] + [ring_send(mine, i) for i in range(1, ctx_ax)]

    w_rest = jnp.concatenate(
        [w_out] + [w_up[:, i * D : (i + 1) * D] for i in range(4)] + [w_down], axis=0
    )
    rest = [w_rest]
    near, ahead, behind = swap_head(tokens, 2), ring_send(tokens, 1), ring_send(w_rest, 1)
    near, ahead, behind, *ring_mine = tie(near, ahead, behind, *ring_mine)
    rest.append(behind)
    packed = jnp.zeros((ctx_ax,) + mine.shape, BF16)
    for r in range(ctx_ax):
        packed = lax.dynamic_update_index_in_dim(packed, ring_mine[r], sources[r], 0)

    def weights_here(packed):
        packed = jnp.swapaxes(gather_seq(packed[None]), 1, 2).reshape(D, wide)
        g_one, b_one, g_two, b_two = [packed[:, 3 * group + i].astype(F32) for i in range(4)]
        norm_one = jnp.pad(jnp.stack([g_one, b_one]), ((0, 6), (0, 0)))
        w_mine = packed[:, : 3 * group].reshape(D, 3, 3, HDIM)
        w_kv = w_mine[:, :, 1:].reshape(D, 6 * HDIM)
        w_q = jnp.pad(w_mine[:, :, :1], ((0, 0), (0, 0), (0, 1), (0, 0))).reshape(D, 6 * HDIM)
        about_all = packed[::shard, 3 * group + 4 : 3 * group + 7].astype(jnp.int32)
        about_all = lax.dynamic_index_in_dim(
            about_all.reshape(seq_ax, heads_ax, ctx_ax, 3), lax.axis_index("seq"), 0, keepdims=False
        )
        pick_head = jnp.stack(order)[:, None] == jnp.arange(heads_ax)[None, :]
        pick_ctx = sources[:, None] == jnp.arange(ctx_ax)[None, :]
        pick = pick_ctx[:, None, None, :] & pick_head[None, :, :, None]
        slot_about = jnp.sum(jnp.where(pick[..., None], about_all[None, None], 0), axis=(2, 3))
        slot_ids = slot_about[:, :, 0]
        slot_valid = (tok_rows - (slot_about[:, :, 1] * 16 + slot_about[:, :, 2])).reshape(-1)
        counts, lists = scene_lists(slot_ids[0][None, :, None] == slot_ids[:, None, :])
        return (g_one, b_one, g_two, b_two), norm_one, (w_kv, w_q), (counts, lists, slot_valid)

    planes, key_vals, queries, acc = [], [], None, None
    block = tokens
    ready = None
    for r in range(ctx_ax + 1):
        if r < ctx_ax:
            travelers = [swap_head(jnp.stack([block, near]), 1)]
        else:
            travelers = []
        if r + 1 < ctx_ax:
            travelers.append(swap_head(ahead, 2))
        if r + 2 < ctx_ax:
            travelers.append(ring_send(ahead, 1))
            travelers.append(ring_send(rest[-1], 1))
        count = len(travelers)
        if r == ctx_ax - 2:
            line = in_order(rest, sources, shard)
            middle_row = line.shape[0] // 2
            travelers += [swap_head(line[:middle_row], 2), swap_seq(line)]
        if r == ctx_ax - 1:
            travelers += [swap_head(line[middle_row:], 2), swap_seq(x_first), swap_head(line, 1)]
        if r == ctx_ax:
            travelers += [swap_seq(x_second), swap_head(y_line, 1), swap_head(x_first, 1)]
        results = []
        if ready is not None:
            results = list(
                attend_forward(
                    r - 1,
                    r == ctx_ax,
                    counts,
                    lists,
                    slot_valid,
                    ready,
                    norm_one,
                    w_kv,
                    w_q,
                    queries,
                    acc,
                    key_vals,
                )
            )
        tied = list(tie(*travelers, *results))
        extra, tied = tied[count : len(travelers)], tied[:count] + tied[len(travelers) :]
        if r == 0:
            norms, norm_one, weights, scenes = weights_here(packed)
            g_one, b_one, g_two, b_two = norms
            w_kv, w_q = weights
            w_kv_t, w_q_t = w_kv.T, w_q.T
            counts, lists, slot_valid = scenes
        if r == ctx_ax - 2:
            x_first, y_line = extra
        if r == ctx_ax - 1:
            x_second, xy_first, core_line = extra
        if r == ctx_ax:
            xy_second, core_y, core_x_first = extra
            results = tied
            break
        planes.append([block, near, tied.pop(0)])
        ready = planes[-1]
        if r + 1 < ctx_ax:
            block, near = ahead, tied.pop(0)
        if r + 2 < ctx_ax:
            ahead = tied.pop(0)
            rest.append(tied.pop(0))
        if results:
            key_vals.append(tied.pop(0))
            if r == 1:
                queries = tied.pop(0)
            acc = tied.pop(0)
    key_vals.append(results[0])
    attended, lse = results[1:]
    owns = [line, y_line, x_first, x_second, xy_first, xy_second]
    cores = [core_line, core_y, core_x_first]
    cores += [swap_head(v, 1) for v in (x_second, xy_first, xy_second)]
    offs = [((0, 1), 0, 0), ((0, 1), 0, 1), ((0,), 1, 0), ((1,), 1, 0), ((0,), 1, 1), ((1,), 1, 1)]
    me_x, me_core, me_seq = me_head // 2, me_head % 2, lax.axis_index("seq")
    pieces, places = [], []
    for core, arrays in enumerate((owns, cores)):
        for array, (halves, x, y) in zip(arrays, offs):
            pieces.append(array)
            places.append((halves, (me_x ^ x) * 2 + (me_core ^ core), y))
    reach = 2
    while reach < seq_ax:
        pieces += [swap_seq(array, reach) for array in pieces]
        places += [(halves, place, y ^ reach) for halves, place, y in places]
        reach *= 2
    if (ctx_ax // 2 * shard) % 8:
        pieces, places = join_halves(pieces, places, len(offs))
    starts = [
        ((me_seq ^ y) * heads_ax + place) * ctx_ax + half * (ctx_ax // 2)
        for halves, place, y in places
        for half in halves
    ]
    starts = jnp.stack(starts).astype(jnp.int32)

    merged = []
    for j in range(heads_ax):
        part = attended[:, :, j * tok_rows : (j + 1) * tok_rows].reshape(group, tok_rows)
        merged.append(swap_head(part, j) if j else part)

    norm_two = jnp.pad(jnp.stack([g_two, b_two]), ((0, 6), (0, 0)))
    groups = jnp.stack(order).astype(jnp.int32)
    output, grad_y_one, grad_z, h_two, hidden, grad_up, *rest_out = middle(
        starts, groups, merged, tokens, cotangent, norm_two, pieces, shard
    )
    grad_merged, sums_two = rest_out[:4], rest_out[4]

    grad_parts = [swap_head(p, j) if j else p for j, p in enumerate(grad_merged)]
    grad_w_down = jnp.einsum("tf,td->fd", hidden, cotangent, preferred_element_type=F32)
    down_sum = sum_over_core(grad_w_down.astype(BF16))
    grad_w_up = jnp.einsum("td,tf->df", h_two, grad_up, preferred_element_type=F32)
    grad_w_up = grad_w_up.astype(BF16)
    grad_w_out = jnp.zeros((heads_ax, group, D), BF16)
    for j in range(heads_ax):
        part = jnp.einsum("at,td->ad", merged[j], grad_z, preferred_element_type=F32)
        grad_w_out = lax.dynamic_update_index_in_dim(grad_w_out, part.astype(BF16), order[j], 0)
    sums_two = jnp.pad(sums_two, ((0, LANES - 8), (0, 0))).T.astype(BF16)
    grad_w_out = jnp.concatenate([grad_w_out.reshape(D, D), sums_two], axis=1)
    tied = tie(down_sum, grad_w_up, grad_w_out, *grad_parts)
    down_sum, grad_w_up, grad_w_out = tied[:3]
    grad_local = jnp.concatenate(tied[3:], axis=1).reshape(3, HDIM, heads_ax * tok_rows)
    up_sum, out_sum = sum_over_core(grad_w_up), sum_over_core(grad_w_out)
    down_sum = sum_over_seq(down_sum)

    carry, traveling, near_half, far_half = (), None, None, None
    for r in reversed(range(ctx_ax)):
        step = ctx_ax - 1 - r
        travelers = []
        if step >= 1:
            travelers.append(swap_head(far_half, 2))
        if step >= 2:
            travelers.append(ring_send(traveling, -1))
        count = len(travelers)
        if step == 0:
            travelers += [down_sum, up_sum, out_sum]
        if step == 1:
            wide_sum = sum_over_seq(jnp.concatenate([up_sum, out_sum], axis=-1))
            travelers += [sum_over_x(down_sum), wide_sum]
        if step == 2:
            travelers += [sum_over_x(wide_sum)] + [send_term(down_sum, i) for i in (1, 3)]
        if step == 3:
            travelers += [send_term(down_sum, 2)] + [send_term(wide_sum, i) for i in (1, 3)]
        keep, give, dw, fourth, sums = attend_backward(
            r,
            counts,
            lists,
            slot_valid,
            queries,
            key_vals[r],
            attended,
            lse,
            grad_local,
            norm_one,
            w_kv_t,
            w_q_t,
            planes[r],
            carry,
            r == 0,
        )
        if r == 0:
            keep, give, dw, *travelers = tie(keep, give, dw, *travelers)
        else:
            keep, give, fourth, dw, sums, *travelers = tie(
                keep, give, fourth, dw, sums, *travelers
            )
        extra = travelers[count:]
        if step >= 1:
            moved = near_half.astype(F32) + travelers[0].astype(F32)
            if step >= 2:
                moved = moved + travelers[1].astype(F32)
            traveling = moved.astype(BF16)
        if step == 0:
            down_sum, up_sum, out_sum = extra
        if step == 1:
            down_sum, wide_sum = extra
        if step == 2:
            wide_sum, *down_terms = extra
        if step == 3:
            down_terms.append(extra[0])
            wide_terms = extra[1:]
        taken = swap_head(give, 1)
        near_half = (keep[0].astype(F32) + taken[0].astype(F32)).astype(BF16)
        far_half = (keep[1].astype(F32) + taken[1].astype(F32)).astype(BF16)
        if r:
            tied = [near_half, far_half, fourth, dw, sums, down_sum]
            tied += [up_sum, out_sum] if step == 0 else [wide_sum]
            tied += [traveling] if step >= 1 else []
            near_half, far_half, fourth, dw, sums, down_sum, *tied = tie(*tied)
            if step == 0:
                up_sum, out_sum, *tied = tied
            else:
                wide_sum, *tied = tied
            if step >= 1:
                traveling = tied[0]
        carry = (fourth, dw, sums)
    near_half, far_half, traveling, dw, wide_sum = tie(
        near_half, far_half, traveling, dw, wide_sum
    )
    dw_mine = sum_over_seq(dw.reshape(seq_ax, heads_ax, ctx_ax, shard, wide))
    taken, carried, term, dw_mine = tie(
        swap_head(far_half, 2), ring_send(traveling, -1), send_term(wide_sum, 2), dw_mine
    )
    grad_h_one = near_half.astype(F32) + taken.astype(F32) + carried.astype(F32)
    wide_terms.append(term)
    down_sum, wide_sum = sum_terms(down_sum, down_terms), sum_terms(wide_sum, wide_terms)
    up_sum, out_sum = wide_sum[:, : 4 * D], wide_sum[:, 4 * D :]
    dw_mine = sum_over_ctx(jnp.swapaxes(dw_mine, 0, 1)).astype(BF16)
    groups = []
    for j in range(heads_ax):
        part = lax.dynamic_index_in_dim(dw_mine, order[j], 0, keepdims=False)
        groups.append(swap_head(part, j) if j else part)
    groups = jnp.stack(groups)
    groups = jnp.stack(
        [lax.dynamic_index_in_dim(groups, o, 0, keepdims=False) for o in order]
    ).astype(F32)
    grad_w_qkv = jnp.swapaxes(groups[:, :, : 3 * group], 0, 1).reshape(shard, 3 * D)
    norm_sums = jnp.sum(groups[:, :, 3 * group : 3 * group + 2], axis=0)

    ignored, unit_one, inv_one = norm_rows(tokens.astype(F32), g_one, b_one)
    grad_tokens = (grad_y_one + norm_back(grad_h_one, unit_one, inv_one, g_one)).astype(BF16)
    return (
        output,
        grad_tokens,
        grad_w_qkv,
        out_sum[:, :D],
        up_sum,
        down_sum,
        norm_sums[:, 0],
        norm_sums[:, 1],
        out_sum[:, D],
        out_sum[:, D + 1],
    )


def solution(mesh):
    rows = P(ALL_AXES, None)
    vector = P(ALL_AXES)
    return jax.shard_map(
        body,
        mesh=mesh,
        in_specs=(rows, vector, rows, rows, rows, rows, vector, vector, vector, vector, rows),
        out_specs=(rows, rows, rows, rows, rows, rows, vector, vector, vector, vector),
        check_vma=False,
    )
```

```python
from functools import partial

import jax
import jax.numpy as jnp
from jax import lax
from jax.experimental import pallas as pl
from jax.experimental.pallas import tpu as pltpu
from jax.sharding import PartitionSpec as P

D = 768
HEADS = 12
HDIM = 64
BLOCK = 512
LANES = 128
EPSILON = 1e-05
MASKED = -1e30
LOG2E = 1.4426950408889634
LN2 = 0.6931471805599453
ALL_AXES = ("seq", "head", "ctx")
BF16 = jnp.bfloat16
F32 = jnp.float32


def dot_on(left, right, left_dim, right_dim):
    return lax.dot_general(
        left, right, (((left_dim,), (right_dim,)), ((), ())), preferred_element_type=F32
    )


def norm_rows(values, gain_vec, bias_vec):
    row_mean = jnp.mean(values, axis=-1, keepdims=True)
    centered = values - row_mean
    variance = jnp.mean(centered * centered, axis=-1, keepdims=True)
    inv_rows = lax.rsqrt(variance + EPSILON)
    unit_rows = centered * inv_rows
    return (unit_rows * gain_vec + bias_vec, unit_rows, inv_rows)


def norm_back(grad_norm, unit_rows, inv_rows, gain_vec):
    scaled = grad_norm * gain_vec
    return inv_rows * (
        scaled
        - jnp.mean(scaled, axis=-1, keepdims=True)
        - unit_rows * jnp.mean(scaled * unit_rows, axis=-1, keepdims=True)
    )


def gelu_exact(values):
    return jax.nn.gelu(values, approximate=False)


def swap_head(value, mask):
    count = lax.axis_size("head")
    return lax.ppermute(value, "head", [(i, i ^ mask) for i in range(count)])


def ring_order(count):
    return [0, 1, 3, 2] if count == 4 else list(range(count))


def ring_pairs(count, step):
    order = ring_order(count)
    return [(order[i], order[(i + step) % count]) for i in range(count)]


def ring_send(value, step):
    return lax.ppermute(value, "ctx", ring_pairs(lax.axis_size("ctx"), step))


def plane_blocks(block):
    near = swap_head(block, 2)
    return [block, swap_head(block, 1), near, swap_head(near, 1)]


def split_three(values):
    high = values.astype(BF16)
    rest = values - high.astype(F32)
    middle = rest.astype(BF16)
    low = (rest - middle.astype(F32)).astype(BF16)
    return [high.astype(F32), middle.astype(F32), low.astype(F32)]


def key_marks(valid, lane):
    row = lax.broadcasted_iota(jnp.int32, (BLOCK, LANES), 0)
    real = row < valid
    marks = jnp.where((lane >= 64) & (lane < 67), 1.0, 0.0)
    marks = jnp.where((lane == 67) & jnp.logical_not(real), MASKED, marks)
    return jnp.where((lane == 68) & real, MASKED, marks)


def fill_keys(slots, kv_ref, valid_ref, keys_out, values_t=None, values_out=None, marks_first=0):
    lane = lax.broadcasted_iota(jnp.int32, (BLOCK, LANES), 1)

    def fill(slot, carry):
        rows = pl.ds(pl.multiple_of(slot * BLOCK, BLOCK), BLOCK)
        marks = key_marks(valid_ref[slot + marks_first], lane)
        for head in range(3):
            pair = kv_ref[rows, head * LANES : (head + 1) * LANES].astype(F32)
            keys_out[head, rows, :] = jnp.where(lane < 64, pair, marks).astype(BF16)
            if values_out is not None:
                ones = jnp.where(lane < 3, 1.0, 0.0)
                values_out[head, rows, :] = jnp.where(lane < 64, ones, pair).astype(BF16)
            if values_t is not None:
                turned = pair.T[64:128].astype(BF16)
                values_t[head, :, rows] = jnp.concatenate(
                    [turned, jnp.ones((16, BLOCK), BF16)], axis=0
                )
        return carry

    lax.fori_loop(0, slots, fill, 0)


def query_marks(valid, width):
    row = lax.broadcasted_iota(jnp.int32, (1, width), 1)
    real = jnp.where(row < valid, 1.0, 0.0)
    return [real, 1.0 - real]


def forward_kernel(plane, last, *refs):
    refs = list(refs)
    count_ref, list_ref, valid_ref = refs[:3]
    x_refs = [refs[3], refs[5].at[0], refs[4], refs[5].at[1]]
    w_ref = refs[6]
    refs = refs[7:]
    if plane:
        q_ref, acc_in = refs.pop(0), refs.pop(0)
    if last:
        before, refs = refs[:plane], refs[plane:]
    kv_ref = refs.pop(0)
    if plane == 0:
        q_ref = refs.pop(0)
    if last:
        out_ref, lse_ref = refs.pop(0), refs.pop(0)
        keys, values_t, q_ext, acc, top, kv_copy, copied = refs
    else:
        acc = refs.pop(0)
        keys, values_t, q_ext = refs
    marks = w_ref[:, 3 * LANES : 4 * LANES].astype(F32).T
    gain, bias = marks[64:65], marks[65:66]
    for slot, x_ref in enumerate(x_refs):
        rows = slice(slot * BLOCK, (slot + 1) * BLOCK)
        normed, ignored, ignored_too = norm_rows(x_ref[...].astype(F32), gain, bias)
        normed = normed.astype(BF16)
        kv_ref[rows, :] = dot_on(normed, w_ref[:, : 3 * LANES], 1, 0).astype(BF16)
        if plane == 0:
            own = dot_on(normed, w_ref[:, 3 * LANES :], 1, 0) * (HDIM ** (-0.5) * LOG2E)
            q_ref[rows, :] = own.astype(BF16)
    fill_keys(4, kv_ref, valid_ref, keys, values_t=values_t, marks_first=4 * plane)
    if plane == 0:
        acc[...] = jnp.zeros_like(acc)
    else:
        acc[...] = acc_in[...]

    def set_queries(block):
        q_rows = pl.ds(pl.multiple_of(block * BLOCK, BLOCK), BLOCK)
        lane = lax.broadcasted_iota(jnp.int32, (BLOCK, LANES), 1)
        row = lax.broadcasted_iota(jnp.int32, (BLOCK, LANES), 0)
        real = row < valid_ref[block]
        marks = jnp.where((lane == 67) & real, 1.0, 0.0)
        marks = jnp.where((lane == 68) & jnp.logical_not(real), 1.0, marks)
        for head in range(3):
            own = q_ref[q_rows, head * LANES : (head + 1) * LANES].astype(F32)
            q_ext[head] = jnp.where(lane < 64, own, marks).astype(BF16)
        return q_rows

    def scores_of(slot, head):
        rows = pl.ds(pl.multiple_of(slot * BLOCK, BLOCK), BLOCK)
        return dot_on(keys[head, rows, :], q_ext[head], 1, 1)

    def over_queries(block, carry):
        q_rows = set_queries(block)

        def over_keys(item, carry_in):
            slot = list_ref[plane, block, item]
            rows = pl.ds(pl.multiple_of(slot * BLOCK, BLOCK), BLOCK)
            ready = [scores_of(slot, 0), scores_of(slot, 1)]
            for head in range(3):
                if head == 0:
                    ready.append(scores_of(slot, 2))
                weights = jnp.exp2(ready.pop(0)).astype(BF16)
                acc[head, :, q_rows] += dot_on(values_t[head, :, rows], weights, 1, 0)
            return carry_in

        lax.fori_loop(0, count_ref[plane, block], over_keys, 0)
        return carry

    lax.fori_loop(0, 4, over_queries, 0)
    if not last:
        return
    sums = acc[:, 64:65, :]
    good = (sums >= 2.0**-60) & (sums <= 2.0**100)
    safe = jnp.min(jnp.where(good, 1.0, 0.0)) > 0.5
    top[...] = jnp.zeros_like(top)

    @pl.when(jnp.logical_not(safe))
    def _():
        top[...] = jnp.full_like(top, MASKED)
        acc[...] = jnp.zeros_like(acc)
        for which, source in enumerate(list(before) + [kv_ref]):
            if which < plane:
                move = pltpu.make_async_copy(source, kv_copy, copied)
                move.start()
                move.wait()
                source = kv_copy
            fill_keys(4, source, valid_ref, keys, values_t=values_t, marks_first=4 * which)

            def over_queries_again(block, carry, which=which):
                q_rows = set_queries(block)

                def with_max(item, carry_in):
                    slot = list_ref[which, block, item]
                    rows = pl.ds(pl.multiple_of(slot * BLOCK, BLOCK), BLOCK)
                    for head in range(3):
                        scores = scores_of(slot, head)
                        old = top[head, :, q_rows]
                        now = jnp.maximum(old, jnp.max(scores, axis=0, keepdims=True))
                        weights = jnp.exp2(scores - now).astype(BF16)
                        top[head, :, q_rows] = now
                        acc[head, :, q_rows] = acc[head, :, q_rows] * jnp.exp2(
                            old - now
                        ) + dot_on(values_t[head, :, rows], weights, 1, 0)
                    return carry_in

                lax.fori_loop(0, count_ref[which, block], with_max, 0)
                return carry

            lax.fori_loop(0, 4, over_queries_again, 0)

    for head in range(3):
        total = acc[head, 64:65, :]
        out_ref[head] = (acc[head, 0:64, :] / total).astype(BF16)
        lse_ref[head] = top[head] + jnp.log2(total)


def attend_forward(plane, last, counts, lists, valid, blocks, weights, queries, acc, before):
    kv_rows = 4 * BLOCK
    smem = pl.BlockSpec(memory_space=pltpu.SMEM)
    vmem = pl.BlockSpec(memory_space=pltpu.VMEM)
    anywhere = pl.BlockSpec(memory_space=pl.ANY)
    packed = jax.ShapeDtypeStruct((kv_rows, 3 * LANES), BF16)
    sums = jax.ShapeDtypeStruct((3, 80, kv_rows), F32)
    inputs = [counts, lists, valid] + list(blocks) + [weights]
    inputs += [queries, acc] if plane else []
    outs = [packed] + ([packed] if plane == 0 else [])
    scratch = [
        pltpu.VMEM((3, kv_rows, LANES), BF16),
        pltpu.VMEM((3, 80, kv_rows), BF16),
        pltpu.VMEM((3, BLOCK, LANES), BF16),
    ]
    in_specs = [smem] * 3 + [vmem] * (len(inputs) - 3)
    if last:
        inputs += list(before)
        in_specs += [anywhere] * len(before)
        outs += [
            jax.ShapeDtypeStruct((3, HDIM, kv_rows), BF16),
            jax.ShapeDtypeStruct((3, 1, kv_rows), F32),
        ]
        scratch += [
            pltpu.VMEM((3, 80, kv_rows), F32),
            pltpu.VMEM((3, 1, kv_rows), F32),
            pltpu.VMEM((kv_rows, 3 * LANES), BF16),
            pltpu.SemaphoreType.DMA,
        ]
    else:
        outs += [sums]
    return pl.pallas_call(
        partial(forward_kernel, plane, last),
        out_shape=tuple(outs),
        in_specs=in_specs,
        out_specs=(vmem,) * len(outs),
        scratch_shapes=scratch,
        compiler_params=pltpu.CompilerParams(vmem_limit_bytes=40 << 20),
        cost_estimate=pl.CostEstimate(
            flops=12 * 1000 * 1000 * 1000, bytes_accessed=10 << 20, transcendentals=7 << 20
        ),
        name="attend_forward",
    )(*inputs)


def backward_kernel(plane, carried, last, *refs):
    refs = list(refs)
    count_ref, list_ref, valid_ref = refs[:3]
    q_ref, kv_ref, out_ref, lse_ref, grad_ref, w_ref = refs[3:9]
    x_from = [refs[9], refs[11].at[0], refs[10], refs[11].at[1]]
    refs = refs[12:]
    sum_in, refs = refs[0], refs[1:]
    if carried:
        dq_in, dw_in = refs[:2]
        refs = refs[2:]
    if last:
        keep_ref, send_ref, dw_out = refs[:3]
        dw_ref, dwq_ref, sum_ref = refs[-3:]
        dq_ref = None
        refs = refs[3:-3]
    else:
        keep_ref, send_ref, dw_ref, dq_ref, sum_ref = refs[:5]
        refs = refs[5:]
    keys, values, q_ext, g_ext, q_turned, dq_acc, dkv_acc, x_ref, moved = refs
    slots = 4
    moves = [
        pltpu.make_async_copy(x_from[i], x_ref.at[pl.ds(i * BLOCK, BLOCK)], moved.at[i])
        for i in range(slots)
    ]
    if carried:
        moves.append(pltpu.make_async_copy(dq_in, dq_acc, moved.at[4]))
    for move in moves:
        move.start()
    fill_keys(slots, kv_ref, valid_ref, keys, values_out=values, marks_first=4 * plane)
    lane = lax.broadcasted_iota(jnp.int32, (BLOCK, LANES), 1)

    def clear(slot, carry):
        rows = pl.ds(pl.multiple_of(slot * BLOCK, BLOCK), BLOCK)
        for head in range(3):
            dkv_acc[head, :, rows] = jnp.zeros((LANES, BLOCK), F32)
        return carry

    lax.fori_loop(0, slots, clear, 0)
    if carried:
        moves[4].wait()
    else:
        dq_acc[...] = jnp.zeros_like(dq_acc)

    def over_queries(block, carry):
        q_rows = pl.ds(pl.multiple_of(block * BLOCK, BLOCK), BLOCK)
        for head in range(3):
            lanes = slice(head * LANES, (head + 1) * LANES)
            turned = q_ref[q_rows, lanes].astype(F32).T[0:64]
            grad_t = grad_ref[head, :, q_rows].astype(F32)
            delta = jnp.sum(grad_t * out_ref[head, :, q_rows].astype(F32), axis=0, keepdims=True)
            marks = split_three(-lse_ref[head, :, q_rows]) + query_marks(valid_ref[block], BLOCK)
            blank = jnp.zeros((64 - len(marks), BLOCK), F32)
            q_turned[head] = turned.astype(BF16)
            q_ext[head] = jnp.concatenate([turned] + marks + [blank], axis=0).T.astype(BF16)
            minus = split_three(-delta)
            blank = jnp.zeros((64 - len(minus), BLOCK), F32)
            g_ext[head] = jnp.concatenate(minus + [blank, grad_t], axis=0).T.astype(BF16)

        def over_keys(item, carry_in):
            slot = list_ref[plane, block, item]
            rows = pl.ds(pl.multiple_of(slot * BLOCK, BLOCK), BLOCK)

            def products(head):
                return (
                    dot_on(q_ext[head], keys[head, rows, :], 1, 1),
                    dot_on(g_ext[head], values[head, rows, :], 1, 1),
                )

            ready = [products(0)]
            for head in range(3):
                lanes = slice(head * LANES, (head + 1) * LANES)
                if head < 2:
                    ready.append(products(head + 1))
                scores, grad_probs = ready.pop(0)
                probs = jnp.exp2(scores)
                grad_scores = (probs * grad_probs).astype(BF16)
                dkv_acc[head, 64:128, rows] += dot_on(
                    grad_ref[head, :, q_rows], probs.astype(BF16), 1, 0
                )
                dkv_acc[head, 0:64, rows] += dot_on(q_turned[head], grad_scores, 1, 0)
                dq_acc[q_rows, lanes] += dot_on(grad_scores, keys[head, rows, :], 1, 0)
            return carry_in

        lax.fori_loop(0, count_ref[plane, block], over_keys, 0)
        return carry

    lax.fori_loop(0, 4, over_queries, 0)
    for move in moves[:4]:
        move.wait()
    if not last:
        leave = pltpu.make_async_copy(dq_acc, dq_ref, moved.at[4])
        leave.start()
    if carried:
        dw_ref[...] = dw_in[...]
    else:
        dw_ref[...] = jnp.zeros_like(dw_ref)
    sum_ref[...] = sum_in[...]
    if last:
        dwq_ref[...] = jnp.zeros_like(dwq_ref)
    marks = w_ref[:, 3 * LANES : 4 * LANES].astype(F32).T
    gain, bias = marks[64:65], marks[65:66]

    def finish(slot, carry):
        rows = pl.ds(pl.multiple_of(slot * BLOCK, BLOCK), BLOCK)
        pieces = []
        for head in range(3):
            pieces.append(dkv_acc[head, 0:64, rows] * LN2)
            pieces.append(dkv_acc[head, 64:128, rows])
        turned = jnp.concatenate(pieces, axis=0)
        part = dot_on(turned.T.astype(BF16), w_ref[:, : 3 * LANES], 1, 1)
        values_now = x_ref[rows, :].astype(F32)
        normed, unit, ignored = norm_rows(values_now, gain, bias)
        normed = normed.astype(BF16)
        dw_ref[...] += dot_on(turned.astype(BF16), normed, 1, 0)
        if last:
            scaled = [
                jnp.where(lane < 64, dq_acc[rows, h * LANES : (h + 1) * LANES], 0.0)
                for h in range(3)
            ]
            scaled = jnp.concatenate(scaled, axis=1) * HDIM ** (-0.5)
            part = part + dot_on(scaled.astype(BF16), w_ref[:, 3 * LANES :], 1, 1)
            dwq_ref[...] += dot_on(scaled.T.astype(BF16), normed, 1, 0)
        sum_ref[0:1, :] += jnp.sum(part * unit, axis=0, keepdims=True)
        sum_ref[1:2, :] += jnp.sum(part, axis=0, keepdims=True)
        low = part.astype(BF16)

        @pl.when(slot % 2 == 0)
        def _():
            keep_ref[slot // 2] = low

        @pl.when(slot % 2 == 1)
        def _():
            send_ref[slot // 2] = low

        return carry

    lax.fori_loop(0, slots, finish, 0)
    if not last:
        leave.wait()
        return
    pieces = []
    for head in range(3):
        first = head * LANES
        pieces.append(dwq_ref[first : first + 64, :])
        pieces.append(dw_ref[first : first + LANES, :])
    pieces += [sum_ref[...], jnp.zeros((LANES - 8, D), F32)]
    dw_out[...] = jnp.concatenate(pieces, axis=0).T.astype(BF16)


def attend_backward(
    plane, counts, lists, valid, queries, key_vals, attended, lse, grads, weights, blocks, carry, last
):
    q_rows = queries.shape[0]
    smem = pl.BlockSpec(memory_space=pltpu.SMEM)
    vmem = pl.BlockSpec(memory_space=pltpu.VMEM)
    anywhere = pl.BlockSpec(memory_space=pl.ANY)
    carry = list(carry)
    half = jax.ShapeDtypeStruct((2, BLOCK, D), BF16)
    weight = jax.ShapeDtypeStruct((3 * LANES, D), F32)
    sums = jax.ShapeDtypeStruct((8, D), F32)
    if last:
        outs = (jax.ShapeDtypeStruct((D, 9 * HDIM + LANES), BF16),)
        spaces, kept = (vmem,), [weight, weight, sums]
    else:
        outs = (weight, jax.ShapeDtypeStruct((q_rows, 3 * LANES), F32), sums)
        spaces, kept = (vmem, anywhere, vmem), []
    result = pl.pallas_call(
        partial(backward_kernel, plane, len(carry) > 1, last),
        out_shape=(half, half) + outs,
        in_specs=[smem] * 3 + [vmem] * 6 + [anywhere] * 3 + [vmem, anywhere, vmem][: len(carry)],
        out_specs=(vmem, vmem) + spaces,
        scratch_shapes=[
            pltpu.VMEM((3, q_rows, LANES), BF16),
            pltpu.VMEM((3, q_rows, LANES), BF16),
            pltpu.VMEM((3, BLOCK, LANES), BF16),
            pltpu.VMEM((3, BLOCK, LANES), BF16),
            pltpu.VMEM((3, HDIM, BLOCK), BF16),
            pltpu.VMEM((q_rows, 3 * LANES), F32),
            pltpu.VMEM((3, LANES, q_rows), F32),
            pltpu.VMEM((q_rows, D), BF16),
            pltpu.SemaphoreType.DMA((5,)),
        ]
        + [pltpu.VMEM(k.shape, k.dtype) for k in kept],
        compiler_params=pltpu.CompilerParams(vmem_limit_bytes=34 << 20),
        cost_estimate=pl.CostEstimate(
            flops=25 * 1000 * 1000 * 1000, bytes_accessed=16 << 20, transcendentals=7 << 20
        ),
        name="attend_backward",
    )(
        counts, lists, valid, queries, key_vals, attended, lse, grads, weights, *blocks, *carry
    )
    return tuple(result) + (None,) * (5 - len(result))


def erf_of(values):
    clamped = jnp.clip(values, -4.0, 4.0)
    square = clamped * clamped
    top = jnp.float32(-2.72614225801306e-10)
    for term in (
        2.77068142495902e-08,
        -2.10102402082508e-06,
        -5.69250639462346e-05,
        -7.34990630326855e-04,
        -2.95459980854025e-03,
        -1.60960333262415e-02,
    ):
        top = top * square + term
    low = jnp.float32(-1.45660718464996e-05)
    for term in (
        -2.13374055278905e-04,
        -1.68282697438203e-03,
        -7.37332916720468e-03,
        -1.42647390514189e-02,
    ):
        low = low * square + term
    return clamped * top / low


def middle_kernel(pieces, pair, shard, *refs):
    refs = list(refs)
    start_ref, group_ref = refs[:2]
    merged_refs, refs = refs[2:6], refs[6:]
    token_ref, cot_ref, mark_ref = refs[:3]
    piece_refs, refs = refs[3 : 3 + pieces], refs[3 + pieces :]
    output_ref, grad_y_ref, grad_z_ref, h_two_ref, hidden_ref, grad_up_ref = refs[:6]
    part_refs, sum_ref, norm_ref, refs = refs[6:10], refs[10], refs[11], refs[12:]
    w_out, w_up, w_down, moved = refs
    parts = []
    for piece in piece_refs:
        parts += [(piece, base) for base in range(0, piece.shape[0], 9 * pair)]

    def moves_of(weight):
        moves = []
        for i, (piece, base) in enumerate(parts):
            if weight < 5:
                source = piece.at[pl.ds(base + weight * pair, pair)]
                rows = pl.ds(pl.multiple_of(start_ref[i] * shard, pair), pair)
                target = w_out.at[rows] if weight == 0 else w_up.at[weight - 1, rows]
            else:
                source = piece.at[pl.ds(base + 5 * pair, 4 * pair)]
                rows = pl.ds(pl.multiple_of(start_ref[i] * 4 * shard, 4 * pair), 4 * pair)
                target = w_down.at[rows]
            moves.append(pltpu.make_async_copy(source, target, moved.at[weight, i]))
        return moves

    arriving = [moves_of(weight) for weight in range(6)]
    for weight in (0, 1, 5, 2, 3, 4):
        for move in arriving[weight]:
            move.start()
    norm_ref[...] = mark_ref[...].astype(F32).T[64:72]
    for move in arriving[0]:
        move.wait()
    y_one = token_ref[...].astype(F32)
    group = D // 4
    for j, merged_ref in enumerate(merged_refs):
        rows = pl.ds(pl.multiple_of(group_ref[j] * group, group), group)
        turned = merged_ref[...].astype(F32).T.astype(BF16)
        y_one = y_one + dot_on(turned, w_out[rows, :], 1, 0)
    grad_y_ref[...] = y_one
    gain, bias = norm_ref[2:3, :], norm_ref[3:4, :]
    normed, unit, inv_rows = norm_rows(y_one, gain, bias)
    h_two_ref[...] = normed.astype(BF16)

    output_sum = jnp.zeros((BLOCK, D), F32)
    grad_sum = jnp.zeros((BLOCK, D), F32)
    for j in range(4):
        for move in arriving[1 + j]:
            move.wait()
        if j == 0:
            for move in arriving[5]:
                move.wait()
        columns = slice(j * D, (j + 1) * D)
        up = dot_on(h_two_ref[...], w_up[j], 1, 0)
        grad_hidden = dot_on(cot_ref[...], w_down[columns, :], 1, 1)
        normal = 0.5 + 0.5 * erf_of(up * 0.7071067811865476)
        density = jnp.exp(-0.5 * up * up) * 0.3989422804014327
        hidden = (up * normal).astype(BF16)
        grad_up = (grad_hidden * (normal + up * density)).astype(BF16)
        hidden_ref[:, columns] = hidden
        grad_up_ref[:, columns] = grad_up
        output_sum = output_sum + dot_on(hidden, w_down[columns, :], 1, 0)
        grad_sum = grad_sum + dot_on(grad_up, w_up[j], 1, 1)
    y_one = grad_y_ref[...]
    output_ref[...] = (y_one + output_sum).astype(BF16)
    normed, unit, inv_rows = norm_rows(y_one, gain, bias)
    sum_ref[...] = jnp.zeros_like(sum_ref)
    sum_ref[2:3, :] = jnp.sum(grad_sum * unit, axis=0, keepdims=True)
    sum_ref[3:4, :] = jnp.sum(grad_sum, axis=0, keepdims=True)
    grad_y = cot_ref[...].astype(F32) + norm_back(grad_sum, unit, inv_rows, gain)
    grad_y_ref[...] = grad_y
    grad_z = grad_y.astype(BF16)
    grad_z_ref[...] = grad_z
    for j, part_ref in enumerate(part_refs):
        rows = pl.ds(pl.multiple_of(group_ref[j] * group, group), group)
        part_ref[...] = dot_on(w_out[rows, :], grad_z, 1, 1).astype(BF16)


def middle(starts, groups, merged, tokens, cotangent, marks, pieces, shard):
    smem = pl.BlockSpec(memory_space=pltpu.SMEM)
    vmem = pl.BlockSpec(memory_space=pltpu.VMEM)
    anywhere = pl.BlockSpec(memory_space=pl.ANY)
    rows = tokens.shape[0]
    number = starts.shape[0]
    pair = sum(piece.shape[0] for piece in pieces) // (9 * number)

    def shape(columns, dtype, height=rows):
        return jax.ShapeDtypeStruct((height, columns), dtype)

    return pl.pallas_call(
        partial(middle_kernel, len(pieces), pair, shard),
        out_shape=(
            shape(D, BF16),
            shape(D, F32),
            shape(D, BF16),
            shape(D, BF16),
            shape(4 * D, BF16),
            shape(4 * D, BF16),
        )
        + (shape(rows, BF16, D // 4),) * 4
        + (shape(D, F32, 8),) * 2,
        in_specs=[smem, smem] + [vmem] * 7 + [anywhere] * len(pieces),
        out_specs=(vmem,) * 12,
        scratch_shapes=[
            pltpu.VMEM((D, D), BF16),
            pltpu.VMEM((4, D, D), BF16),
            pltpu.VMEM((4 * D, D), BF16),
            pltpu.SemaphoreType.DMA((6, number)),
        ],
        compiler_params=pltpu.CompilerParams(vmem_limit_bytes=58 << 20),
        cost_estimate=pl.CostEstimate(
            flops=12 * 1000 * 1000 * 1000, bytes_accessed=24 << 20, transcendentals=3 << 20
        ),
        name="middle",
    )(starts, groups, *merged, tokens, cotangent, marks, *pieces)


def put_halves(core, rows, keep_ref, give_ref, place, columns, values):
    for i in range(values.shape[0] // (2 * rows)):
        for which in range(2):
            first = (2 * i + which) * rows
            piece = values[first : first + rows].astype(BF16)
            start = place + i * rows
            if not isinstance(start, int):
                start = pl.multiple_of(start, rows)
            target = pl.ds(start, rows)

            @pl.when(core == which)
            def _(piece=piece, target=target):
                keep_ref[target, columns] = piece

            @pl.when(core != which)
            def _(piece=piece, target=target):
                give_ref[target, columns] = piece


def down_kernel(line, core_ref, hidden_ref, cot_ref, keep_ref, give_ref):
    block = dot_on(hidden_ref[...], cot_ref[...], 0, 0)
    put_halves(core_ref[0], 4 * line, keep_ref, give_ref, 0, slice(0, D), block)


def wide_kernel(line, *refs):
    core_ref, group_ref, h_two_ref, grad_up_ref, grad_z_ref = refs[:5]
    merged_refs, (keep_ref, give_ref) = refs[5:9], refs[9:]
    core, step = core_ref[0], pl.program_id(0)
    columns = slice(0, D)

    @pl.when(step < 4)
    def _():
        block = dot_on(h_two_ref[...], grad_up_ref[...], 0, 0)
        put_halves(core, line, keep_ref, give_ref, 0, columns, block)

    @pl.when(step == 4)
    def _():
        group = D // 4
        for j, merged_ref in enumerate(merged_refs):
            block = dot_on(merged_ref[...], grad_z_ref[...], 1, 0)
            place = group_ref[j] * (group // 2)
            put_halves(core, line, keep_ref, give_ref, place, columns, block)


def halves_of_down(line, core, hidden, cotangent):
    rows = cotangent.shape[0]
    half = pl.BlockSpec((D // 2, D), lambda j: (j, 0))
    return pl.pallas_call(
        partial(down_kernel, line),
        grid=(4,),
        out_shape=(jax.ShapeDtypeStruct((2 * D, D), BF16),) * 2,
        in_specs=[
            pl.BlockSpec(memory_space=pltpu.SMEM),
            pl.BlockSpec((rows, D), lambda j: (0, j)),
            pl.BlockSpec((rows, D), lambda j: (0, 0)),
        ],
        out_specs=(half, half),
        compiler_params=pltpu.CompilerParams(vmem_limit_bytes=54 << 20),
        cost_estimate=pl.CostEstimate(
            flops=3 * 10**9, bytes_accessed=10 << 20, transcendentals=0
        ),
        name="grad_down",
    )(core, hidden, cotangent)


def halves_of_wide(line, core, groups, h_two, grad_up, grad_z, merged):
    rows = h_two.shape[0]
    smem = pl.BlockSpec(memory_space=pltpu.SMEM)
    whole = pl.BlockSpec((rows, D), lambda j: (0, 0))
    half = pl.BlockSpec((D // 2, D), lambda j: (0, j))
    return pl.pallas_call(
        partial(wide_kernel, line),
        grid=(5,),
        out_shape=(jax.ShapeDtypeStruct((D // 2, 5 * D), BF16),) * 2,
        in_specs=[smem, smem, whole]
        + [pl.BlockSpec((rows, D), lambda j: (0, jnp.minimum(j, 3))), whole]
        + [pl.BlockSpec((D // 4, rows), lambda j: (0, 0))] * 4,
        out_specs=(half, half),
        compiler_params=pltpu.CompilerParams(vmem_limit_bytes=54 << 20),
        cost_estimate=pl.CostEstimate(
            flops=4 * 10**9, bytes_accessed=12 << 20, transcendentals=0
        ),
        name="grad_wide",
    )(core, groups, h_two, grad_up, grad_z, *merged)


def scene_lists(same):
    number = same.shape[-1]
    slot = jnp.arange(number)
    counts = jnp.sum(same, axis=-1).astype(jnp.int32)
    earlier = slot[None, :] < slot[:, None]
    place = jnp.sum(same[:, :, None, :] & earlier, axis=-1)
    hits = same[:, :, None, :] & (place[:, :, None, :] == slot[:, None])
    lists = jnp.sum(jnp.where(hits, slot, 0), axis=-1)
    return counts, lists.astype(jnp.int32)


def halve(value, axis, bit, send):
    give = lax.dynamic_index_in_dim(value, 1 - bit, axis, keepdims=False)
    return value, send(give)


def settle(pending, axis, bit):
    value, taken = pending
    keep = lax.dynamic_index_in_dim(value, bit, axis, keepdims=False)
    return (keep.astype(F32) + taken.astype(F32)).astype(BF16)


def ring_sources(count):
    order = ring_order(count)
    table = [[order[(order.index(c) - r) % count] for r in range(count)] for c in range(count)]
    return jnp.array(table, jnp.int32)[lax.axis_index("ctx")]


def give_over_seq(value):
    count = lax.axis_size("seq")
    me = lax.axis_index("seq")
    while True:
        count //= 2
        pairs = [(i, i ^ count) for i in range(lax.axis_size("seq"))]
        pending = halve(
            value.reshape((2, count) + value.shape[1:]),
            0,
            (me // count) % 2,
            lambda give: lax.ppermute(give, "seq", pairs),
        )
        if count == 1:
            return pending
        value = settle(pending, 0, (me // count) % 2)


def sum_over_seq(pending):
    value = settle(pending, 0, lax.axis_index("seq") % 2)
    return value.reshape(value.shape[1:])


def gather_bit(value, bit, send):
    other = send(value)
    first = jnp.where(bit == 0, value, other)
    return jnp.concatenate([first, jnp.where(bit == 0, other, value)], axis=0)


def gather_seq(value):
    count, reach = lax.axis_size("seq"), 1
    me = lax.axis_index("seq")
    while reach < count:
        pairs = [(i, i ^ reach) for i in range(count)]
        value = gather_bit(
            value[None], (me // reach) % 2, lambda v: lax.ppermute(v, "seq", pairs)
        ).reshape((2 * reach,) + value.shape[1:])
        reach *= 2
    return value


def swap_seq(value, mask=1):
    return lax.ppermute(value, "seq", [(i, i ^ mask) for i in range(lax.axis_size("seq"))])


def in_order(blocks, sources, shard):
    count = len(blocks)
    full = jnp.zeros((count,) + blocks[0].shape, BF16)
    for r in range(count):
        full = lax.dynamic_update_index_in_dim(full, blocks[r], sources[r], 0)
    cuts = []
    for half in range(2):
        part = full[half * (count // 2) : (half + 1) * (count // 2)]
        cut = [part[:, i * shard : (i + 1) * shard] for i in range(5)] + [part[:, 5 * shard :]]
        cuts += [c.reshape(-1, D) for c in cut]
    return jnp.concatenate(cuts, axis=0)


def join_halves(pieces, places, number):
    def woven(first, second):
        rows = first.shape[0] // 9
        cuts = [i * rows for i in range(1, 6)]
        both = zip(jnp.split(first, cuts), jnp.split(second, cuts))
        return jnp.concatenate([part for pair in both for part in pair], axis=0)

    joined, kept = [], []
    for base in range(0, len(pieces), number):
        for i in (0, 1):
            joined.append(woven(*jnp.split(pieces[base + i], 2)))
            kept.append(((0,),) + places[base + i][1:])
        for i in (2, 4):
            joined.append(woven(pieces[base + i], pieces[base + i + 1]))
            kept.append(((0,),) + places[base + i][1:])
    return joined, kept


def gather_ctx(value):
    count = lax.axis_size("ctx")
    sources = ring_sources(count)
    whole = jnp.zeros((count,) + value.shape, value.dtype)
    whole = lax.dynamic_update_index_in_dim(whole, value, sources[0], 0)
    for r in range(1, count):
        whole = lax.dynamic_update_index_in_dim(whole, ring_send(value, r), sources[r], 0)
    return whole


def sum_over_core(pending):
    keep, taken = pending
    return (keep.astype(F32) + taken.astype(F32)).astype(BF16)


def give_over_x(value):
    return halve(value, 0, lax.axis_index("head") // 2, lambda give: swap_head(give, 2))


def sum_over_x(pending):
    return settle(pending, 0, lax.axis_index("head") // 2)


def send_term(value, r):
    source = ring_sources(lax.axis_size("ctx"))[r]
    return ring_send(lax.dynamic_index_in_dim(value, source, 0, keepdims=False), -r)


def sum_terms(value, terms):
    source = ring_sources(lax.axis_size("ctx"))[0]
    total = lax.dynamic_index_in_dim(value, source, 0, keepdims=False).astype(F32)
    for term in terms:
        total = total + term.astype(F32)
    return total


def sum_over_ctx(value):
    count = lax.axis_size("ctx")
    sources = ring_sources(count)
    total = lax.dynamic_index_in_dim(value, sources[0], 0, keepdims=False).astype(F32)
    for r in range(1, count):
        give = lax.dynamic_index_in_dim(value, sources[r], 0, keepdims=False)
        total = total + ring_send(give, -r).astype(F32)
    return total


def tie(*values):
    return lax.optimization_barrier(values)


def body(
    tokens,
    segment_ids,
    w_qkv,
    w_out,
    w_up,
    w_down,
    gain_one,
    bias_one,
    gain_two,
    bias_two,
    cotangent,
):
    heads_ax = lax.axis_size("head")
    ctx_ax = lax.axis_size("ctx")
    seq_ax = lax.axis_size("seq")
    me_head = lax.axis_index("head")
    tok_rows = tokens.shape[0]
    group = D // heads_ax
    shard = w_qkv.shape[0]

    order = [me_head ^ j for j in range(heads_ax)]
    sources = ring_sources(ctx_ax)
    wide = 3 * group + LANES

    padding = tok_rows - jnp.sum(segment_ids >= 0)
    about = jnp.stack([segment_ids[0], padding // 16, padding % 16]).astype(BF16)
    extra = jnp.stack([gain_one, bias_one, gain_two, bias_two], axis=1)
    extra = jnp.concatenate([extra, jnp.broadcast_to(about[None, :], (shard, 3))], axis=1)
    extra = jnp.pad(extra, ((0, 0), (0, HDIM - 7)))
    by_head = w_qkv.reshape(shard, heads_ax, 3, 3, HDIM)
    beside = jnp.zeros((shard, heads_ax, 2, HDIM), BF16)
    beside = jnp.concatenate(
        [jnp.broadcast_to(extra[:, None, None], (shard, heads_ax, 1, HDIM)), beside], axis=2
    )
    packed = jnp.concatenate(
        [
            by_head[:, :, :, 1:].reshape(shard, heads_ax, 3 * LANES),
            jnp.stack([by_head[:, :, :, 0], beside], axis=3).reshape(shard, heads_ax, 3 * LANES),
        ],
        axis=2,
    )
    packed = jnp.swapaxes(packed, 0, 1)
    got = tie(
        *[lax.dynamic_index_in_dim(packed, o, 0, keepdims=False) for o in order]
    )
    got = [swap_head(piece, j) if j else piece for j, piece in enumerate(got)]
    w_rest = jnp.concatenate(
        [w_out] + [w_up[:, i * D : (i + 1) * D] for i in range(4)] + [w_down], axis=0
    )
    w_rest, *got = tie(w_rest, *got)
    mine = jnp.zeros((heads_ax, shard, D), BF16)
    for j in range(heads_ax):
        mine = lax.dynamic_update_index_in_dim(mine, got[j], order[j], 0)
    ring_mine = [mine] + [ring_send(mine, i) for i in range(1, ctx_ax)]

    rest = [w_rest]
    near, ahead, behind = swap_head(tokens, 2), ring_send(tokens, 1), ring_send(w_rest, 1)
    near, ahead, behind, *ring_mine = tie(near, ahead, behind, *ring_mine)
    rest.append(behind)
    packed = jnp.zeros((ctx_ax,) + mine.shape, BF16)
    for r in range(ctx_ax):
        packed = lax.dynamic_update_index_in_dim(packed, ring_mine[r], sources[r], 0)

    def weights_here(packed):
        weights = jnp.swapaxes(gather_seq(packed[None]), 1, 2).reshape(D, D)
        first = 3 * LANES + HDIM + 4
        about_all = weights[::shard, first : first + 3].astype(jnp.int32)
        about_all = lax.dynamic_index_in_dim(
            about_all.reshape(seq_ax, heads_ax, ctx_ax, 3),
            lax.axis_index("seq"),
            0,
            keepdims=False,
        )
        pick_head = jnp.stack(order)[:, None] == jnp.arange(heads_ax)[None, :]
        pick_ctx = sources[:, None] == jnp.arange(ctx_ax)[None, :]
        pick = pick_ctx[:, None, None, :] & pick_head[None, :, :, None]
        slot_about = jnp.sum(jnp.where(pick[..., None], about_all[None, None], 0), axis=(2, 3))
        slot_ids = slot_about[:, :, 0]
        slot_valid = (tok_rows - (slot_about[:, :, 1] * 16 + slot_about[:, :, 2])).reshape(-1)
        counts, lists = scene_lists(slot_ids[0][None, :, None] == slot_ids[:, None, :])
        return weights, counts, lists, slot_valid

    planes, key_vals, queries, acc = [], [], None, None
    block = tokens
    ready = None
    for r in range(ctx_ax + 1):
        if r < ctx_ax:
            travelers = [swap_head(jnp.stack([block, near]), 1)]
        else:
            travelers = []
        if r + 1 < ctx_ax:
            travelers.append(swap_head(ahead, 2))
        if r + 2 < ctx_ax:
            travelers.append(ring_send(ahead, 1))
            travelers.append(ring_send(rest[-1], 1))
        count = len(travelers)
        if r == ctx_ax - 2:
            line = in_order(rest, sources, shard)
            middle_row = line.shape[0] // 2
            travelers += [swap_head(line[:middle_row], 2), swap_seq(line)]
        if r == ctx_ax - 1:
            travelers += [swap_head(line[middle_row:], 2), swap_seq(x_first), swap_head(line, 1)]
        if r == ctx_ax:
            travelers += [swap_seq(x_second), swap_head(y_line, 1), swap_head(x_first, 1)]
        results = []
        if ready is not None:
            results = list(
                attend_forward(
                    r - 1,
                    r == ctx_ax,
                    counts,
                    lists,
                    slot_valid,
                    ready,
                    weights,
                    queries,
                    acc,
                    key_vals,
                )
            )
        tied = list(tie(*travelers, *results))
        extra, tied = tied[count : len(travelers)], tied[:count] + tied[len(travelers) :]
        if r == 0:
            weights, counts, lists, slot_valid = weights_here(packed)
        if r == ctx_ax - 2:
            x_first, y_line = extra
        if r == ctx_ax - 1:
            x_second, xy_first, core_line = extra
        if r == ctx_ax:
            xy_second, core_y, core_x_first = extra
            results = tied
            break
        planes.append([block, near, tied.pop(0)])
        ready = planes[-1]
        if r + 1 < ctx_ax:
            block, near = ahead, tied.pop(0)
        if r + 2 < ctx_ax:
            ahead = tied.pop(0)
            rest.append(tied.pop(0))
        if results:
            key_vals.append(tied.pop(0))
            if r == 1:
                queries = tied.pop(0)
            acc = tied.pop(0)
    key_vals.append(results[0])
    attended, lse = results[1:]
    owns = [line, y_line, x_first, x_second, xy_first, xy_second]
    cores = [core_line, core_y, core_x_first]
    cores += [swap_head(v, 1) for v in (x_second, xy_first, xy_second)]
    offs = [((0, 1), 0, 0), ((0, 1), 0, 1), ((0,), 1, 0), ((1,), 1, 0), ((0,), 1, 1), ((1,), 1, 1)]
    me_x, me_core, me_seq = me_head // 2, me_head % 2, lax.axis_index("seq")
    pieces, places = [], []
    for core, arrays in enumerate((owns, cores)):
        for array, (halves, x, y) in zip(arrays, offs):
            pieces.append(array)
            places.append((halves, (me_x ^ x) * 2 + (me_core ^ core), y))
    reach = 2
    while reach < seq_ax:
        pieces += [swap_seq(array, reach) for array in pieces]
        places += [(halves, place, y ^ reach) for halves, place, y in places]
        reach *= 2
    if (ctx_ax // 2 * shard) % 8:
        pieces, places = join_halves(pieces, places, len(offs))
    starts = [
        ((me_seq ^ y) * heads_ax + place) * ctx_ax + half * (ctx_ax // 2)
        for halves, place, y in places
        for half in halves
    ]
    starts = jnp.stack(starts).astype(jnp.int32)

    merged = []
    for j in range(heads_ax):
        part = attended[:, :, j * tok_rows : (j + 1) * tok_rows].reshape(group, tok_rows)
        merged.append(swap_head(part, j) if j else part)

    marks = weights[:, 3 * LANES : 4 * LANES]
    groups = jnp.stack(order).astype(jnp.int32)
    output, grad_y_one, grad_z, h_two, hidden, grad_up, *rest_out = middle(
        starts, groups, merged, tokens, cotangent, marks, pieces, shard
    )
    grad_merged, sums_two, norms = rest_out[:4], rest_out[4], rest_out[5]

    grad_parts = [swap_head(p, j) if j else p for j, p in enumerate(grad_merged)]
    line = ctx_ax * shard
    outer = (seq_ax, 2, ctx_ax)
    me_bit = (me_head % 2)[None].astype(jnp.int32)
    keep, give = halves_of_down(line, me_bit, hidden, cotangent)
    shape = outer + (4 * shard, D)
    down_sum = (keep.reshape(shape), swap_head(give.reshape(shape), 1))
    h_two, keep, *_ = tie(h_two, down_sum[0])
    keep, give = halves_of_wide(line, me_bit, groups, h_two, grad_up, grad_z, merged)
    shape = outer + (shard, 5 * D)
    keep, give, *tied = tie(keep, give, *down_sum, *grad_parts)
    down_sum, grad_parts = sum_over_core(tied[:2]), tied[2:]
    grad_local = jnp.concatenate(grad_parts, axis=1).reshape(3, HDIM, heads_ax * tok_rows)
    wide_sum = (keep.reshape(shape), swap_head(give.reshape(shape), 1))
    down_sum = give_over_seq(down_sum)

    carry, traveling, near_half, far_half = (sums_two,), None, None, None
    for r in reversed(range(ctx_ax)):
        step = ctx_ax - 1 - r
        travelers = []
        if step >= 1:
            travelers.append(swap_head(far_half, 2))
        if step >= 2:
            travelers.append(ring_send(traveling, -1))
        count = len(travelers)
        if step == 0:
            travelers += [down_sum, wide_sum]
        if step == 1:
            travelers += [give_over_x(down_sum), give_over_seq(wide_sum)]
        if step == 2:
            travelers += [give_over_x(wide_sum)] + [send_term(down_sum, i) for i in (1, 2, 3)]
        if step == 3:
            travelers += [send_term(wide_sum, i) for i in (1, 2, 3)]
        keep, give, dw, fourth, sums = attend_backward(
            r,
            counts,
            lists,
            slot_valid,
            queries,
            key_vals[r],
            attended,
            lse,
            grad_local,
            weights,
            planes[r],
            carry,
            r == 0,
        )
        if r == 0:
            keep, give, dw, *travelers = tie(keep, give, dw, *travelers)
        else:
            keep, give, fourth, dw, sums, *travelers = tie(
                keep, give, fourth, dw, sums, *travelers
            )
        extra = travelers[count:]
        if step >= 1:
            moved = near_half.astype(F32) + travelers[0].astype(F32)
            if step >= 2:
                moved = moved + travelers[1].astype(F32)
            traveling = moved.astype(BF16)
        if step == 0:
            down_sum = sum_over_seq(extra[0])
            wide_sum = sum_over_core(extra[1])
        if step == 1:
            down_sum, wide_sum = sum_over_x(extra[0]), sum_over_seq(extra[1])
        if step == 2:
            wide_sum, down_terms = sum_over_x(extra[0]), list(extra[1:])
        if step == 3:
            wide_terms = list(extra)
        taken = swap_head(give, 1)
        near_half = (keep[0].astype(F32) + taken[0].astype(F32)).astype(BF16)
        far_half = (keep[1].astype(F32) + taken[1].astype(F32)).astype(BF16)
        if r:
            tied = [near_half, far_half, fourth, dw, sums, down_sum, wide_sum]
            tied += [traveling] if step >= 1 else []
            near_half, far_half, fourth, dw, sums, down_sum, wide_sum, *tied = tie(*tied)
            if step >= 1:
                traveling = tied[0]
        carry = (sums, fourth, dw)
    near_half, far_half, traveling, dw, wide_sum = tie(
        near_half, far_half, traveling, dw, wide_sum
    )
    dw_mine = give_over_seq(dw.reshape(seq_ax, heads_ax, ctx_ax, shard, wide))
    taken, carried, *dw_mine = tie(
        swap_head(far_half, 2), ring_send(traveling, -1), *dw_mine
    )
    dw_mine = sum_over_seq(dw_mine)
    grad_h_one = near_half.astype(F32) + taken.astype(F32) + carried.astype(F32)
    down_sum, wide_sum = sum_terms(down_sum, down_terms), sum_terms(wide_sum, wide_terms)
    up_sum, out_sum = wide_sum[:, : 4 * D], wide_sum[:, 4 * D :]
    dw_mine = sum_over_ctx(jnp.swapaxes(dw_mine, 0, 1)).astype(BF16)
    groups = []
    for j in range(heads_ax):
        part = lax.dynamic_index_in_dim(dw_mine, order[j], 0, keepdims=False)
        groups.append(swap_head(part, j) if j else part)
    groups = jnp.stack(groups)
    groups = jnp.stack(
        [lax.dynamic_index_in_dim(groups, o, 0, keepdims=False) for o in order]
    ).astype(F32)
    grad_w_qkv = jnp.swapaxes(groups[:, :, : 3 * group], 0, 1).reshape(shard, 3 * D)
    norm_sums = jnp.sum(groups[:, :, 3 * group : 3 * group + 4], axis=0)

    g_one = norms[0]
    ignored, unit_one, inv_one = norm_rows(tokens.astype(F32), g_one, norms[1])
    grad_tokens = (grad_y_one + norm_back(grad_h_one, unit_one, inv_one, g_one)).astype(BF16)
    return (
        output,
        grad_tokens,
        grad_w_qkv,
        out_sum,
        up_sum,
        down_sum,
        norm_sums[:, 0],
        norm_sums[:, 1],
        norm_sums[:, 2],
        norm_sums[:, 3],
    )


def solution(mesh):
    rows = P(ALL_AXES, None)
    vector = P(ALL_AXES)
    return jax.shard_map(
        body,
        mesh=mesh,
        in_specs=(rows, vector, rows, rows, rows, rows, vector, vector, vector, vector, rows),
        out_specs=(rows, rows, rows, rows, rows, rows, vector, vector, vector, vector),
        check_vma=False,
    )
```

```python
from functools import partial

import jax
import jax.numpy as jnp
from jax import lax
from jax.experimental import pallas as pl
from jax.experimental.pallas import tpu as pltpu
from jax.sharding import PartitionSpec as P

D = 768
HEADS = 12
HDIM = 64
BLOCK = 512
LANES = 128
EPSILON = 1e-05
MASKED = -1e30
ALL_AXES = ("seq", "head", "ctx")
BF16 = jnp.bfloat16
F32 = jnp.float32


def dot_on(left, right, left_dim, right_dim):
    return lax.dot_general(
        left, right, (((left_dim,), (right_dim,)), ((), ())), preferred_element_type=F32
    )


def norm_rows(values, gain_vec, bias_vec):
    row_mean = jnp.mean(values, axis=-1, keepdims=True)
    centered = values - row_mean
    variance = jnp.mean(centered * centered, axis=-1, keepdims=True)
    inv_rows = lax.rsqrt(variance + EPSILON)
    unit_rows = centered * inv_rows
    return (unit_rows * gain_vec + bias_vec, unit_rows, inv_rows)


def norm_back(grad_norm, unit_rows, inv_rows, gain_vec):
    scaled = grad_norm * gain_vec
    return inv_rows * (
        scaled
        - jnp.mean(scaled, axis=-1, keepdims=True)
        - unit_rows * jnp.mean(scaled * unit_rows, axis=-1, keepdims=True)
    )


def gelu_exact(values):
    return jax.nn.gelu(values, approximate=False)


def swap_head(value, mask):
    count = lax.axis_size("head")
    return lax.ppermute(value, "head", [(i, i ^ mask) for i in range(count)])


def ring_order(count):
    return [0, 1, 3, 2] if count == 4 else list(range(count))


def ring_pairs(count, step):
    order = ring_order(count)
    return [(order[i], order[(i + step) % count]) for i in range(count)]


def ring_send(value, step):
    return lax.ppermute(value, "ctx", ring_pairs(lax.axis_size("ctx"), step))


def plane_blocks(block):
    near = swap_head(block, 2)
    return [block, swap_head(block, 1), near, swap_head(near, 1)]


def split_three(values):
    high = values.astype(BF16)
    rest = values - high.astype(F32)
    middle = rest.astype(BF16)
    low = (rest - middle.astype(F32)).astype(BF16)
    return [high.astype(F32), middle.astype(F32), low.astype(F32)]


def key_marks(valid, lane):
    row = lax.broadcasted_iota(jnp.int32, (BLOCK, LANES), 0)
    real = row < valid
    marks = jnp.where((lane >= 64) & (lane < 67), 1.0, 0.0)
    marks = jnp.where((lane == 67) & jnp.logical_not(real), MASKED, marks)
    return jnp.where((lane == 68) & real, MASKED, marks)


def fill_keys(slots, kv_ref, valid_ref, keys_out, values_t=None, values_out=None, marks_first=0):
    lane = lax.broadcasted_iota(jnp.int32, (BLOCK, LANES), 1)

    def fill(slot, carry):
        rows = pl.ds(pl.multiple_of(slot * BLOCK, BLOCK), BLOCK)
        marks = key_marks(valid_ref[slot + marks_first], lane)
        for head in range(3):
            pair = kv_ref[rows, head * LANES : (head + 1) * LANES].astype(F32)
            keys_out[head, rows, :] = jnp.where(lane < 64, pair, marks).astype(BF16)
            if values_out is not None:
                ones = jnp.where(lane < 3, 1.0, 0.0)
                values_out[head, rows, :] = jnp.where(lane < 64, ones, pair).astype(BF16)
            if values_t is not None:
                turned = pair.T[64:128].astype(BF16)
                values_t[head, :, rows] = jnp.concatenate(
                    [turned, jnp.ones((16, BLOCK), BF16)], axis=0
                )
        return carry

    lax.fori_loop(0, slots, fill, 0)


def query_marks(valid, width):
    row = lax.broadcasted_iota(jnp.int32, (1, width), 1)
    real = jnp.where(row < valid, 1.0, 0.0)
    return [real, 1.0 - real]


def forward_kernel(plane, last, *refs):
    refs = list(refs)
    count_ref, list_ref, valid_ref = refs[:3]
    x_refs = [refs[3], refs[5].at[0], refs[4], refs[5].at[1]]
    w_ref = refs[6]
    refs = refs[7:]
    if plane:
        q_ref, acc_in = refs.pop(0), refs.pop(0)
    if last:
        before, refs = refs[:plane], refs[plane:]
    kv_ref = refs.pop(0)
    if plane == 0:
        q_ref = refs.pop(0)
    if last:
        out_ref, exact_ref, lse_ref = refs.pop(0), refs.pop(0), refs.pop(0)
        keys, values_t, q_ext, acc, top, kv_copy, copied = refs
    else:
        acc = refs.pop(0)
        keys, values_t, q_ext = refs
    marks = w_ref[:, 3 * LANES : 4 * LANES].astype(F32).T
    gain, bias = marks[64:65], marks[65:66]
    for slot, x_ref in enumerate(x_refs):
        rows = slice(slot * BLOCK, (slot + 1) * BLOCK)
        normed, ignored, ignored_too = norm_rows(x_ref[...].astype(F32), gain, bias)
        normed = normed.astype(BF16)
        kv_ref[rows, :] = dot_on(normed, w_ref[:, : 3 * LANES], 1, 0).astype(BF16)
        if plane == 0:
            own = dot_on(normed, w_ref[:, 3 * LANES :], 1, 0) * HDIM ** (-0.5)
            q_ref[rows, :] = own.astype(BF16)
    fill_keys(4, kv_ref, valid_ref, keys, values_t=values_t, marks_first=4 * plane)
    if plane == 0:
        acc[...] = jnp.zeros_like(acc)
    else:
        acc[...] = acc_in[...]

    def set_queries(block):
        q_rows = pl.ds(pl.multiple_of(block * BLOCK, BLOCK), BLOCK)
        lane = lax.broadcasted_iota(jnp.int32, (BLOCK, LANES), 1)
        row = lax.broadcasted_iota(jnp.int32, (BLOCK, LANES), 0)
        real = row < valid_ref[block]
        marks = jnp.where((lane == 67) & real, 1.0, 0.0)
        marks = jnp.where((lane == 68) & jnp.logical_not(real), 1.0, marks)
        for head in range(3):
            own = q_ref[q_rows, head * LANES : (head + 1) * LANES].astype(F32)
            q_ext[head] = jnp.where(lane < 64, own, marks).astype(BF16)
        return q_rows

    def scores_of(slot, head):
        rows = pl.ds(pl.multiple_of(slot * BLOCK, BLOCK), BLOCK)
        return dot_on(keys[head, rows, :], q_ext[head], 1, 1)

    def over_queries(block, carry):
        q_rows = set_queries(block)

        def over_keys(item, carry_in):
            slot = list_ref[plane, block, item]
            rows = pl.ds(pl.multiple_of(slot * BLOCK, BLOCK), BLOCK)
            ready = [scores_of(slot, 0), scores_of(slot, 1)]
            for head in range(3):
                if head == 0:
                    ready.append(scores_of(slot, 2))
                weights = jnp.exp(ready.pop(0)).astype(BF16)
                acc[head, :, q_rows] += dot_on(values_t[head, :, rows], weights, 1, 0)
            return carry_in

        lax.fori_loop(0, count_ref[plane, block], over_keys, 0)
        return carry

    lax.fori_loop(0, 4, over_queries, 0)
    if not last:
        return
    sums = acc[:, 64:65, :]
    good = (sums >= 2.0**-60) & (sums <= 2.0**100)
    safe = jnp.min(jnp.where(good, 1.0, 0.0)) > 0.5
    top[...] = jnp.zeros_like(top)

    @pl.when(jnp.logical_not(safe))
    def _():
        top[...] = jnp.full_like(top, MASKED)
        acc[...] = jnp.zeros_like(acc)
        for which, source in enumerate(list(before) + [kv_ref]):
            if which < plane:
                move = pltpu.make_async_copy(source, kv_copy, copied)
                move.start()
                move.wait()
                source = kv_copy
            fill_keys(4, source, valid_ref, keys, values_t=values_t, marks_first=4 * which)

            def over_queries_again(block, carry, which=which):
                q_rows = set_queries(block)

                def with_max(item, carry_in):
                    slot = list_ref[which, block, item]
                    rows = pl.ds(pl.multiple_of(slot * BLOCK, BLOCK), BLOCK)
                    for head in range(3):
                        scores = scores_of(slot, head)
                        old = top[head, :, q_rows]
                        now = jnp.maximum(old, jnp.max(scores, axis=0, keepdims=True))
                        weights = jnp.exp(scores - now).astype(BF16)
                        top[head, :, q_rows] = now
                        acc[head, :, q_rows] = acc[head, :, q_rows] * jnp.exp(
                            old - now
                        ) + dot_on(values_t[head, :, rows], weights, 1, 0)
                    return carry_in

                lax.fori_loop(0, count_ref[which, block], with_max, 0)
                return carry

            lax.fori_loop(0, 4, over_queries_again, 0)

    for head in range(3):
        total = acc[head, 64:65, :]
        result = acc[head, 0:64, :] / total
        exact_ref[head] = result
        out_ref[head] = result.astype(BF16)
        lse_ref[head] = top[head] + jnp.log(total)


def attend_forward(plane, last, counts, lists, valid, blocks, weights, queries, acc, before):
    kv_rows = 4 * BLOCK
    smem = pl.BlockSpec(memory_space=pltpu.SMEM)
    vmem = pl.BlockSpec(memory_space=pltpu.VMEM)
    anywhere = pl.BlockSpec(memory_space=pl.ANY)
    packed = jax.ShapeDtypeStruct((kv_rows, 3 * LANES), BF16)
    sums = jax.ShapeDtypeStruct((3, 80, kv_rows), F32)
    inputs = [counts, lists, valid] + list(blocks) + [weights]
    inputs += [queries, acc] if plane else []
    outs = [packed] + ([packed] if plane == 0 else [])
    scratch = [
        pltpu.VMEM((3, kv_rows, LANES), BF16),
        pltpu.VMEM((3, 80, kv_rows), BF16),
        pltpu.VMEM((3, BLOCK, LANES), BF16),
    ]
    in_specs = [smem] * 3 + [vmem] * (len(inputs) - 3)
    if last:
        inputs += list(before)
        in_specs += [anywhere] * len(before)
        outs += [
            jax.ShapeDtypeStruct((3, HDIM, kv_rows), BF16),
            jax.ShapeDtypeStruct((3, HDIM, kv_rows), F32),
            jax.ShapeDtypeStruct((3, 1, kv_rows), F32),
        ]
        scratch += [
            pltpu.VMEM((3, 80, kv_rows), F32),
            pltpu.VMEM((3, 1, kv_rows), F32),
            pltpu.VMEM((kv_rows, 3 * LANES), BF16),
            pltpu.SemaphoreType.DMA,
        ]
    else:
        outs += [sums]
    return pl.pallas_call(
        partial(forward_kernel, plane, last),
        out_shape=tuple(outs),
        in_specs=in_specs,
        out_specs=(vmem,) * len(outs),
        scratch_shapes=scratch,
        compiler_params=pltpu.CompilerParams(vmem_limit_bytes=40 << 20),
        cost_estimate=pl.CostEstimate(
            flops=12 * 1000 * 1000 * 1000, bytes_accessed=10 << 20, transcendentals=7 << 20
        ),
        name="attend_forward",
    )(*inputs)


def backward_kernel(plane, carried, last, *refs):
    refs = list(refs)
    count_ref, list_ref, valid_ref = refs[:3]
    q_ref, kv_ref, out_ref, lse_ref, grad_ref, w_ref = refs[3:9]
    x_from = [refs[9], refs[11].at[0], refs[10], refs[11].at[1]]
    refs = refs[12:]
    sum_in, refs = refs[0], refs[1:]
    if carried:
        dq_in, dw_in = refs[:2]
        refs = refs[2:]
    if last:
        keep_ref, send_ref, dw_out = refs[:3]
        dw_ref, dwq_ref, sum_ref = refs[-3:]
        dq_ref = None
        refs = refs[3:-3]
    else:
        keep_ref, send_ref, dw_ref, dq_ref, sum_ref = refs[:5]
        refs = refs[5:]
    keys, values, q_ext, g_ext, q_turned, dq_acc, dkv_acc, x_ref, moved = refs
    slots = 4
    moves = [
        pltpu.make_async_copy(x_from[i], x_ref.at[pl.ds(i * BLOCK, BLOCK)], moved.at[i])
        for i in range(slots)
    ]
    if carried:
        moves.append(pltpu.make_async_copy(dq_in, dq_acc, moved.at[4]))
    for move in moves:
        move.start()
    fill_keys(slots, kv_ref, valid_ref, keys, values_out=values, marks_first=4 * plane)
    lane = lax.broadcasted_iota(jnp.int32, (BLOCK, LANES), 1)

    def clear(slot, carry):
        rows = pl.ds(pl.multiple_of(slot * BLOCK, BLOCK), BLOCK)
        for head in range(3):
            dkv_acc[head, :, rows] = jnp.zeros((LANES, BLOCK), F32)
        return carry

    lax.fori_loop(0, slots, clear, 0)
    if carried:
        moves[4].wait()
    else:
        dq_acc[...] = jnp.zeros_like(dq_acc)

    def over_queries(block, carry):
        q_rows = pl.ds(pl.multiple_of(block * BLOCK, BLOCK), BLOCK)
        for head in range(3):
            lanes = slice(head * LANES, (head + 1) * LANES)
            turned = q_ref[q_rows, lanes].astype(F32).T[0:64]
            grad_t = grad_ref[head, :, q_rows].astype(F32)
            delta = jnp.sum(grad_t * out_ref[head, :, q_rows], axis=0, keepdims=True)
            marks = split_three(-lse_ref[head, :, q_rows]) + query_marks(valid_ref[block], BLOCK)
            blank = jnp.zeros((64 - len(marks), BLOCK), F32)
            q_turned[head] = turned.astype(BF16)
            q_ext[head] = jnp.concatenate([turned] + marks + [blank], axis=0).T.astype(BF16)
            minus = split_three(-delta)
            blank = jnp.zeros((64 - len(minus), BLOCK), F32)
            g_ext[head] = jnp.concatenate(minus + [blank, grad_t], axis=0).T.astype(BF16)

        def over_keys(item, carry_in):
            slot = list_ref[plane, block, item]
            rows = pl.ds(pl.multiple_of(slot * BLOCK, BLOCK), BLOCK)

            def products(head):
                return (
                    dot_on(q_ext[head], keys[head, rows, :], 1, 1),
                    dot_on(g_ext[head], values[head, rows, :], 1, 1),
                )

            ready = [products(0)]
            for head in range(3):
                lanes = slice(head * LANES, (head + 1) * LANES)
                if head < 2:
                    ready.append(products(head + 1))
                scores, grad_probs = ready.pop(0)
                probs = jnp.exp(scores)
                grad_scores = (probs * grad_probs).astype(BF16)
                dkv_acc[head, 64:128, rows] += dot_on(
                    grad_ref[head, :, q_rows], probs.astype(BF16), 1, 0
                )
                dkv_acc[head, 0:64, rows] += dot_on(q_turned[head], grad_scores, 1, 0)
                dq_acc[q_rows, lanes] += dot_on(grad_scores, keys[head, rows, :], 1, 0)
            return carry_in

        lax.fori_loop(0, count_ref[plane, block], over_keys, 0)
        return carry

    lax.fori_loop(0, 4, over_queries, 0)
    for move in moves[:4]:
        move.wait()
    if not last:
        leave = pltpu.make_async_copy(dq_acc, dq_ref, moved.at[4])
        leave.start()
    if carried:
        dw_ref[...] = dw_in[...]
    else:
        dw_ref[...] = jnp.zeros_like(dw_ref)
    sum_ref[...] = sum_in[...]
    if last:
        dwq_ref[...] = jnp.zeros_like(dwq_ref)
    marks = w_ref[:, 3 * LANES : 4 * LANES].astype(F32).T
    gain, bias = marks[64:65], marks[65:66]

    def finish(slot, carry):
        rows = pl.ds(pl.multiple_of(slot * BLOCK, BLOCK), BLOCK)
        pieces = []
        for head in range(3):
            pieces.append(dkv_acc[head, 0:64, rows])
            pieces.append(dkv_acc[head, 64:128, rows])
        turned = jnp.concatenate(pieces, axis=0)
        part = dot_on(turned.T.astype(BF16), w_ref[:, : 3 * LANES], 1, 1)
        values_now = x_ref[rows, :].astype(F32)
        normed, unit, ignored = norm_rows(values_now, gain, bias)
        normed = normed.astype(BF16)
        dw_ref[...] += dot_on(turned.astype(BF16), normed, 1, 0)
        if last:
            scaled = [
                jnp.where(lane < 64, dq_acc[rows, h * LANES : (h + 1) * LANES], 0.0)
                for h in range(3)
            ]
            scaled = jnp.concatenate(scaled, axis=1) * HDIM ** (-0.5)
            part = part + dot_on(scaled.astype(BF16), w_ref[:, 3 * LANES :], 1, 1)
            dwq_ref[...] += dot_on(scaled.T.astype(BF16), normed, 1, 0)
        sum_ref[0:1, :] += jnp.sum(part * unit, axis=0, keepdims=True)
        sum_ref[1:2, :] += jnp.sum(part, axis=0, keepdims=True)
        low = part.astype(BF16)

        @pl.when(slot % 2 == 0)
        def _():
            keep_ref[slot // 2] = low

        @pl.when(slot % 2 == 1)
        def _():
            send_ref[slot // 2] = low

        return carry

    lax.fori_loop(0, slots, finish, 0)
    if not last:
        leave.wait()
        return
    pieces = []
    for head in range(3):
        first = head * LANES
        pieces.append(dwq_ref[first : first + 64, :])
        pieces.append(dw_ref[first : first + LANES, :])
    pieces += [sum_ref[...], jnp.zeros((LANES - 8, D), F32)]
    dw_out[...] = jnp.concatenate(pieces, axis=0).T.astype(BF16)


def attend_backward(
    plane, counts, lists, valid, queries, key_vals, attended, lse, grads, weights, blocks, carry, last
):
    q_rows = queries.shape[0]
    smem = pl.BlockSpec(memory_space=pltpu.SMEM)
    vmem = pl.BlockSpec(memory_space=pltpu.VMEM)
    anywhere = pl.BlockSpec(memory_space=pl.ANY)
    carry = list(carry)
    half = jax.ShapeDtypeStruct((2, BLOCK, D), BF16)
    weight = jax.ShapeDtypeStruct((3 * LANES, D), F32)
    sums = jax.ShapeDtypeStruct((8, D), F32)
    if last:
        outs = (jax.ShapeDtypeStruct((D, 9 * HDIM + LANES), BF16),)
        spaces, kept = (vmem,), [weight, weight, sums]
    else:
        outs = (weight, jax.ShapeDtypeStruct((q_rows, 3 * LANES), F32), sums)
        spaces, kept = (vmem, anywhere, vmem), []
    result = pl.pallas_call(
        partial(backward_kernel, plane, len(carry) > 1, last),
        out_shape=(half, half) + outs,
        in_specs=[smem] * 3 + [vmem] * 6 + [anywhere] * 3 + [vmem, anywhere, vmem][: len(carry)],
        out_specs=(vmem, vmem) + spaces,
        scratch_shapes=[
            pltpu.VMEM((3, q_rows, LANES), BF16),
            pltpu.VMEM((3, q_rows, LANES), BF16),
            pltpu.VMEM((3, BLOCK, LANES), BF16),
            pltpu.VMEM((3, BLOCK, LANES), BF16),
            pltpu.VMEM((3, HDIM, BLOCK), BF16),
            pltpu.VMEM((q_rows, 3 * LANES), F32),
            pltpu.VMEM((3, LANES, q_rows), F32),
            pltpu.VMEM((q_rows, D), BF16),
            pltpu.SemaphoreType.DMA((5,)),
        ]
        + [pltpu.VMEM(k.shape, k.dtype) for k in kept],
        compiler_params=pltpu.CompilerParams(vmem_limit_bytes=34 << 20),
        cost_estimate=pl.CostEstimate(
            flops=25 * 1000 * 1000 * 1000, bytes_accessed=16 << 20, transcendentals=7 << 20
        ),
        name="attend_backward",
    )(
        counts, lists, valid, queries, key_vals, attended, lse, grads, weights, *blocks, *carry
    )
    return tuple(result) + (None,) * (5 - len(result))


def erf_of(values):
    clamped = jnp.clip(values, -4.0, 4.0)
    square = clamped * clamped
    top = jnp.float32(-2.72614225801306e-10)
    for term in (
        2.77068142495902e-08,
        -2.10102402082508e-06,
        -5.69250639462346e-05,
        -7.34990630326855e-04,
        -2.95459980854025e-03,
        -1.60960333262415e-02,
    ):
        top = top * square + term
    low = jnp.float32(-1.45660718464996e-05)
    for term in (
        -2.13374055278905e-04,
        -1.68282697438203e-03,
        -7.37332916720468e-03,
        -1.42647390514189e-02,
    ):
        low = low * square + term
    return clamped * top / low


def middle_kernel(pieces, pair, shard, *refs):
    refs = list(refs)
    start_ref, group_ref = refs[:2]
    merged_refs, refs = refs[2:6], refs[6:]
    token_ref, cot_ref, mark_ref = refs[:3]
    piece_refs, refs = refs[3 : 3 + pieces], refs[3 + pieces :]
    output_ref, grad_y_ref, grad_z_ref, h_two_ref, hidden_ref, grad_up_ref = refs[:6]
    part_refs, sum_ref, norm_ref, refs = refs[6:10], refs[10], refs[11], refs[12:]
    w_out, w_up, w_down, moved = refs
    parts = []
    for piece in piece_refs:
        parts += [(piece, base) for base in range(0, piece.shape[0], 9 * pair)]

    def moves_of(weight):
        moves = []
        for i, (piece, base) in enumerate(parts):
            if weight < 5:
                source = piece.at[pl.ds(base + weight * pair, pair)]
                rows = pl.ds(pl.multiple_of(start_ref[i] * shard, pair), pair)
                target = w_out.at[rows] if weight == 0 else w_up.at[weight - 1, rows]
            else:
                source = piece.at[pl.ds(base + 5 * pair, 4 * pair)]
                rows = pl.ds(pl.multiple_of(start_ref[i] * 4 * shard, 4 * pair), 4 * pair)
                target = w_down.at[rows]
            moves.append(pltpu.make_async_copy(source, target, moved.at[weight, i]))
        return moves

    arriving = [moves_of(weight) for weight in range(6)]
    for weight in (0, 1, 5, 2, 3, 4):
        for move in arriving[weight]:
            move.start()
    norm_ref[...] = mark_ref[...].astype(F32).T[64:72]
    for move in arriving[0]:
        move.wait()
    y_one = token_ref[...].astype(F32)
    group = D // 4
    for j, merged_ref in enumerate(merged_refs):
        rows = pl.ds(pl.multiple_of(group_ref[j] * group, group), group)
        turned = merged_ref[...].astype(F32).T.astype(BF16)
        y_one = y_one + dot_on(turned, w_out[rows, :], 1, 0)
    grad_y_ref[...] = y_one
    gain, bias = norm_ref[2:3, :], norm_ref[3:4, :]
    normed, unit, inv_rows = norm_rows(y_one, gain, bias)
    h_two_ref[...] = normed.astype(BF16)

    output_sum = jnp.zeros((BLOCK, D), F32)
    grad_sum = jnp.zeros((BLOCK, D), F32)
    for j in range(4):
        for move in arriving[1 + j]:
            move.wait()
        if j == 0:
            for move in arriving[5]:
                move.wait()
        columns = slice(j * D, (j + 1) * D)
        up = dot_on(h_two_ref[...], w_up[j], 1, 0)
        grad_hidden = dot_on(cot_ref[...], w_down[columns, :], 1, 1)
        normal = 0.5 + 0.5 * erf_of(up * 0.7071067811865476)
        density = jnp.exp(-0.5 * up * up) * 0.3989422804014327
        hidden = (up * normal).astype(BF16)
        grad_up = (grad_hidden * (normal + up * density)).astype(BF16)
        hidden_ref[:, columns] = hidden
        grad_up_ref[:, columns] = grad_up
        output_sum = output_sum + dot_on(hidden, w_down[columns, :], 1, 0)
        grad_sum = grad_sum + dot_on(grad_up, w_up[j], 1, 1)
    y_one = grad_y_ref[...]
    output_ref[...] = (y_one + output_sum).astype(BF16)
    normed, unit, inv_rows = norm_rows(y_one, gain, bias)
    sum_ref[...] = jnp.zeros_like(sum_ref)
    sum_ref[2:3, :] = jnp.sum(grad_sum * unit, axis=0, keepdims=True)
    sum_ref[3:4, :] = jnp.sum(grad_sum, axis=0, keepdims=True)
    grad_y = cot_ref[...].astype(F32) + norm_back(grad_sum, unit, inv_rows, gain)
    grad_y_ref[...] = grad_y
    grad_z = grad_y.astype(BF16)
    grad_z_ref[...] = grad_z
    for j, part_ref in enumerate(part_refs):
        rows = pl.ds(pl.multiple_of(group_ref[j] * group, group), group)
        part_ref[...] = dot_on(w_out[rows, :], grad_z, 1, 1).astype(BF16)


def middle(starts, groups, merged, tokens, cotangent, marks, pieces, shard):
    smem = pl.BlockSpec(memory_space=pltpu.SMEM)
    vmem = pl.BlockSpec(memory_space=pltpu.VMEM)
    anywhere = pl.BlockSpec(memory_space=pl.ANY)
    rows = tokens.shape[0]
    number = starts.shape[0]
    pair = sum(piece.shape[0] for piece in pieces) // (9 * number)

    def shape(columns, dtype, height=rows):
        return jax.ShapeDtypeStruct((height, columns), dtype)

    return pl.pallas_call(
        partial(middle_kernel, len(pieces), pair, shard),
        out_shape=(
            shape(D, BF16),
            shape(D, F32),
            shape(D, BF16),
            shape(D, BF16),
            shape(4 * D, BF16),
            shape(4 * D, BF16),
        )
        + (shape(rows, BF16, D // 4),) * 4
        + (shape(D, F32, 8),) * 2,
        in_specs=[smem, smem] + [vmem] * 7 + [anywhere] * len(pieces),
        out_specs=(vmem,) * 12,
        scratch_shapes=[
            pltpu.VMEM((D, D), BF16),
            pltpu.VMEM((4, D, D), BF16),
            pltpu.VMEM((4 * D, D), BF16),
            pltpu.SemaphoreType.DMA((6, number)),
        ],
        compiler_params=pltpu.CompilerParams(vmem_limit_bytes=58 << 20),
        cost_estimate=pl.CostEstimate(
            flops=12 * 1000 * 1000 * 1000, bytes_accessed=24 << 20, transcendentals=3 << 20
        ),
        name="middle",
    )(starts, groups, *merged, tokens, cotangent, marks, *pieces)


def put_halves(core, rows, keep_ref, give_ref, place, columns, values):
    for i in range(values.shape[0] // (2 * rows)):
        for which in range(2):
            first = (2 * i + which) * rows
            piece = values[first : first + rows].astype(BF16)
            start = place + i * rows
            if not isinstance(start, int):
                start = pl.multiple_of(start, rows)
            target = pl.ds(start, rows)

            @pl.when(core == which)
            def _(piece=piece, target=target):
                keep_ref[target, columns] = piece

            @pl.when(core != which)
            def _(piece=piece, target=target):
                give_ref[target, columns] = piece


def down_kernel(line, core_ref, hidden_ref, cot_ref, keep_ref, give_ref):
    block = dot_on(hidden_ref[...], cot_ref[...], 0, 0)
    put_halves(core_ref[0], 4 * line, keep_ref, give_ref, 0, slice(0, D), block)


def wide_kernel(line, *refs):
    core_ref, group_ref, h_two_ref, grad_up_ref, grad_z_ref = refs[:5]
    merged_refs, (keep_ref, give_ref) = refs[5:9], refs[9:]
    core, step = core_ref[0], pl.program_id(0)
    columns = slice(0, D)

    @pl.when(step < 4)
    def _():
        block = dot_on(h_two_ref[...], grad_up_ref[...], 0, 0)
        put_halves(core, line, keep_ref, give_ref, 0, columns, block)

    @pl.when(step == 4)
    def _():
        group = D // 4
        for j, merged_ref in enumerate(merged_refs):
            block = dot_on(merged_ref[...], grad_z_ref[...], 1, 0)
            place = group_ref[j] * (group // 2)
            put_halves(core, line, keep_ref, give_ref, place, columns, block)


def halves_of_down(line, core, hidden, cotangent):
    rows = cotangent.shape[0]
    half = pl.BlockSpec((D // 2, D), lambda j: (j, 0))
    return pl.pallas_call(
        partial(down_kernel, line),
        grid=(4,),
        out_shape=(jax.ShapeDtypeStruct((2 * D, D), BF16),) * 2,
        in_specs=[
            pl.BlockSpec(memory_space=pltpu.SMEM),
            pl.BlockSpec((rows, D), lambda j: (0, j)),
            pl.BlockSpec((rows, D), lambda j: (0, 0)),
        ],
        out_specs=(half, half),
        compiler_params=pltpu.CompilerParams(vmem_limit_bytes=54 << 20),
        cost_estimate=pl.CostEstimate(
            flops=3 * 10**9, bytes_accessed=10 << 20, transcendentals=0
        ),
        name="grad_down",
    )(core, hidden, cotangent)


def halves_of_wide(line, core, groups, h_two, grad_up, grad_z, merged):
    rows = h_two.shape[0]
    smem = pl.BlockSpec(memory_space=pltpu.SMEM)
    whole = pl.BlockSpec((rows, D), lambda j: (0, 0))
    half = pl.BlockSpec((D // 2, D), lambda j: (0, j))
    return pl.pallas_call(
        partial(wide_kernel, line),
        grid=(5,),
        out_shape=(jax.ShapeDtypeStruct((D // 2, 5 * D), BF16),) * 2,
        in_specs=[smem, smem, whole]
        + [pl.BlockSpec((rows, D), lambda j: (0, jnp.minimum(j, 3))), whole]
        + [pl.BlockSpec((D // 4, rows), lambda j: (0, 0))] * 4,
        out_specs=(half, half),
        compiler_params=pltpu.CompilerParams(vmem_limit_bytes=54 << 20),
        cost_estimate=pl.CostEstimate(
            flops=4 * 10**9, bytes_accessed=12 << 20, transcendentals=0
        ),
        name="grad_wide",
    )(core, groups, h_two, grad_up, grad_z, *merged)


def scene_lists(same):
    number = same.shape[-1]
    slot = jnp.arange(number)
    counts = jnp.sum(same, axis=-1).astype(jnp.int32)
    earlier = slot[None, :] < slot[:, None]
    place = jnp.sum(same[:, :, None, :] & earlier, axis=-1)
    hits = same[:, :, None, :] & (place[:, :, None, :] == slot[:, None])
    lists = jnp.sum(jnp.where(hits, slot, 0), axis=-1)
    return counts, lists.astype(jnp.int32)


def halve(value, axis, bit, send):
    give = lax.dynamic_index_in_dim(value, 1 - bit, axis, keepdims=False)
    return value, send(give)


def settle(pending, axis, bit):
    value, taken = pending
    keep = lax.dynamic_index_in_dim(value, bit, axis, keepdims=False)
    return (keep.astype(F32) + taken.astype(F32)).astype(BF16)


def ring_sources(count):
    order = ring_order(count)
    table = [[order[(order.index(c) - r) % count] for r in range(count)] for c in range(count)]
    return jnp.array(table, jnp.int32)[lax.axis_index("ctx")]


def give_over_seq(value):
    count = lax.axis_size("seq")
    me = lax.axis_index("seq")
    while True:
        count //= 2
        pairs = [(i, i ^ count) for i in range(lax.axis_size("seq"))]
        pending = halve(
            value.reshape((2, count) + value.shape[1:]),
            0,
            (me // count) % 2,
            lambda give: lax.ppermute(give, "seq", pairs),
        )
        if count == 1:
            return pending
        value = settle(pending, 0, (me // count) % 2)


def sum_over_seq(pending):
    value = settle(pending, 0, lax.axis_index("seq") % 2)
    return value.reshape(value.shape[1:])


def gather_bit(value, bit, send):
    other = send(value)
    first = jnp.where(bit == 0, value, other)
    return jnp.concatenate([first, jnp.where(bit == 0, other, value)], axis=0)


def gather_seq(value):
    count, reach = lax.axis_size("seq"), 1
    me = lax.axis_index("seq")
    while reach < count:
        pairs = [(i, i ^ reach) for i in range(count)]
        value = gather_bit(
            value[None], (me // reach) % 2, lambda v: lax.ppermute(v, "seq", pairs)
        ).reshape((2 * reach,) + value.shape[1:])
        reach *= 2
    return value


def swap_seq(value, mask=1):
    return lax.ppermute(value, "seq", [(i, i ^ mask) for i in range(lax.axis_size("seq"))])


def in_order(blocks, sources, shard):
    count = len(blocks)
    full = jnp.zeros((count,) + blocks[0].shape, BF16)
    for r in range(count):
        full = lax.dynamic_update_index_in_dim(full, blocks[r], sources[r], 0)
    cuts = []
    for half in range(2):
        part = full[half * (count // 2) : (half + 1) * (count // 2)]
        cut = [part[:, i * shard : (i + 1) * shard] for i in range(5)] + [part[:, 5 * shard :]]
        cuts += [c.reshape(-1, D) for c in cut]
    return jnp.concatenate(cuts, axis=0)


def join_halves(pieces, places, number):
    def woven(first, second):
        rows = first.shape[0] // 9
        cuts = [i * rows for i in range(1, 6)]
        both = zip(jnp.split(first, cuts), jnp.split(second, cuts))
        return jnp.concatenate([part for pair in both for part in pair], axis=0)

    joined, kept = [], []
    for base in range(0, len(pieces), number):
        for i in (0, 1):
            joined.append(woven(*jnp.split(pieces[base + i], 2)))
            kept.append(((0,),) + places[base + i][1:])
        for i in (2, 4):
            joined.append(woven(pieces[base + i], pieces[base + i + 1]))
            kept.append(((0,),) + places[base + i][1:])
    return joined, kept


def gather_ctx(value):
    count = lax.axis_size("ctx")
    sources = ring_sources(count)
    whole = jnp.zeros((count,) + value.shape, value.dtype)
    whole = lax.dynamic_update_index_in_dim(whole, value, sources[0], 0)
    for r in range(1, count):
        whole = lax.dynamic_update_index_in_dim(whole, ring_send(value, r), sources[r], 0)
    return whole


def sum_over_core(pending):
    keep, taken = pending
    return (keep.astype(F32) + taken.astype(F32)).astype(BF16)


def give_over_x(value):
    return halve(value, 0, lax.axis_index("head") // 2, lambda give: swap_head(give, 2))


def sum_over_x(pending):
    return settle(pending, 0, lax.axis_index("head") // 2)


def send_term(value, r):
    source = ring_sources(lax.axis_size("ctx"))[r]
    return ring_send(lax.dynamic_index_in_dim(value, source, 0, keepdims=False), -r)


def sum_terms(value, terms):
    source = ring_sources(lax.axis_size("ctx"))[0]
    total = lax.dynamic_index_in_dim(value, source, 0, keepdims=False).astype(F32)
    for term in terms:
        total = total + term.astype(F32)
    return total


def sum_over_ctx(value):
    count = lax.axis_size("ctx")
    sources = ring_sources(count)
    total = lax.dynamic_index_in_dim(value, sources[0], 0, keepdims=False).astype(F32)
    for r in range(1, count):
        give = lax.dynamic_index_in_dim(value, sources[r], 0, keepdims=False)
        total = total + ring_send(give, -r).astype(F32)
    return total


def tie(*values):
    return lax.optimization_barrier(values)


def body(
    tokens,
    segment_ids,
    w_qkv,
    w_out,
    w_up,
    w_down,
    gain_one,
    bias_one,
    gain_two,
    bias_two,
    cotangent,
):
    heads_ax = lax.axis_size("head")
    ctx_ax = lax.axis_size("ctx")
    seq_ax = lax.axis_size("seq")
    me_head = lax.axis_index("head")
    tok_rows = tokens.shape[0]
    group = D // heads_ax
    shard = w_qkv.shape[0]

    order = [me_head ^ j for j in range(heads_ax)]
    sources = ring_sources(ctx_ax)
    wide = 3 * group + LANES

    padding = tok_rows - jnp.sum(segment_ids >= 0)
    about = jnp.stack([segment_ids[0], padding // 16, padding % 16]).astype(BF16)
    extra = jnp.stack([gain_one, bias_one, gain_two, bias_two], axis=1)
    extra = jnp.concatenate([extra, jnp.broadcast_to(about[None, :], (shard, 3))], axis=1)
    extra = jnp.pad(extra, ((0, 0), (0, HDIM - 7)))
    by_head = w_qkv.reshape(shard, heads_ax, 3, 3, HDIM)
    beside = jnp.zeros((shard, heads_ax, 2, HDIM), BF16)
    beside = jnp.concatenate(
        [jnp.broadcast_to(extra[:, None, None], (shard, heads_ax, 1, HDIM)), beside], axis=2
    )
    packed = jnp.concatenate(
        [
            by_head[:, :, :, 1:].reshape(shard, heads_ax, 3 * LANES),
            jnp.stack([by_head[:, :, :, 0], beside], axis=3).reshape(shard, heads_ax, 3 * LANES),
        ],
        axis=2,
    )
    packed = jnp.swapaxes(packed, 0, 1)
    got = tie(
        *[lax.dynamic_index_in_dim(packed, o, 0, keepdims=False) for o in order]
    )
    got = [swap_head(piece, j) if j else piece for j, piece in enumerate(got)]
    w_rest = jnp.concatenate(
        [w_out] + [w_up[:, i * D : (i + 1) * D] for i in range(4)] + [w_down], axis=0
    )
    w_rest, *got = tie(w_rest, *got)
    mine = jnp.zeros((heads_ax, shard, D), BF16)
    for j in range(heads_ax):
        mine = lax.dynamic_update_index_in_dim(mine, got[j], order[j], 0)
    ring_mine = [mine] + [ring_send(mine, i) for i in range(1, ctx_ax)]

    rest = [w_rest]
    near, ahead, behind = swap_head(tokens, 2), ring_send(tokens, 1), ring_send(w_rest, 1)
    near, ahead, behind, *ring_mine = tie(near, ahead, behind, *ring_mine)
    rest.append(behind)
    packed = jnp.zeros((ctx_ax,) + mine.shape, BF16)
    for r in range(ctx_ax):
        packed = lax.dynamic_update_index_in_dim(packed, ring_mine[r], sources[r], 0)

    def weights_here(packed):
        weights = jnp.swapaxes(gather_seq(packed[None]), 1, 2).reshape(D, D)
        first = 3 * LANES + HDIM + 4
        about_all = weights[::shard, first : first + 3].astype(jnp.int32)
        about_all = lax.dynamic_index_in_dim(
            about_all.reshape(seq_ax, heads_ax, ctx_ax, 3),
            lax.axis_index("seq"),
            0,
            keepdims=False,
        )
        pick_head = jnp.stack(order)[:, None] == jnp.arange(heads_ax)[None, :]
        pick_ctx = sources[:, None] == jnp.arange(ctx_ax)[None, :]
        pick = pick_ctx[:, None, None, :] & pick_head[None, :, :, None]
        slot_about = jnp.sum(jnp.where(pick[..., None], about_all[None, None], 0), axis=(2, 3))
        slot_ids = slot_about[:, :, 0]
        slot_valid = (tok_rows - (slot_about[:, :, 1] * 16 + slot_about[:, :, 2])).reshape(-1)
        counts, lists = scene_lists(slot_ids[0][None, :, None] == slot_ids[:, None, :])
        return weights, counts, lists, slot_valid

    planes, key_vals, queries, acc = [], [], None, None
    block = tokens
    ready = None
    for r in range(ctx_ax + 1):
        if r < ctx_ax:
            travelers = [swap_head(jnp.stack([block, near]), 1)]
        else:
            travelers = []
        if r + 1 < ctx_ax:
            travelers.append(swap_head(ahead, 2))
        if r + 2 < ctx_ax:
            travelers.append(ring_send(ahead, 1))
            travelers.append(ring_send(rest[-1], 1))
        count = len(travelers)
        if r == ctx_ax - 2:
            line = in_order(rest, sources, shard)
            middle_row = line.shape[0] // 2
            travelers += [swap_head(line[:middle_row], 2), swap_seq(line)]
        if r == ctx_ax - 1:
            travelers += [swap_head(line[middle_row:], 2), swap_seq(x_first), swap_head(line, 1)]
        if r == ctx_ax:
            travelers += [swap_seq(x_second), swap_head(y_line, 1), swap_head(x_first, 1)]
        results = []
        if ready is not None:
            results = list(
                attend_forward(
                    r - 1,
                    r == ctx_ax,
                    counts,
                    lists,
                    slot_valid,
                    ready,
                    weights,
                    queries,
                    acc,
                    key_vals,
                )
            )
        tied = list(tie(*travelers, *results))
        extra, tied = tied[count : len(travelers)], tied[:count] + tied[len(travelers) :]
        if r == 0:
            weights, counts, lists, slot_valid = weights_here(packed)
        if r == ctx_ax - 2:
            x_first, y_line = extra
        if r == ctx_ax - 1:
            x_second, xy_first, core_line = extra
        if r == ctx_ax:
            xy_second, core_y, core_x_first = extra
            results = tied
            break
        planes.append([block, near, tied.pop(0)])
        ready = planes[-1]
        if r + 1 < ctx_ax:
            block, near = ahead, tied.pop(0)
        if r + 2 < ctx_ax:
            ahead = tied.pop(0)
            rest.append(tied.pop(0))
        if results:
            key_vals.append(tied.pop(0))
            if r == 1:
                queries = tied.pop(0)
            acc = tied.pop(0)
    key_vals.append(results[0])
    attended, exact, lse = results[1:]
    owns = [line, y_line, x_first, x_second, xy_first, xy_second]
    cores = [core_line, core_y, core_x_first]
    cores += [swap_head(v, 1) for v in (x_second, xy_first, xy_second)]
    offs = [((0, 1), 0, 0), ((0, 1), 0, 1), ((0,), 1, 0), ((1,), 1, 0), ((0,), 1, 1), ((1,), 1, 1)]
    me_x, me_core, me_seq = me_head // 2, me_head % 2, lax.axis_index("seq")
    pieces, places = [], []
    for core, arrays in enumerate((owns, cores)):
        for array, (halves, x, y) in zip(arrays, offs):
            pieces.append(array)
            places.append((halves, (me_x ^ x) * 2 + (me_core ^ core), y))
    reach = 2
    while reach < seq_ax:
        pieces += [swap_seq(array, reach) for array in pieces]
        places += [(halves, place, y ^ reach) for halves, place, y in places]
        reach *= 2
    if (ctx_ax // 2 * shard) % 8:
        pieces, places = join_halves(pieces, places, len(offs))
    starts = [
        ((me_seq ^ y) * heads_ax + place) * ctx_ax + half * (ctx_ax // 2)
        for halves, place, y in places
        for half in halves
    ]
    starts = jnp.stack(starts).astype(jnp.int32)

    merged = []
    for j in range(heads_ax):
        part = attended[:, :, j * tok_rows : (j + 1) * tok_rows].reshape(group, tok_rows)
        merged.append(swap_head(part, j) if j else part)

    marks = weights[:, 3 * LANES : 4 * LANES]
    groups = jnp.stack(order).astype(jnp.int32)
    output, grad_y_one, grad_z, h_two, hidden, grad_up, *rest_out = middle(
        starts, groups, merged, tokens, cotangent, marks, pieces, shard
    )
    grad_merged, sums_two, norms = rest_out[:4], rest_out[4], rest_out[5]

    grad_parts = [swap_head(p, j) if j else p for j, p in enumerate(grad_merged)]
    line = ctx_ax * shard
    outer = (seq_ax, 2, ctx_ax)
    me_bit = (me_head % 2)[None].astype(jnp.int32)
    keep, give = halves_of_down(line, me_bit, hidden, cotangent)
    shape = outer + (4 * shard, D)
    down_sum = (keep.reshape(shape), swap_head(give.reshape(shape), 1))
    h_two, keep, *_ = tie(h_two, down_sum[0])
    keep, give = halves_of_wide(line, me_bit, groups, h_two, grad_up, grad_z, merged)
    shape = outer + (shard, 5 * D)
    keep, give, *tied = tie(keep, give, *down_sum, *grad_parts)
    down_sum, grad_parts = sum_over_core(tied[:2]), tied[2:]
    grad_local = jnp.concatenate(grad_parts, axis=1).reshape(3, HDIM, heads_ax * tok_rows)
    wide_sum = (keep.reshape(shape), swap_head(give.reshape(shape), 1))
    down_sum = give_over_seq(down_sum)

    carry, traveling, near_half, far_half = (sums_two,), None, None, None
    for r in reversed(range(ctx_ax)):
        step = ctx_ax - 1 - r
        travelers = []
        if step >= 1:
            travelers.append(swap_head(far_half, 2))
        if step >= 2:
            travelers.append(ring_send(traveling, -1))
        count = len(travelers)
        if step == 0:
            travelers += [down_sum, wide_sum]
        if step == 1:
            travelers += [give_over_x(down_sum), give_over_seq(wide_sum)]
        if step == 2:
            travelers += [give_over_x(wide_sum)] + [send_term(down_sum, i) for i in (1, 2, 3)]
        if step == 3:
            travelers += [send_term(wide_sum, i) for i in (1, 2, 3)]
        keep, give, dw, fourth, sums = attend_backward(
            r,
            counts,
            lists,
            slot_valid,
            queries,
            key_vals[r],
            exact,
            lse,
            grad_local,
            weights,
            planes[r],
            carry,
            r == 0,
        )
        if r == 0:
            keep, give, dw, *travelers = tie(keep, give, dw, *travelers)
        else:
            keep, give, fourth, dw, sums, *travelers = tie(
                keep, give, fourth, dw, sums, *travelers
            )
        extra = travelers[count:]
        if step >= 1:
            moved = near_half.astype(F32) + travelers[0].astype(F32)
            if step >= 2:
                moved = moved + travelers[1].astype(F32)
            traveling = moved.astype(BF16)
        if step == 0:
            down_sum = sum_over_seq(extra[0])
            wide_sum = sum_over_core(extra[1])
        if step == 1:
            down_sum, wide_sum = sum_over_x(extra[0]), sum_over_seq(extra[1])
        if step == 2:
            wide_sum, down_terms = sum_over_x(extra[0]), list(extra[1:])
        if step == 3:
            wide_terms = list(extra)
        taken = swap_head(give, 1)
        near_half = (keep[0].astype(F32) + taken[0].astype(F32)).astype(BF16)
        far_half = (keep[1].astype(F32) + taken[1].astype(F32)).astype(BF16)
        if r:
            tied = [near_half, far_half, fourth, dw, sums, down_sum, wide_sum]
            tied += [traveling] if step >= 1 else []
            near_half, far_half, fourth, dw, sums, down_sum, wide_sum, *tied = tie(*tied)
            if step >= 1:
                traveling = tied[0]
        carry = (sums, fourth, dw)
    near_half, far_half, traveling, dw, wide_sum = tie(
        near_half, far_half, traveling, dw, wide_sum
    )
    dw_mine = give_over_seq(dw.reshape(seq_ax, heads_ax, ctx_ax, shard, wide))
    taken, carried, *dw_mine = tie(
        swap_head(far_half, 2), ring_send(traveling, -1), *dw_mine
    )
    dw_mine = sum_over_seq(dw_mine)
    grad_h_one = near_half.astype(F32) + taken.astype(F32) + carried.astype(F32)
    down_sum, wide_sum = sum_terms(down_sum, down_terms), sum_terms(wide_sum, wide_terms)
    up_sum, out_sum = wide_sum[:, : 4 * D], wide_sum[:, 4 * D :]
    dw_mine = sum_over_ctx(jnp.swapaxes(dw_mine, 0, 1)).astype(BF16)
    groups = []
    for j in range(heads_ax):
        part = lax.dynamic_index_in_dim(dw_mine, order[j], 0, keepdims=False)
        groups.append(swap_head(part, j) if j else part)
    groups = jnp.stack(groups)
    groups = jnp.stack(
        [lax.dynamic_index_in_dim(groups, o, 0, keepdims=False) for o in order]
    ).astype(F32)
    grad_w_qkv = jnp.swapaxes(groups[:, :, : 3 * group], 0, 1).reshape(shard, 3 * D)
    norm_sums = jnp.sum(groups[:, :, 3 * group : 3 * group + 4], axis=0)

    g_one = norms[0]
    ignored, unit_one, inv_one = norm_rows(tokens.astype(F32), g_one, norms[1])
    grad_tokens = (grad_y_one + norm_back(grad_h_one, unit_one, inv_one, g_one)).astype(BF16)
    return (
        output,
        grad_tokens,
        grad_w_qkv,
        out_sum,
        up_sum,
        down_sum,
        norm_sums[:, 0],
        norm_sums[:, 1],
        norm_sums[:, 2],
        norm_sums[:, 3],
    )


def solution(mesh):
    rows = P(ALL_AXES, None)
    vector = P(ALL_AXES)
    return jax.shard_map(
        body,
        mesh=mesh,
        in_specs=(rows, vector, rows, rows, rows, rows, vector, vector, vector, vector, rows),
        out_specs=(rows, rows, rows, rows, rows, rows, vector, vector, vector, vector),
        check_vma=False,
    )
```

```python
from functools import partial

import jax
import jax.numpy as jnp
from jax import lax
from jax.experimental import pallas as pl
from jax.experimental.pallas import tpu as pltpu
from jax.sharding import PartitionSpec as P

D = 768
HEADS = 12
HDIM = 64
BLOCK = 512
LANES = 128
EPSILON = 1e-05
MASKED = -1e30
ALL_AXES = ("seq", "head", "ctx")
BF16 = jnp.bfloat16
F32 = jnp.float32


def dot_on(left, right, left_dim, right_dim):
    return lax.dot_general(
        left, right, (((left_dim,), (right_dim,)), ((), ())), preferred_element_type=F32
    )


def norm_rows(values, gain_vec, bias_vec):
    row_mean = jnp.mean(values, axis=-1, keepdims=True)
    centered = values - row_mean
    variance = jnp.mean(centered * centered, axis=-1, keepdims=True)
    inv_rows = lax.rsqrt(variance + EPSILON)
    unit_rows = centered * inv_rows
    return (unit_rows * gain_vec + bias_vec, unit_rows, inv_rows)


def norm_back(grad_norm, unit_rows, inv_rows, gain_vec):
    scaled = grad_norm * gain_vec
    return inv_rows * (
        scaled
        - jnp.mean(scaled, axis=-1, keepdims=True)
        - unit_rows * jnp.mean(scaled * unit_rows, axis=-1, keepdims=True)
    )


def gelu_exact(values):
    return jax.nn.gelu(values, approximate=False)


def swap_head(value, mask):
    count = lax.axis_size("head")
    return lax.ppermute(value, "head", [(i, i ^ mask) for i in range(count)])


def ring_order(count):
    return [0, 1, 3, 2] if count == 4 else list(range(count))


def ring_pairs(count, step):
    order = ring_order(count)
    return [(order[i], order[(i + step) % count]) for i in range(count)]


def ring_send(value, step):
    return lax.ppermute(value, "ctx", ring_pairs(lax.axis_size("ctx"), step))


def plane_blocks(block):
    near = swap_head(block, 2)
    return [block, swap_head(block, 1), near, swap_head(near, 1)]


def split_three(values):
    high = values.astype(BF16)
    rest = values - high.astype(F32)
    middle = rest.astype(BF16)
    low = (rest - middle.astype(F32)).astype(BF16)
    return [high.astype(F32), middle.astype(F32), low.astype(F32)]


def key_marks(valid, lane):
    row = lax.broadcasted_iota(jnp.int32, (BLOCK, LANES), 0)
    real = row < valid
    marks = jnp.where((lane >= 64) & (lane < 67), 1.0, 0.0)
    marks = jnp.where((lane == 67) & jnp.logical_not(real), MASKED, marks)
    return jnp.where((lane == 68) & real, MASKED, marks)


def fill_keys(slots, kv_ref, valid_ref, keys_out, values_t=None, values_out=None, marks_first=0):
    lane = lax.broadcasted_iota(jnp.int32, (BLOCK, LANES), 1)

    def fill(slot, carry):
        rows = pl.ds(pl.multiple_of(slot * BLOCK, BLOCK), BLOCK)
        marks = key_marks(valid_ref[slot + marks_first], lane)
        for head in range(3):
            pair = kv_ref[rows, head * LANES : (head + 1) * LANES].astype(F32)
            keys_out[head, rows, :] = jnp.where(lane < 64, pair, marks).astype(BF16)
            if values_out is not None:
                ones = jnp.where(lane < 3, 1.0, 0.0)
                values_out[head, rows, :] = jnp.where(lane < 64, ones, pair).astype(BF16)
            if values_t is not None:
                turned = pair.T[64:128].astype(BF16)
                values_t[head, :, rows] = jnp.concatenate(
                    [turned, jnp.ones((16, BLOCK), BF16)], axis=0
                )
        return carry

    lax.fori_loop(0, slots, fill, 0)


def query_marks(valid, width):
    row = lax.broadcasted_iota(jnp.int32, (1, width), 1)
    real = jnp.where(row < valid, 1.0, 0.0)
    return [real, 1.0 - real]


def forward_kernel(plane, last, *refs):
    refs = list(refs)
    count_ref, list_ref, valid_ref = refs[:3]
    x_refs = refs[3:7]
    w_ref = refs[7]
    refs = refs[8:]
    if plane:
        q_ref, acc_in = refs.pop(0), refs.pop(0)
    if last:
        before, refs = refs[:plane], refs[plane:]
    kv_ref = refs.pop(0)
    if plane == 0:
        q_ref = refs.pop(0)
    if last:
        out_ref, exact_ref, lse_ref = refs.pop(0), refs.pop(0), refs.pop(0)
        keys, values_t, q_ext, acc, top, kv_copy, copied = refs
    else:
        acc = refs.pop(0)
        keys, values_t, q_ext = refs
    marks = w_ref[:, 3 * LANES : 4 * LANES].astype(F32).T
    gain, bias = marks[64:65], marks[65:66]
    for slot, x_ref in enumerate(x_refs):
        rows = slice(slot * BLOCK, (slot + 1) * BLOCK)
        normed, ignored, ignored_too = norm_rows(x_ref[...].astype(F32), gain, bias)
        normed = normed.astype(BF16)
        kv_ref[rows, :] = dot_on(normed, w_ref[:, : 3 * LANES], 1, 0).astype(BF16)
        if plane == 0:
            own = dot_on(normed, w_ref[:, 3 * LANES :], 1, 0) * HDIM ** (-0.5)
            q_ref[rows, :] = own.astype(BF16)
    fill_keys(4, kv_ref, valid_ref, keys, values_t=values_t, marks_first=4 * plane)
    if plane == 0:
        acc[...] = jnp.zeros_like(acc)
    else:
        acc[...] = acc_in[...]

    def set_queries(block):
        q_rows = pl.ds(pl.multiple_of(block * BLOCK, BLOCK), BLOCK)
        lane = lax.broadcasted_iota(jnp.int32, (BLOCK, LANES), 1)
        row = lax.broadcasted_iota(jnp.int32, (BLOCK, LANES), 0)
        real = row < valid_ref[block]
        marks = jnp.where((lane == 67) & real, 1.0, 0.0)
        marks = jnp.where((lane == 68) & jnp.logical_not(real), 1.0, marks)
        for head in range(3):
            own = q_ref[q_rows, head * LANES : (head + 1) * LANES].astype(F32)
            q_ext[head] = jnp.where(lane < 64, own, marks).astype(BF16)
        return q_rows

    def scores_of(slot, head):
        rows = pl.ds(pl.multiple_of(slot * BLOCK, BLOCK), BLOCK)
        return dot_on(keys[head, rows, :], q_ext[head], 1, 1)

    def over_queries(block, carry):
        q_rows = set_queries(block)

        def over_keys(item, carry_in):
            slot = list_ref[plane, block, item]
            rows = pl.ds(pl.multiple_of(slot * BLOCK, BLOCK), BLOCK)
            ready = [scores_of(slot, 0), scores_of(slot, 1)]
            for head in range(3):
                if head == 0:
                    ready.append(scores_of(slot, 2))
                weights = jnp.exp(ready.pop(0)).astype(BF16)
                acc[head, :, q_rows] += dot_on(values_t[head, :, rows], weights, 1, 0)
            return carry_in

        lax.fori_loop(0, count_ref[plane, block], over_keys, 0)
        return carry

    lax.fori_loop(0, 4, over_queries, 0)
    if not last:
        return
    sums = acc[:, 64:65, :]
    good = (sums >= 2.0**-60) & (sums <= 2.0**100)
    safe = jnp.min(jnp.where(good, 1.0, 0.0)) > 0.5
    top[...] = jnp.zeros_like(top)

    @pl.when(jnp.logical_not(safe))
    def _():
        top[...] = jnp.full_like(top, MASKED)
        acc[...] = jnp.zeros_like(acc)
        for which, source in enumerate(list(before) + [kv_ref]):
            if which < plane:
                move = pltpu.make_async_copy(source, kv_copy, copied)
                move.start()
                move.wait()
                source = kv_copy
            fill_keys(4, source, valid_ref, keys, values_t=values_t, marks_first=4 * which)

            def over_queries_again(block, carry, which=which):
                q_rows = set_queries(block)

                def with_max(item, carry_in):
                    slot = list_ref[which, block, item]
                    rows = pl.ds(pl.multiple_of(slot * BLOCK, BLOCK), BLOCK)
                    for head in range(3):
                        scores = scores_of(slot, head)
                        old = top[head, :, q_rows]
                        now = jnp.maximum(old, jnp.max(scores, axis=0, keepdims=True))
                        weights = jnp.exp(scores - now).astype(BF16)
                        top[head, :, q_rows] = now
                        acc[head, :, q_rows] = acc[head, :, q_rows] * jnp.exp(
                            old - now
                        ) + dot_on(values_t[head, :, rows], weights, 1, 0)
                    return carry_in

                lax.fori_loop(0, count_ref[which, block], with_max, 0)
                return carry

            lax.fori_loop(0, 4, over_queries_again, 0)

    for head in range(3):
        total = acc[head, 64:65, :]
        result = acc[head, 0:64, :] / total
        exact_ref[head] = result
        out_ref[head] = result.astype(BF16)
        lse_ref[head] = top[head] + jnp.log(total)


def attend_forward(plane, last, counts, lists, valid, blocks, weights, queries, acc, before):
    kv_rows = 4 * BLOCK
    smem = pl.BlockSpec(memory_space=pltpu.SMEM)
    vmem = pl.BlockSpec(memory_space=pltpu.VMEM)
    anywhere = pl.BlockSpec(memory_space=pl.ANY)
    packed = jax.ShapeDtypeStruct((kv_rows, 3 * LANES), BF16)
    sums = jax.ShapeDtypeStruct((3, 80, kv_rows), F32)
    inputs = [counts, lists, valid] + list(blocks) + [weights]
    inputs += [queries, acc] if plane else []
    outs = [packed] + ([packed] if plane == 0 else [])
    scratch = [
        pltpu.VMEM((3, kv_rows, LANES), BF16),
        pltpu.VMEM((3, 80, kv_rows), BF16),
        pltpu.VMEM((3, BLOCK, LANES), BF16),
    ]
    in_specs = [smem] * 3 + [vmem] * (len(inputs) - 3)
    if last:
        inputs += list(before)
        in_specs += [anywhere] * len(before)
        outs += [
            jax.ShapeDtypeStruct((3, HDIM, kv_rows), BF16),
            jax.ShapeDtypeStruct((3, HDIM, kv_rows), F32),
            jax.ShapeDtypeStruct((3, 1, kv_rows), F32),
        ]
        scratch += [
            pltpu.VMEM((3, 80, kv_rows), F32),
            pltpu.VMEM((3, 1, kv_rows), F32),
            pltpu.VMEM((kv_rows, 3 * LANES), BF16),
            pltpu.SemaphoreType.DMA,
        ]
    else:
        outs += [sums]
    return pl.pallas_call(
        partial(forward_kernel, plane, last),
        out_shape=tuple(outs),
        in_specs=in_specs,
        out_specs=(vmem,) * len(outs),
        scratch_shapes=scratch,
        compiler_params=pltpu.CompilerParams(vmem_limit_bytes=40 << 20),
        cost_estimate=pl.CostEstimate(
            flops=12 * 1000 * 1000 * 1000, bytes_accessed=10 << 20, transcendentals=7 << 20
        ),
        name="attend_forward",
    )(*inputs)


def backward_kernel(plane, carried, last, *refs):
    refs = list(refs)
    count_ref, list_ref, valid_ref = refs[:3]
    q_ref, kv_ref, out_ref, lse_ref, grad_ref, w_ref = refs[3:9]
    x_from, refs = refs[9:13], refs[13:]
    sum_in, refs = refs[0], refs[1:]
    if carried:
        dq_in, dw_in = refs[:2]
        refs = refs[2:]
    if last:
        keep_ref, send_ref, dw_out = refs[:3]
        dw_ref, dwq_ref, sum_ref = refs[-3:]
        dq_ref = None
        refs = refs[3:-3]
    else:
        keep_ref, send_ref, dw_ref, dq_ref, sum_ref = refs[:5]
        refs = refs[5:]
    keys, values, q_ext, g_ext, q_turned, dq_acc, dkv_acc, x_ref, moved = refs
    slots = 4
    moves = [
        pltpu.make_async_copy(x_from[i], x_ref.at[pl.ds(i * BLOCK, BLOCK)], moved.at[i])
        for i in range(slots)
    ]
    if carried:
        moves.append(pltpu.make_async_copy(dq_in, dq_acc, moved.at[4]))
    for move in moves:
        move.start()
    fill_keys(slots, kv_ref, valid_ref, keys, values_out=values, marks_first=4 * plane)
    lane = lax.broadcasted_iota(jnp.int32, (BLOCK, LANES), 1)

    def clear(slot, carry):
        rows = pl.ds(pl.multiple_of(slot * BLOCK, BLOCK), BLOCK)
        for head in range(3):
            dkv_acc[head, :, rows] = jnp.zeros((LANES, BLOCK), F32)
        return carry

    lax.fori_loop(0, slots, clear, 0)
    if carried:
        moves[4].wait()
    else:
        dq_acc[...] = jnp.zeros_like(dq_acc)

    def over_queries(block, carry):
        q_rows = pl.ds(pl.multiple_of(block * BLOCK, BLOCK), BLOCK)
        for head in range(3):
            lanes = slice(head * LANES, (head + 1) * LANES)
            turned = q_ref[q_rows, lanes].astype(F32).T[0:64]
            grad_t = grad_ref[head, :, q_rows].astype(F32)
            delta = jnp.sum(grad_t * out_ref[head, :, q_rows], axis=0, keepdims=True)
            marks = split_three(-lse_ref[head, :, q_rows]) + query_marks(valid_ref[block], BLOCK)
            blank = jnp.zeros((64 - len(marks), BLOCK), F32)
            q_turned[head] = turned.astype(BF16)
            q_ext[head] = jnp.concatenate([turned] + marks + [blank], axis=0).T.astype(BF16)
            minus = split_three(-delta)
            blank = jnp.zeros((64 - len(minus), BLOCK), F32)
            g_ext[head] = jnp.concatenate(minus + [blank, grad_t], axis=0).T.astype(BF16)

        def over_keys(item, carry_in):
            slot = list_ref[plane, block, item]
            rows = pl.ds(pl.multiple_of(slot * BLOCK, BLOCK), BLOCK)

            def products(head):
                return (
                    dot_on(q_ext[head], keys[head, rows, :], 1, 1),
                    dot_on(g_ext[head], values[head, rows, :], 1, 1),
                )

            ready = [products(0)]
            for head in range(3):
                lanes = slice(head * LANES, (head + 1) * LANES)
                if head < 2:
                    ready.append(products(head + 1))
                scores, grad_probs = ready.pop(0)
                probs = jnp.exp(scores)
                grad_scores = (probs * grad_probs).astype(BF16)
                dkv_acc[head, 64:128, rows] += dot_on(
                    grad_ref[head, :, q_rows], probs.astype(BF16), 1, 0
                )
                dkv_acc[head, 0:64, rows] += dot_on(q_turned[head], grad_scores, 1, 0)
                dq_acc[q_rows, lanes] += dot_on(grad_scores, keys[head, rows, :], 1, 0)
            return carry_in

        lax.fori_loop(0, count_ref[plane, block], over_keys, 0)
        return carry

    lax.fori_loop(0, 4, over_queries, 0)
    for move in moves[:4]:
        move.wait()
    if not last:
        leave = pltpu.make_async_copy(dq_acc, dq_ref, moved.at[4])
        leave.start()
    if carried:
        dw_ref[...] = dw_in[...]
    else:
        dw_ref[...] = jnp.zeros_like(dw_ref)
    sum_ref[...] = sum_in[...]
    if last:
        dwq_ref[...] = jnp.zeros_like(dwq_ref)
    marks = w_ref[:, 3 * LANES : 4 * LANES].astype(F32).T
    gain, bias = marks[64:65], marks[65:66]

    def finish(slot, carry):
        rows = pl.ds(pl.multiple_of(slot * BLOCK, BLOCK), BLOCK)
        pieces = []
        for head in range(3):
            pieces.append(dkv_acc[head, 0:64, rows])
            pieces.append(dkv_acc[head, 64:128, rows])
        turned = jnp.concatenate(pieces, axis=0)
        part = dot_on(turned.T.astype(BF16), w_ref[:, : 3 * LANES], 1, 1)
        values_now = x_ref[rows, :].astype(F32)
        normed, unit, ignored = norm_rows(values_now, gain, bias)
        normed = normed.astype(BF16)
        dw_ref[...] += dot_on(turned.astype(BF16), normed, 1, 0)
        if last:
            scaled = [
                jnp.where(lane < 64, dq_acc[rows, h * LANES : (h + 1) * LANES], 0.0)
                for h in range(3)
            ]
            scaled = jnp.concatenate(scaled, axis=1) * HDIM ** (-0.5)
            part = part + dot_on(scaled.astype(BF16), w_ref[:, 3 * LANES :], 1, 1)
            dwq_ref[...] += dot_on(scaled.T.astype(BF16), normed, 1, 0)
        sum_ref[0:1, :] += jnp.sum(part * unit, axis=0, keepdims=True)
        sum_ref[1:2, :] += jnp.sum(part, axis=0, keepdims=True)
        low = part.astype(BF16)

        @pl.when(slot % 2 == 0)
        def _():
            keep_ref[slot // 2] = low

        @pl.when(slot % 2 == 1)
        def _():
            send_ref[slot // 2] = low

        return carry

    lax.fori_loop(0, slots, finish, 0)
    if not last:
        leave.wait()
        return
    pieces = []
    for head in range(3):
        first = head * LANES
        pieces.append(dwq_ref[first : first + 64, :])
        pieces.append(dw_ref[first : first + LANES, :])
    pieces += [sum_ref[...], jnp.zeros((LANES - 8, D), F32)]
    dw_out[...] = jnp.concatenate(pieces, axis=0).T.astype(BF16)


def attend_backward(
    plane, counts, lists, valid, queries, key_vals, attended, lse, grads, weights, blocks, carry, last
):
    q_rows = queries.shape[0]
    smem = pl.BlockSpec(memory_space=pltpu.SMEM)
    vmem = pl.BlockSpec(memory_space=pltpu.VMEM)
    anywhere = pl.BlockSpec(memory_space=pl.ANY)
    carry = list(carry)
    half = jax.ShapeDtypeStruct((2, BLOCK, D), BF16)
    weight = jax.ShapeDtypeStruct((3 * LANES, D), F32)
    sums = jax.ShapeDtypeStruct((8, D), F32)
    if last:
        outs = (jax.ShapeDtypeStruct((D, 9 * HDIM + LANES), BF16),)
        spaces, kept = (vmem,), [weight, weight, sums]
    else:
        outs = (weight, jax.ShapeDtypeStruct((q_rows, 3 * LANES), F32), sums)
        spaces, kept = (vmem, anywhere, vmem), []
    result = pl.pallas_call(
        partial(backward_kernel, plane, len(carry) > 1, last),
        out_shape=(half, half) + outs,
        in_specs=[smem] * 3 + [vmem] * 6 + [anywhere] * 4 + [vmem, anywhere, vmem][: len(carry)],
        out_specs=(vmem, vmem) + spaces,
        scratch_shapes=[
            pltpu.VMEM((3, q_rows, LANES), BF16),
            pltpu.VMEM((3, q_rows, LANES), BF16),
            pltpu.VMEM((3, BLOCK, LANES), BF16),
            pltpu.VMEM((3, BLOCK, LANES), BF16),
            pltpu.VMEM((3, HDIM, BLOCK), BF16),
            pltpu.VMEM((q_rows, 3 * LANES), F32),
            pltpu.VMEM((3, LANES, q_rows), F32),
            pltpu.VMEM((q_rows, D), BF16),
            pltpu.SemaphoreType.DMA((5,)),
        ]
        + [pltpu.VMEM(k.shape, k.dtype) for k in kept],
        compiler_params=pltpu.CompilerParams(vmem_limit_bytes=34 << 20),
        cost_estimate=pl.CostEstimate(
            flops=25 * 1000 * 1000 * 1000, bytes_accessed=16 << 20, transcendentals=7 << 20
        ),
        name="attend_backward",
    )(
        counts, lists, valid, queries, key_vals, attended, lse, grads, weights, *blocks, *carry
    )
    return tuple(result) + (None,) * (5 - len(result))


def erf_of(values):
    clamped = jnp.clip(values, -4.0, 4.0)
    square = clamped * clamped
    top = jnp.float32(-2.72614225801306e-10)
    for term in (
        2.77068142495902e-08,
        -2.10102402082508e-06,
        -5.69250639462346e-05,
        -7.34990630326855e-04,
        -2.95459980854025e-03,
        -1.60960333262415e-02,
    ):
        top = top * square + term
    low = jnp.float32(-1.45660718464996e-05)
    for term in (
        -2.13374055278905e-04,
        -1.68282697438203e-03,
        -7.37332916720468e-03,
        -1.42647390514189e-02,
    ):
        low = low * square + term
    return clamped * top / low


def middle_kernel(pieces, pair, shard, *refs):
    refs = list(refs)
    start_ref, group_ref = refs[:2]
    merged_refs, refs = refs[2:6], refs[6:]
    token_ref, cot_ref, mark_ref = refs[:3]
    piece_refs, refs = refs[3 : 3 + pieces], refs[3 + pieces :]
    output_ref, grad_y_ref, grad_z_ref, h_two_ref, hidden_ref, grad_up_ref = refs[:6]
    part_refs, sum_ref, norm_ref, refs = refs[6:10], refs[10], refs[11], refs[12:]
    w_out, w_up, w_down, moved = refs
    parts = []
    for piece in piece_refs:
        parts += [(piece, base) for base in range(0, piece.shape[0], 9 * pair)]

    def moves_of(weight):
        moves = []
        for i, (piece, base) in enumerate(parts):
            if weight < 5:
                source = piece.at[pl.ds(base + weight * pair, pair)]
                rows = pl.ds(pl.multiple_of(start_ref[i] * shard, pair), pair)
                target = w_out.at[rows] if weight == 0 else w_up.at[weight - 1, rows]
            else:
                source = piece.at[pl.ds(base + 5 * pair, 4 * pair)]
                rows = pl.ds(pl.multiple_of(start_ref[i] * 4 * shard, 4 * pair), 4 * pair)
                target = w_down.at[rows]
            moves.append(pltpu.make_async_copy(source, target, moved.at[weight, i]))
        return moves

    arriving = [moves_of(weight) for weight in range(6)]
    for weight in (0, 1, 5, 2, 3, 4):
        for move in arriving[weight]:
            move.start()
    norm_ref[...] = mark_ref[...].astype(F32).T[64:72]
    for move in arriving[0]:
        move.wait()
    y_one = token_ref[...].astype(F32)
    group = D // 4
    for j, merged_ref in enumerate(merged_refs):
        rows = pl.ds(pl.multiple_of(group_ref[j] * group, group), group)
        turned = merged_ref[...].astype(F32).T.astype(BF16)
        y_one = y_one + dot_on(turned, w_out[rows, :], 1, 0)
    grad_y_ref[...] = y_one
    gain, bias = norm_ref[2:3, :], norm_ref[3:4, :]
    normed, unit, inv_rows = norm_rows(y_one, gain, bias)
    h_two_ref[...] = normed.astype(BF16)

    output_sum = jnp.zeros((BLOCK, D), F32)
    grad_sum = jnp.zeros((BLOCK, D), F32)
    for j in range(4):
        for move in arriving[1 + j]:
            move.wait()
        if j == 0:
            for move in arriving[5]:
                move.wait()
        columns = slice(j * D, (j + 1) * D)
        up = dot_on(h_two_ref[...], w_up[j], 1, 0)
        grad_hidden = dot_on(cot_ref[...], w_down[columns, :], 1, 1)
        normal = 0.5 + 0.5 * erf_of(up * 0.7071067811865476)
        density = jnp.exp(-0.5 * up * up) * 0.3989422804014327
        hidden = (up * normal).astype(BF16)
        grad_up = (grad_hidden * (normal + up * density)).astype(BF16)
        hidden_ref[:, columns] = hidden
        grad_up_ref[:, columns] = grad_up
        output_sum = output_sum + dot_on(hidden, w_down[columns, :], 1, 0)
        grad_sum = grad_sum + dot_on(grad_up, w_up[j], 1, 1)
    y_one = grad_y_ref[...]
    output_ref[...] = (y_one + output_sum).astype(BF16)
    normed, unit, inv_rows = norm_rows(y_one, gain, bias)
    sum_ref[...] = jnp.zeros_like(sum_ref)
    sum_ref[2:3, :] = jnp.sum(grad_sum * unit, axis=0, keepdims=True)
    sum_ref[3:4, :] = jnp.sum(grad_sum, axis=0, keepdims=True)
    grad_y = cot_ref[...].astype(F32) + norm_back(grad_sum, unit, inv_rows, gain)
    grad_y_ref[...] = grad_y
    grad_z = grad_y.astype(BF16)
    grad_z_ref[...] = grad_z
    for j, part_ref in enumerate(part_refs):
        rows = pl.ds(pl.multiple_of(group_ref[j] * group, group), group)
        part_ref[...] = dot_on(w_out[rows, :], grad_z, 1, 1).astype(BF16)


def middle(starts, groups, merged, tokens, cotangent, marks, pieces, shard):
    smem = pl.BlockSpec(memory_space=pltpu.SMEM)
    vmem = pl.BlockSpec(memory_space=pltpu.VMEM)
    anywhere = pl.BlockSpec(memory_space=pl.ANY)
    rows = tokens.shape[0]
    number = starts.shape[0]
    pair = sum(piece.shape[0] for piece in pieces) // (9 * number)

    def shape(columns, dtype, height=rows):
        return jax.ShapeDtypeStruct((height, columns), dtype)

    return pl.pallas_call(
        partial(middle_kernel, len(pieces), pair, shard),
        out_shape=(
            shape(D, BF16),
            shape(D, F32),
            shape(D, BF16),
            shape(D, BF16),
            shape(4 * D, BF16),
            shape(4 * D, BF16),
        )
        + (shape(rows, BF16, D // 4),) * 4
        + (shape(D, F32, 8),) * 2,
        in_specs=[smem, smem] + [vmem] * 7 + [anywhere] * len(pieces),
        out_specs=(vmem,) * 12,
        scratch_shapes=[
            pltpu.VMEM((D, D), BF16),
            pltpu.VMEM((4, D, D), BF16),
            pltpu.VMEM((4 * D, D), BF16),
            pltpu.SemaphoreType.DMA((6, number)),
        ],
        compiler_params=pltpu.CompilerParams(vmem_limit_bytes=58 << 20),
        cost_estimate=pl.CostEstimate(
            flops=12 * 1000 * 1000 * 1000, bytes_accessed=24 << 20, transcendentals=3 << 20
        ),
        name="middle",
    )(starts, groups, *merged, tokens, cotangent, marks, *pieces)


def put_halves(core, rows, keep_ref, give_ref, place, columns, values):
    for i in range(values.shape[0] // (2 * rows)):
        for which in range(2):
            first = (2 * i + which) * rows
            piece = values[first : first + rows].astype(BF16)
            start = place + i * rows
            if not isinstance(start, int):
                start = pl.multiple_of(start, rows)
            target = pl.ds(start, rows)

            @pl.when(core == which)
            def _(piece=piece, target=target):
                keep_ref[target, columns] = piece

            @pl.when(core != which)
            def _(piece=piece, target=target):
                give_ref[target, columns] = piece


def down_kernel(line, core_ref, hidden_ref, cot_ref, keep_ref, give_ref):
    block = dot_on(hidden_ref[...], cot_ref[...], 0, 0)
    put_halves(core_ref[0], 4 * line, keep_ref, give_ref, 0, slice(0, D), block)


def wide_kernel(line, *refs):
    core_ref, group_ref, h_two_ref, grad_up_ref, grad_z_ref = refs[:5]
    merged_refs, (keep_ref, give_ref) = refs[5:9], refs[9:]
    core, step = core_ref[0], pl.program_id(0)
    columns = slice(0, D)

    @pl.when(step < 4)
    def _():
        block = dot_on(h_two_ref[...], grad_up_ref[...], 0, 0)
        put_halves(core, line, keep_ref, give_ref, 0, columns, block)

    @pl.when(step == 4)
    def _():
        group = D // 4
        for j, merged_ref in enumerate(merged_refs):
            block = dot_on(merged_ref[...], grad_z_ref[...], 1, 0)
            place = group_ref[j] * (group // 2)
            put_halves(core, line, keep_ref, give_ref, place, columns, block)


def halves_of_down(line, core, hidden, cotangent):
    rows = cotangent.shape[0]
    half = pl.BlockSpec((D // 2, D), lambda j: (j, 0))
    return pl.pallas_call(
        partial(down_kernel, line),
        grid=(4,),
        out_shape=(jax.ShapeDtypeStruct((2 * D, D), BF16),) * 2,
        in_specs=[
            pl.BlockSpec(memory_space=pltpu.SMEM),
            pl.BlockSpec((rows, D), lambda j: (0, j)),
            pl.BlockSpec((rows, D), lambda j: (0, 0)),
        ],
        out_specs=(half, half),
        compiler_params=pltpu.CompilerParams(vmem_limit_bytes=54 << 20),
        cost_estimate=pl.CostEstimate(
            flops=3 * 10**9, bytes_accessed=10 << 20, transcendentals=0
        ),
        name="grad_down",
    )(core, hidden, cotangent)


def halves_of_wide(line, core, groups, h_two, grad_up, grad_z, merged):
    rows = h_two.shape[0]
    smem = pl.BlockSpec(memory_space=pltpu.SMEM)
    whole = pl.BlockSpec((rows, D), lambda j: (0, 0))
    half = pl.BlockSpec((D // 2, D), lambda j: (0, j))
    return pl.pallas_call(
        partial(wide_kernel, line),
        grid=(5,),
        out_shape=(jax.ShapeDtypeStruct((D // 2, 5 * D), BF16),) * 2,
        in_specs=[smem, smem, whole]
        + [pl.BlockSpec((rows, D), lambda j: (0, jnp.minimum(j, 3))), whole]
        + [pl.BlockSpec((D // 4, rows), lambda j: (0, 0))] * 4,
        out_specs=(half, half),
        compiler_params=pltpu.CompilerParams(vmem_limit_bytes=54 << 20),
        cost_estimate=pl.CostEstimate(
            flops=4 * 10**9, bytes_accessed=12 << 20, transcendentals=0
        ),
        name="grad_wide",
    )(core, groups, h_two, grad_up, grad_z, *merged)


def scene_lists(same):
    number = same.shape[-1]
    slot = jnp.arange(number)
    counts = jnp.sum(same, axis=-1).astype(jnp.int32)
    earlier = slot[None, :] < slot[:, None]
    place = jnp.sum(same[:, :, None, :] & earlier, axis=-1)
    hits = same[:, :, None, :] & (place[:, :, None, :] == slot[:, None])
    lists = jnp.sum(jnp.where(hits, slot, 0), axis=-1)
    return counts, lists.astype(jnp.int32)


def halve(value, axis, bit, send):
    give = lax.dynamic_index_in_dim(value, 1 - bit, axis, keepdims=False)
    return value, send(give)


def settle(pending, axis, bit):
    value, taken = pending
    keep = lax.dynamic_index_in_dim(value, bit, axis, keepdims=False)
    return (keep.astype(F32) + taken.astype(F32)).astype(BF16)


def ring_sources(count):
    order = ring_order(count)
    table = [[order[(order.index(c) - r) % count] for r in range(count)] for c in range(count)]
    return jnp.array(table, jnp.int32)[lax.axis_index("ctx")]


def give_over_seq(value):
    count = lax.axis_size("seq")
    me = lax.axis_index("seq")
    while True:
        count //= 2
        pairs = [(i, i ^ count) for i in range(lax.axis_size("seq"))]
        pending = halve(
            value.reshape((2, count) + value.shape[1:]),
            0,
            (me // count) % 2,
            lambda give: lax.ppermute(give, "seq", pairs),
        )
        if count == 1:
            return pending
        value = settle(pending, 0, (me // count) % 2)


def sum_over_seq(pending):
    value = settle(pending, 0, lax.axis_index("seq") % 2)
    return value.reshape(value.shape[1:])


def gather_bit(value, bit, send):
    other = send(value)
    first = jnp.where(bit == 0, value, other)
    return jnp.concatenate([first, jnp.where(bit == 0, other, value)], axis=0)


def gather_seq(value):
    count, reach = lax.axis_size("seq"), 1
    me = lax.axis_index("seq")
    while reach < count:
        pairs = [(i, i ^ reach) for i in range(count)]
        value = gather_bit(
            value[None], (me // reach) % 2, lambda v: lax.ppermute(v, "seq", pairs)
        ).reshape((2 * reach,) + value.shape[1:])
        reach *= 2
    return value


def swap_seq(value, mask=1):
    return lax.ppermute(value, "seq", [(i, i ^ mask) for i in range(lax.axis_size("seq"))])


def in_order(blocks, sources, shard):
    count = len(blocks)
    full = jnp.zeros((count,) + blocks[0].shape, BF16)
    for r in range(count):
        full = lax.dynamic_update_index_in_dim(full, blocks[r], sources[r], 0)
    cuts = []
    for half in range(2):
        part = full[half * (count // 2) : (half + 1) * (count // 2)]
        cut = [part[:, i * shard : (i + 1) * shard] for i in range(5)] + [part[:, 5 * shard :]]
        cuts += [c.reshape(-1, D) for c in cut]
    return jnp.concatenate(cuts, axis=0)


def join_halves(pieces, places, number):
    def woven(first, second):
        rows = first.shape[0] // 9
        cuts = [i * rows for i in range(1, 6)]
        both = zip(jnp.split(first, cuts), jnp.split(second, cuts))
        return jnp.concatenate([part for pair in both for part in pair], axis=0)

    joined, kept = [], []
    for base in range(0, len(pieces), number):
        for i in (0, 1):
            joined.append(woven(*jnp.split(pieces[base + i], 2)))
            kept.append(((0,),) + places[base + i][1:])
        for i in (2, 4):
            joined.append(woven(pieces[base + i], pieces[base + i + 1]))
            kept.append(((0,),) + places[base + i][1:])
    return joined, kept


def gather_ctx(value):
    count = lax.axis_size("ctx")
    sources = ring_sources(count)
    whole = jnp.zeros((count,) + value.shape, value.dtype)
    whole = lax.dynamic_update_index_in_dim(whole, value, sources[0], 0)
    for r in range(1, count):
        whole = lax.dynamic_update_index_in_dim(whole, ring_send(value, r), sources[r], 0)
    return whole


def sum_over_core(pending):
    keep, taken = pending
    return (keep.astype(F32) + taken.astype(F32)).astype(BF16)


def give_over_x(value):
    return halve(value, 0, lax.axis_index("head") // 2, lambda give: swap_head(give, 2))


def sum_over_x(pending):
    return settle(pending, 0, lax.axis_index("head") // 2)


def send_term(value, r):
    source = ring_sources(lax.axis_size("ctx"))[r]
    return ring_send(lax.dynamic_index_in_dim(value, source, 0, keepdims=False), -r)


def sum_terms(value, terms):
    source = ring_sources(lax.axis_size("ctx"))[0]
    total = lax.dynamic_index_in_dim(value, source, 0, keepdims=False).astype(F32)
    for term in terms:
        total = total + term.astype(F32)
    return total


def sum_over_ctx(value):
    count = lax.axis_size("ctx")
    sources = ring_sources(count)
    total = lax.dynamic_index_in_dim(value, sources[0], 0, keepdims=False).astype(F32)
    for r in range(1, count):
        give = lax.dynamic_index_in_dim(value, sources[r], 0, keepdims=False)
        total = total + ring_send(give, -r).astype(F32)
    return total


def tie(*values):
    return lax.optimization_barrier(values)


def body(
    tokens,
    segment_ids,
    w_qkv,
    w_out,
    w_up,
    w_down,
    gain_one,
    bias_one,
    gain_two,
    bias_two,
    cotangent,
):
    heads_ax = lax.axis_size("head")
    ctx_ax = lax.axis_size("ctx")
    seq_ax = lax.axis_size("seq")
    me_head = lax.axis_index("head")
    tok_rows = tokens.shape[0]
    group = D // heads_ax
    shard = w_qkv.shape[0]

    order = [me_head ^ j for j in range(heads_ax)]
    sources = ring_sources(ctx_ax)
    wide = 3 * group + LANES

    padding = tok_rows - jnp.sum(segment_ids >= 0)
    about = jnp.stack([segment_ids[0], padding // 16, padding % 16]).astype(BF16)
    extra = jnp.stack([gain_one, bias_one, gain_two, bias_two], axis=1)
    extra = jnp.concatenate([extra, jnp.broadcast_to(about[None, :], (shard, 3))], axis=1)
    extra = jnp.pad(extra, ((0, 0), (0, HDIM - 7)))
    by_head = w_qkv.reshape(shard, heads_ax, 3, 3, HDIM)
    beside = jnp.zeros((shard, heads_ax, 2, HDIM), BF16)
    beside = jnp.concatenate(
        [jnp.broadcast_to(extra[:, None, None], (shard, heads_ax, 1, HDIM)), beside], axis=2
    )
    packed = jnp.concatenate(
        [
            by_head[:, :, :, 1:].reshape(shard, heads_ax, 3 * LANES),
            jnp.stack([by_head[:, :, :, 0], beside], axis=3).reshape(shard, heads_ax, 3 * LANES),
        ],
        axis=2,
    )
    packed = jnp.swapaxes(packed, 0, 1)
    got = tie(
        *[lax.dynamic_index_in_dim(packed, o, 0, keepdims=False) for o in order]
    )
    got = [swap_head(piece, j) if j else piece for j, piece in enumerate(got)]
    w_rest = jnp.concatenate(
        [w_out] + [w_up[:, i * D : (i + 1) * D] for i in range(4)] + [w_down], axis=0
    )
    w_rest, *got = tie(w_rest, *got)
    mine = jnp.zeros((heads_ax, shard, D), BF16)
    for j in range(heads_ax):
        mine = lax.dynamic_update_index_in_dim(mine, got[j], order[j], 0)
    ring_mine = [mine] + [ring_send(mine, i) for i in range(1, ctx_ax)]

    rest = [w_rest]
    near, ahead, behind = swap_head(tokens, 2), ring_send(tokens, 1), ring_send(w_rest, 1)
    near, ahead, behind, *ring_mine = tie(near, ahead, behind, *ring_mine)
    rest.append(behind)
    packed = jnp.zeros((ctx_ax,) + mine.shape, BF16)
    for r in range(ctx_ax):
        packed = lax.dynamic_update_index_in_dim(packed, ring_mine[r], sources[r], 0)

    def weights_here(packed):
        weights = jnp.swapaxes(gather_seq(packed[None]), 1, 2).reshape(D, D)
        first = 3 * LANES + HDIM + 4
        about_all = weights[::shard, first : first + 3].astype(jnp.int32)
        about_all = lax.dynamic_index_in_dim(
            about_all.reshape(seq_ax, heads_ax, ctx_ax, 3),
            lax.axis_index("seq"),
            0,
            keepdims=False,
        )
        pick_head = jnp.stack(order)[:, None] == jnp.arange(heads_ax)[None, :]
        pick_ctx = sources[:, None] == jnp.arange(ctx_ax)[None, :]
        pick = pick_ctx[:, None, None, :] & pick_head[None, :, :, None]
        slot_about = jnp.sum(jnp.where(pick[..., None], about_all[None, None], 0), axis=(2, 3))
        slot_ids = slot_about[:, :, 0]
        slot_valid = (tok_rows - (slot_about[:, :, 1] * 16 + slot_about[:, :, 2])).reshape(-1)
        counts, lists = scene_lists(slot_ids[0][None, :, None] == slot_ids[:, None, :])
        return weights, counts, lists, slot_valid

    planes, key_vals, queries, acc = [], [], None, None
    block = tokens
    ready = None
    for r in range(ctx_ax + 1):
        if r < ctx_ax:
            travelers = [swap_head(block, 1), swap_head(near, 1)]
        else:
            travelers = []
        if r + 1 < ctx_ax:
            travelers.append(swap_head(ahead, 2))
        if r + 2 < ctx_ax:
            travelers.append(ring_send(ahead, 1))
            travelers.append(ring_send(rest[-1], 1))
        count = len(travelers)
        if r == ctx_ax - 2:
            line = in_order(rest, sources, shard)
            middle_row = line.shape[0] // 2
            travelers += [swap_head(line[:middle_row], 2), swap_seq(line)]
        if r == ctx_ax - 1:
            travelers += [swap_head(line[middle_row:], 2), swap_seq(x_first), swap_head(line, 1)]
        if r == ctx_ax:
            travelers += [swap_seq(x_second), swap_head(y_line, 1), swap_head(x_first, 1)]
        results = []
        if ready is not None:
            results = list(
                attend_forward(
                    r - 1,
                    r == ctx_ax,
                    counts,
                    lists,
                    slot_valid,
                    ready,
                    weights,
                    queries,
                    acc,
                    key_vals,
                )
            )
        tied = list(tie(*travelers, *results))
        extra, tied = tied[count : len(travelers)], tied[:count] + tied[len(travelers) :]
        if r == 0:
            weights, counts, lists, slot_valid = weights_here(packed)
        if r == ctx_ax - 2:
            x_first, y_line = extra
        if r == ctx_ax - 1:
            x_second, xy_first, core_line = extra
        if r == ctx_ax:
            xy_second, core_y, core_x_first = extra
            results = tied
            break
        planes.append([block, tied.pop(0), near, tied.pop(0)])
        ready = planes[-1]
        if r + 1 < ctx_ax:
            block, near = ahead, tied.pop(0)
        if r + 2 < ctx_ax:
            ahead = tied.pop(0)
            rest.append(tied.pop(0))
        if results:
            key_vals.append(tied.pop(0))
            if r == 1:
                queries = tied.pop(0)
            acc = tied.pop(0)
    key_vals.append(results[0])
    attended, exact, lse = results[1:]
    owns = [line, y_line, x_first, x_second, xy_first, xy_second]
    cores = [core_line, core_y, core_x_first]
    cores += [swap_head(v, 1) for v in (x_second, xy_first, xy_second)]
    offs = [((0, 1), 0, 0), ((0, 1), 0, 1), ((0,), 1, 0), ((1,), 1, 0), ((0,), 1, 1), ((1,), 1, 1)]
    me_x, me_core, me_seq = me_head // 2, me_head % 2, lax.axis_index("seq")
    pieces, places = [], []
    for core, arrays in enumerate((owns, cores)):
        for array, (halves, x, y) in zip(arrays, offs):
            pieces.append(array)
            places.append((halves, (me_x ^ x) * 2 + (me_core ^ core), y))
    reach = 2
    while reach < seq_ax:
        pieces += [swap_seq(array, reach) for array in pieces]
        places += [(halves, place, y ^ reach) for halves, place, y in places]
        reach *= 2
    if (ctx_ax // 2 * shard) % 8:
        pieces, places = join_halves(pieces, places, len(offs))
    starts = [
        ((me_seq ^ y) * heads_ax + place) * ctx_ax + half * (ctx_ax // 2)
        for halves, place, y in places
        for half in halves
    ]
    starts = jnp.stack(starts).astype(jnp.int32)

    merged = []
    for j in range(heads_ax):
        part = attended[:, :, j * tok_rows : (j + 1) * tok_rows].reshape(group, tok_rows)
        merged.append(swap_head(part, j) if j else part)

    marks = weights[:, 3 * LANES : 4 * LANES]
    groups = jnp.stack(order).astype(jnp.int32)
    output, grad_y_one, grad_z, h_two, hidden, grad_up, *rest_out = middle(
        starts, groups, merged, tokens, cotangent, marks, pieces, shard
    )
    grad_merged, sums_two, norms = rest_out[:4], rest_out[4], rest_out[5]

    grad_parts = [swap_head(p, j) if j else p for j, p in enumerate(grad_merged)]
    line = ctx_ax * shard
    outer = (seq_ax, 2, ctx_ax)
    me_bit = (me_head % 2)[None].astype(jnp.int32)
    keep, give = halves_of_down(line, me_bit, hidden, cotangent)
    shape = outer + (4 * shard, D)
    down_sum = (keep.reshape(shape), swap_head(give.reshape(shape), 1))
    h_two, keep, *_ = tie(h_two, down_sum[0])
    keep, give = halves_of_wide(line, me_bit, groups, h_two, grad_up, grad_z, merged)
    shape = outer + (shard, 5 * D)
    keep, give, *tied = tie(keep, give, *down_sum, *grad_parts)
    down_sum, grad_parts = sum_over_core(tied[:2]), tied[2:]
    grad_local = jnp.concatenate(grad_parts, axis=1).reshape(3, HDIM, heads_ax * tok_rows)
    wide_sum = (keep.reshape(shape), swap_head(give.reshape(shape), 1))
    down_sum = give_over_seq(down_sum)

    carry, traveling, near_half, far_half = (sums_two,), None, None, None
    for r in reversed(range(ctx_ax)):
        step = ctx_ax - 1 - r
        travelers = []
        if step >= 1:
            travelers.append(swap_head(far_half, 2))
        if step >= 2:
            travelers.append(ring_send(traveling, -1))
        count = len(travelers)
        if step == 0:
            travelers += [down_sum, wide_sum]
        if step == 1:
            travelers += [give_over_x(down_sum), give_over_seq(wide_sum)]
        if step == 2:
            travelers += [give_over_x(wide_sum)] + [send_term(down_sum, i) for i in (1, 2, 3)]
        if step == 3:
            travelers += [send_term(wide_sum, i) for i in (1, 2, 3)]
        keep, give, dw, fourth, sums = attend_backward(
            r,
            counts,
            lists,
            slot_valid,
            queries,
            key_vals[r],
            exact,
            lse,
            grad_local,
            weights,
            planes[r],
            carry,
            r == 0,
        )
        if r == 0:
            keep, give, dw, *travelers = tie(keep, give, dw, *travelers)
        else:
            keep, give, fourth, dw, sums, *travelers = tie(
                keep, give, fourth, dw, sums, *travelers
            )
        extra = travelers[count:]
        if step >= 1:
            moved = near_half.astype(F32) + travelers[0].astype(F32)
            if step >= 2:
                moved = moved + travelers[1].astype(F32)
            traveling = moved.astype(BF16)
        if step == 0:
            down_sum = sum_over_seq(extra[0])
            wide_sum = sum_over_core(extra[1])
        if step == 1:
            down_sum, wide_sum = sum_over_x(extra[0]), sum_over_seq(extra[1])
        if step == 2:
            wide_sum, down_terms = sum_over_x(extra[0]), list(extra[1:])
        if step == 3:
            wide_terms = list(extra)
        taken = swap_head(give, 1)
        near_half = (keep[0].astype(F32) + taken[0].astype(F32)).astype(BF16)
        far_half = (keep[1].astype(F32) + taken[1].astype(F32)).astype(BF16)
        if r:
            tied = [near_half, far_half, fourth, dw, sums, down_sum, wide_sum]
            tied += [traveling] if step >= 1 else []
            near_half, far_half, fourth, dw, sums, down_sum, wide_sum, *tied = tie(*tied)
            if step >= 1:
                traveling = tied[0]
        carry = (sums, fourth, dw)
    near_half, far_half, traveling = tie(near_half, far_half, traveling)
    dw_mine = give_over_seq(dw.reshape(seq_ax, heads_ax, ctx_ax, shard, wide))
    taken, carried, *dw_mine = tie(
        swap_head(far_half, 2), ring_send(traveling, -1), *dw_mine
    )
    dw_mine = sum_over_seq(dw_mine)
    grad_h_one = near_half.astype(F32) + taken.astype(F32) + carried.astype(F32)
    down_sum, wide_sum = sum_terms(down_sum, down_terms), sum_terms(wide_sum, wide_terms)
    up_sum, out_sum = wide_sum[:, : 4 * D], wide_sum[:, 4 * D :]
    dw_mine = sum_over_ctx(jnp.swapaxes(dw_mine, 0, 1)).astype(BF16)
    groups = []
    for j in range(heads_ax):
        part = lax.dynamic_index_in_dim(dw_mine, order[j], 0, keepdims=False)
        groups.append(swap_head(part, j) if j else part)
    groups = jnp.stack(groups)
    groups = jnp.stack(
        [lax.dynamic_index_in_dim(groups, o, 0, keepdims=False) for o in order]
    ).astype(F32)
    grad_w_qkv = jnp.swapaxes(groups[:, :, : 3 * group], 0, 1).reshape(shard, 3 * D)
    norm_sums = jnp.sum(groups[:, :, 3 * group : 3 * group + 4], axis=0)

    g_one = norms[0]
    ignored, unit_one, inv_one = norm_rows(tokens.astype(F32), g_one, norms[1])
    grad_tokens = (grad_y_one + norm_back(grad_h_one, unit_one, inv_one, g_one)).astype(BF16)
    return (
        output,
        grad_tokens,
        grad_w_qkv,
        out_sum,
        up_sum,
        down_sum,
        norm_sums[:, 0],
        norm_sums[:, 1],
        norm_sums[:, 2],
        norm_sums[:, 3],
    )


def solution(mesh):
    rows = P(ALL_AXES, None)
    vector = P(ALL_AXES)
    return jax.shard_map(
        body,
        mesh=mesh,
        in_specs=(rows, vector, rows, rows, rows, rows, vector, vector, vector, vector, rows),
        out_specs=(rows, rows, rows, rows, rows, rows, vector, vector, vector, vector),
        check_vma=False,
    )
```

```python
from functools import partial

import jax
import jax.numpy as jnp
from jax import lax
from jax.experimental import pallas as pl
from jax.experimental.pallas import tpu as pltpu
from jax.sharding import PartitionSpec as P

D = 768
HEADS = 12
HDIM = 64
BLOCK = 512
LANES = 128
EPSILON = 1e-05
MASKED = -1e30
ALL_AXES = ("seq", "head", "ctx")
BF16 = jnp.bfloat16
F32 = jnp.float32


def dot_on(left, right, left_dim, right_dim):
    return lax.dot_general(
        left, right, (((left_dim,), (right_dim,)), ((), ())), preferred_element_type=F32
    )


def norm_rows(values, gain_vec, bias_vec):
    row_mean = jnp.mean(values, axis=-1, keepdims=True)
    centered = values - row_mean
    variance = jnp.mean(centered * centered, axis=-1, keepdims=True)
    inv_rows = lax.rsqrt(variance + EPSILON)
    unit_rows = centered * inv_rows
    return (unit_rows * gain_vec + bias_vec, unit_rows, inv_rows)


def norm_back(grad_norm, unit_rows, inv_rows, gain_vec):
    scaled = grad_norm * gain_vec
    return inv_rows * (
        scaled
        - jnp.mean(scaled, axis=-1, keepdims=True)
        - unit_rows * jnp.mean(scaled * unit_rows, axis=-1, keepdims=True)
    )


def gelu_exact(values):
    return jax.nn.gelu(values, approximate=False)


def swap_head(value, mask):
    count = lax.axis_size("head")
    return lax.ppermute(value, "head", [(i, i ^ mask) for i in range(count)])


def ring_order(count):
    return [0, 1, 3, 2] if count == 4 else list(range(count))


def ring_pairs(count, step):
    order = ring_order(count)
    return [(order[i], order[(i + step) % count]) for i in range(count)]


def ring_send(value, step):
    return lax.ppermute(value, "ctx", ring_pairs(lax.axis_size("ctx"), step))


def plane_blocks(block):
    near = swap_head(block, 2)
    return [block, swap_head(block, 1), near, swap_head(near, 1)]


def split_three(values):
    high = values.astype(BF16)
    rest = values - high.astype(F32)
    middle = rest.astype(BF16)
    low = (rest - middle.astype(F32)).astype(BF16)
    return [high.astype(F32), middle.astype(F32), low.astype(F32)]


def key_marks(valid, lane):
    row = lax.broadcasted_iota(jnp.int32, (BLOCK, LANES), 0)
    real = row < valid
    marks = jnp.where((lane >= 64) & (lane < 67), 1.0, 0.0)
    marks = jnp.where((lane == 67) & jnp.logical_not(real), MASKED, marks)
    return jnp.where((lane == 68) & real, MASKED, marks)


def fill_keys(slots, kv_ref, valid_ref, keys_out, values_t=None, values_out=None, marks_first=0):
    lane = lax.broadcasted_iota(jnp.int32, (BLOCK, LANES), 1)

    def fill(slot, carry):
        rows = pl.ds(pl.multiple_of(slot * BLOCK, BLOCK), BLOCK)
        marks = key_marks(valid_ref[slot + marks_first], lane)
        for head in range(3):
            pair = kv_ref[rows, head * LANES : (head + 1) * LANES].astype(F32)
            keys_out[head, rows, :] = jnp.where(lane < 64, pair, marks).astype(BF16)
            if values_out is not None:
                ones = jnp.where(lane < 3, 1.0, 0.0)
                values_out[head, rows, :] = jnp.where(lane < 64, ones, pair).astype(BF16)
            if values_t is not None:
                turned = pair.T[64:128].astype(BF16)
                values_t[head, :, rows] = jnp.concatenate(
                    [turned, jnp.ones((16, BLOCK), BF16)], axis=0
                )
        return carry

    lax.fori_loop(0, slots, fill, 0)


def query_marks(valid, width):
    row = lax.broadcasted_iota(jnp.int32, (1, width), 1)
    real = jnp.where(row < valid, 1.0, 0.0)
    return [real, 1.0 - real]


def forward_kernel(plane, last, *refs):
    refs = list(refs)
    count_ref, list_ref, valid_ref = refs[:3]
    x_refs = refs[3:7]
    w_ref = refs[7]
    refs = refs[8:]
    if plane:
        q_ref, acc_in = refs.pop(0), refs.pop(0)
    if last:
        before, refs = refs[:plane], refs[plane:]
    kv_ref = refs.pop(0)
    if plane == 0:
        q_ref = refs.pop(0)
    if last:
        out_ref, exact_ref, lse_ref = refs.pop(0), refs.pop(0), refs.pop(0)
        keys, values_t, q_ext, acc, top, kv_copy, copied = refs
    else:
        acc = refs.pop(0)
        keys, values_t, q_ext = refs
    marks = w_ref[:, 3 * LANES : 4 * LANES].astype(F32).T
    gain, bias = marks[64:65], marks[65:66]
    for slot, x_ref in enumerate(x_refs):
        rows = slice(slot * BLOCK, (slot + 1) * BLOCK)
        normed, ignored, ignored_too = norm_rows(x_ref[...].astype(F32), gain, bias)
        normed = normed.astype(BF16)
        kv_ref[rows, :] = dot_on(normed, w_ref[:, : 3 * LANES], 1, 0).astype(BF16)
        if plane == 0:
            own = dot_on(normed, w_ref[:, 3 * LANES :], 1, 0) * HDIM ** (-0.5)
            q_ref[rows, :] = own.astype(BF16)
    fill_keys(4, kv_ref, valid_ref, keys, values_t=values_t, marks_first=4 * plane)
    if plane == 0:
        acc[...] = jnp.zeros_like(acc)
    else:
        acc[...] = acc_in[...]

    def set_queries(block):
        q_rows = pl.ds(pl.multiple_of(block * BLOCK, BLOCK), BLOCK)
        lane = lax.broadcasted_iota(jnp.int32, (BLOCK, LANES), 1)
        row = lax.broadcasted_iota(jnp.int32, (BLOCK, LANES), 0)
        real = row < valid_ref[block]
        marks = jnp.where((lane == 67) & real, 1.0, 0.0)
        marks = jnp.where((lane == 68) & jnp.logical_not(real), 1.0, marks)
        for head in range(3):
            own = q_ref[q_rows, head * LANES : (head + 1) * LANES].astype(F32)
            q_ext[head] = jnp.where(lane < 64, own, marks).astype(BF16)
        return q_rows

    def scores_of(slot, head):
        rows = pl.ds(pl.multiple_of(slot * BLOCK, BLOCK), BLOCK)
        return dot_on(keys[head, rows, :], q_ext[head], 1, 1)

    def over_queries(block, carry):
        q_rows = set_queries(block)

        def over_keys(item, carry_in):
            slot = list_ref[plane, block, item]
            rows = pl.ds(pl.multiple_of(slot * BLOCK, BLOCK), BLOCK)
            ready = [scores_of(slot, 0), scores_of(slot, 1)]
            for head in range(3):
                if head == 0:
                    ready.append(scores_of(slot, 2))
                weights = jnp.exp(ready.pop(0)).astype(BF16)
                acc[head, :, q_rows] += dot_on(values_t[head, :, rows], weights, 1, 0)
            return carry_in

        lax.fori_loop(0, count_ref[plane, block], over_keys, 0)
        return carry

    lax.fori_loop(0, 4, over_queries, 0)
    if not last:
        return
    sums = acc[:, 64:65, :]
    good = (sums >= 2.0**-60) & (sums <= 2.0**100)
    safe = jnp.min(jnp.where(good, 1.0, 0.0)) > 0.5
    top[...] = jnp.zeros_like(top)

    @pl.when(jnp.logical_not(safe))
    def _():
        top[...] = jnp.full_like(top, MASKED)
        acc[...] = jnp.zeros_like(acc)
        for which, source in enumerate(list(before) + [kv_ref]):
            if which < plane:
                move = pltpu.make_async_copy(source, kv_copy, copied)
                move.start()
                move.wait()
                source = kv_copy
            fill_keys(4, source, valid_ref, keys, values_t=values_t, marks_first=4 * which)

            def over_queries_again(block, carry, which=which):
                q_rows = set_queries(block)

                def with_max(item, carry_in):
                    slot = list_ref[which, block, item]
                    rows = pl.ds(pl.multiple_of(slot * BLOCK, BLOCK), BLOCK)
                    for head in range(3):
                        scores = scores_of(slot, head)
                        old = top[head, :, q_rows]
                        now = jnp.maximum(old, jnp.max(scores, axis=0, keepdims=True))
                        weights = jnp.exp(scores - now).astype(BF16)
                        top[head, :, q_rows] = now
                        acc[head, :, q_rows] = acc[head, :, q_rows] * jnp.exp(
                            old - now
                        ) + dot_on(values_t[head, :, rows], weights, 1, 0)
                    return carry_in

                lax.fori_loop(0, count_ref[which, block], with_max, 0)
                return carry

            lax.fori_loop(0, 4, over_queries_again, 0)

    for head in range(3):
        total = acc[head, 64:65, :]
        result = acc[head, 0:64, :] / total
        exact_ref[head] = result
        out_ref[head] = result.astype(BF16)
        lse_ref[head] = top[head] + jnp.log(total)


def attend_forward(plane, last, counts, lists, valid, blocks, weights, queries, acc, before):
    kv_rows = 4 * BLOCK
    smem = pl.BlockSpec(memory_space=pltpu.SMEM)
    vmem = pl.BlockSpec(memory_space=pltpu.VMEM)
    anywhere = pl.BlockSpec(memory_space=pl.ANY)
    packed = jax.ShapeDtypeStruct((kv_rows, 3 * LANES), BF16)
    sums = jax.ShapeDtypeStruct((3, 80, kv_rows), F32)
    inputs = [counts, lists, valid] + list(blocks) + [weights]
    inputs += [queries, acc] if plane else []
    outs = [packed] + ([packed] if plane == 0 else [])
    scratch = [
        pltpu.VMEM((3, kv_rows, LANES), BF16),
        pltpu.VMEM((3, 80, kv_rows), BF16),
        pltpu.VMEM((3, BLOCK, LANES), BF16),
    ]
    in_specs = [smem] * 3 + [vmem] * (len(inputs) - 3)
    if last:
        inputs += list(before)
        in_specs += [anywhere] * len(before)
        outs += [
            jax.ShapeDtypeStruct((3, HDIM, kv_rows), BF16),
            jax.ShapeDtypeStruct((3, HDIM, kv_rows), F32),
            jax.ShapeDtypeStruct((3, 1, kv_rows), F32),
        ]
        scratch += [
            pltpu.VMEM((3, 80, kv_rows), F32),
            pltpu.VMEM((3, 1, kv_rows), F32),
            pltpu.VMEM((kv_rows, 3 * LANES), BF16),
            pltpu.SemaphoreType.DMA,
        ]
    else:
        outs += [sums]
    return pl.pallas_call(
        partial(forward_kernel, plane, last),
        out_shape=tuple(outs),
        in_specs=in_specs,
        out_specs=(vmem,) * len(outs),
        scratch_shapes=scratch,
        compiler_params=pltpu.CompilerParams(vmem_limit_bytes=34 << 20),
        cost_estimate=pl.CostEstimate(
            flops=12 * 1000 * 1000 * 1000, bytes_accessed=10 << 20, transcendentals=7 << 20
        ),
        name="attend_forward",
    )(*inputs)


def backward_kernel(plane, carried, last, *refs):
    refs = list(refs)
    count_ref, list_ref, valid_ref = refs[:3]
    q_ref, kv_ref, out_ref, lse_ref, grad_ref, w_ref = refs[3:9]
    x_from, refs = refs[9:13], refs[13:]
    sum_in, refs = refs[0], refs[1:]
    if carried:
        dq_in, dw_in = refs[:2]
        refs = refs[2:]
    if last:
        keep_ref, send_ref, dw_out = refs[:3]
        dw_ref, dwq_ref, sum_ref = refs[-3:]
        dq_ref = None
        refs = refs[3:-3]
    else:
        keep_ref, send_ref, dw_ref, dq_ref, sum_ref = refs[:5]
        refs = refs[5:]
    keys, values, q_ext, g_ext, q_turned, dq_acc, dkv_acc, x_ref, moved = refs
    slots = 4
    moves = [
        pltpu.make_async_copy(x_from[i], x_ref.at[pl.ds(i * BLOCK, BLOCK)], moved.at[i])
        for i in range(slots)
    ]
    if carried:
        moves.append(pltpu.make_async_copy(dq_in, dq_acc, moved.at[4]))
    for move in moves:
        move.start()
    fill_keys(slots, kv_ref, valid_ref, keys, values_out=values, marks_first=4 * plane)
    lane = lax.broadcasted_iota(jnp.int32, (BLOCK, LANES), 1)

    def clear(slot, carry):
        rows = pl.ds(pl.multiple_of(slot * BLOCK, BLOCK), BLOCK)
        for head in range(3):
            dkv_acc[head, :, rows] = jnp.zeros((LANES, BLOCK), F32)
        return carry

    lax.fori_loop(0, slots, clear, 0)
    if carried:
        moves[4].wait()
    else:
        dq_acc[...] = jnp.zeros_like(dq_acc)

    def over_queries(block, carry):
        q_rows = pl.ds(pl.multiple_of(block * BLOCK, BLOCK), BLOCK)
        for head in range(3):
            lanes = slice(head * LANES, (head + 1) * LANES)
            turned = q_ref[q_rows, lanes].astype(F32).T[0:64]
            grad_t = grad_ref[head, :, q_rows].astype(F32)
            delta = jnp.sum(grad_t * out_ref[head, :, q_rows], axis=0, keepdims=True)
            marks = split_three(-lse_ref[head, :, q_rows]) + query_marks(valid_ref[block], BLOCK)
            blank = jnp.zeros((64 - len(marks), BLOCK), F32)
            q_turned[head] = turned.astype(BF16)
            q_ext[head] = jnp.concatenate([turned] + marks + [blank], axis=0).T.astype(BF16)
            minus = split_three(-delta)
            blank = jnp.zeros((64 - len(minus), BLOCK), F32)
            g_ext[head] = jnp.concatenate(minus + [blank, grad_t], axis=0).T.astype(BF16)

        def over_keys(item, carry_in):
            slot = list_ref[plane, block, item]
            rows = pl.ds(pl.multiple_of(slot * BLOCK, BLOCK), BLOCK)

            def products(head):
                return (
                    dot_on(q_ext[head], keys[head, rows, :], 1, 1),
                    dot_on(g_ext[head], values[head, rows, :], 1, 1),
                )

            ready = [products(0)]
            for head in range(3):
                lanes = slice(head * LANES, (head + 1) * LANES)
                if head < 2:
                    ready.append(products(head + 1))
                scores, grad_probs = ready.pop(0)
                probs = jnp.exp(scores)
                grad_scores = (probs * grad_probs).astype(BF16)
                dkv_acc[head, 64:128, rows] += dot_on(
                    grad_ref[head, :, q_rows], probs.astype(BF16), 1, 0
                )
                dkv_acc[head, 0:64, rows] += dot_on(q_turned[head], grad_scores, 1, 0)
                dq_acc[q_rows, lanes] += dot_on(grad_scores, keys[head, rows, :], 1, 0)
            return carry_in

        lax.fori_loop(0, count_ref[plane, block], over_keys, 0)
        return carry

    lax.fori_loop(0, 4, over_queries, 0)
    for move in moves[:4]:
        move.wait()
    if not last:
        leave = pltpu.make_async_copy(dq_acc, dq_ref, moved.at[4])
        leave.start()
    if carried:
        dw_ref[...] = dw_in[...]
    else:
        dw_ref[...] = jnp.zeros_like(dw_ref)
    sum_ref[...] = sum_in[...]
    if last:
        dwq_ref[...] = jnp.zeros_like(dwq_ref)
    marks = w_ref[:, 3 * LANES : 4 * LANES].astype(F32).T
    gain, bias = marks[64:65], marks[65:66]

    def finish(slot, carry):
        rows = pl.ds(pl.multiple_of(slot * BLOCK, BLOCK), BLOCK)
        pieces = []
        for head in range(3):
            pieces.append(dkv_acc[head, 0:64, rows])
            pieces.append(dkv_acc[head, 64:128, rows])
        turned = jnp.concatenate(pieces, axis=0)
        part = dot_on(turned.T.astype(BF16), w_ref[:, : 3 * LANES], 1, 1)
        values_now = x_ref[rows, :].astype(F32)
        normed, unit, ignored = norm_rows(values_now, gain, bias)
        normed = normed.astype(BF16)
        dw_ref[...] += dot_on(turned.astype(BF16), normed, 1, 0)
        if last:
            scaled = [
                jnp.where(lane < 64, dq_acc[rows, h * LANES : (h + 1) * LANES], 0.0)
                for h in range(3)
            ]
            scaled = jnp.concatenate(scaled, axis=1) * HDIM ** (-0.5)
            part = part + dot_on(scaled.astype(BF16), w_ref[:, 3 * LANES :], 1, 1)
            dwq_ref[...] += dot_on(scaled.T.astype(BF16), normed, 1, 0)
        sum_ref[0:1, :] += jnp.sum(part * unit, axis=0, keepdims=True)
        sum_ref[1:2, :] += jnp.sum(part, axis=0, keepdims=True)
        low = part.astype(BF16)

        @pl.when(slot % 2 == 0)
        def _():
            keep_ref[slot // 2] = low

        @pl.when(slot % 2 == 1)
        def _():
            send_ref[slot // 2] = low

        return carry

    lax.fori_loop(0, slots, finish, 0)
    if not last:
        leave.wait()
        return
    pieces = []
    for head in range(3):
        first = head * LANES
        pieces.append(dwq_ref[first : first + 64, :])
        pieces.append(dw_ref[first : first + LANES, :])
    pieces += [sum_ref[...], jnp.zeros((LANES - 8, D), F32)]
    dw_out[...] = jnp.concatenate(pieces, axis=0).T.astype(BF16)


def attend_backward(
    plane, counts, lists, valid, queries, key_vals, attended, lse, grads, weights, blocks, carry, last
):
    q_rows = queries.shape[0]
    smem = pl.BlockSpec(memory_space=pltpu.SMEM)
    vmem = pl.BlockSpec(memory_space=pltpu.VMEM)
    anywhere = pl.BlockSpec(memory_space=pl.ANY)
    carry = list(carry)
    half = jax.ShapeDtypeStruct((2, BLOCK, D), BF16)
    weight = jax.ShapeDtypeStruct((3 * LANES, D), F32)
    sums = jax.ShapeDtypeStruct((8, D), F32)
    if last:
        outs = (jax.ShapeDtypeStruct((D, 9 * HDIM + LANES), BF16),)
        spaces, kept = (vmem,), [weight, weight, sums]
    else:
        outs = (weight, jax.ShapeDtypeStruct((q_rows, 3 * LANES), F32), sums)
        spaces, kept = (vmem, anywhere, vmem), []
    result = pl.pallas_call(
        partial(backward_kernel, plane, len(carry) > 1, last),
        out_shape=(half, half) + outs,
        in_specs=[smem] * 3 + [vmem] * 6 + [anywhere] * 4 + [vmem, anywhere, vmem][: len(carry)],
        out_specs=(vmem, vmem) + spaces,
        scratch_shapes=[
            pltpu.VMEM((3, q_rows, LANES), BF16),
            pltpu.VMEM((3, q_rows, LANES), BF16),
            pltpu.VMEM((3, BLOCK, LANES), BF16),
            pltpu.VMEM((3, BLOCK, LANES), BF16),
            pltpu.VMEM((3, HDIM, BLOCK), BF16),
            pltpu.VMEM((q_rows, 3 * LANES), F32),
            pltpu.VMEM((3, LANES, q_rows), F32),
            pltpu.VMEM((q_rows, D), BF16),
            pltpu.SemaphoreType.DMA((5,)),
        ]
        + [pltpu.VMEM(k.shape, k.dtype) for k in kept],
        compiler_params=pltpu.CompilerParams(vmem_limit_bytes=32 << 20),
        cost_estimate=pl.CostEstimate(
            flops=25 * 1000 * 1000 * 1000, bytes_accessed=16 << 20, transcendentals=7 << 20
        ),
        name="attend_backward",
    )(
        counts, lists, valid, queries, key_vals, attended, lse, grads, weights, *blocks, *carry
    )
    return tuple(result) + (None,) * (5 - len(result))


def erf_of(values):
    clamped = jnp.clip(values, -4.0, 4.0)
    square = clamped * clamped
    top = jnp.float32(-2.72614225801306e-10)
    for term in (
        2.77068142495902e-08,
        -2.10102402082508e-06,
        -5.69250639462346e-05,
        -7.34990630326855e-04,
        -2.95459980854025e-03,
        -1.60960333262415e-02,
    ):
        top = top * square + term
    low = jnp.float32(-1.45660718464996e-05)
    for term in (
        -2.13374055278905e-04,
        -1.68282697438203e-03,
        -7.37332916720468e-03,
        -1.42647390514189e-02,
    ):
        low = low * square + term
    return clamped * top / low


def middle_kernel(pieces, pair, shard, *refs):
    refs = list(refs)
    start_ref, group_ref = refs[:2]
    merged_refs, refs = refs[2:6], refs[6:]
    token_ref, cot_ref, mark_ref = refs[:3]
    piece_refs, refs = refs[3 : 3 + pieces], refs[3 + pieces :]
    output_ref, grad_y_ref, grad_z_ref, h_two_ref, hidden_ref, grad_up_ref = refs[:6]
    part_refs, sum_ref, norm_ref, refs = refs[6:10], refs[10], refs[11], refs[12:]
    w_out, w_up, w_down, moved = refs
    parts = []
    for piece in piece_refs:
        parts += [(piece, base) for base in range(0, piece.shape[0], 9 * pair)]

    def moves_of(weight):
        moves = []
        for i, (piece, base) in enumerate(parts):
            if weight < 5:
                source = piece.at[pl.ds(base + weight * pair, pair)]
                rows = pl.ds(pl.multiple_of(start_ref[i] * shard, pair), pair)
                target = w_out.at[rows] if weight == 0 else w_up.at[weight - 1, rows]
            else:
                source = piece.at[pl.ds(base + 5 * pair, 4 * pair)]
                rows = pl.ds(pl.multiple_of(start_ref[i] * 4 * shard, 4 * pair), 4 * pair)
                target = w_down.at[rows]
            moves.append(pltpu.make_async_copy(source, target, moved.at[weight, i]))
        return moves

    arriving = [moves_of(weight) for weight in range(6)]
    for weight in (0, 1, 5, 2, 3, 4):
        for move in arriving[weight]:
            move.start()
    norm_ref[...] = mark_ref[...].astype(F32).T[64:72]
    for move in arriving[0]:
        move.wait()
    y_one = token_ref[...].astype(F32)
    group = D // 4
    for j, merged_ref in enumerate(merged_refs):
        rows = pl.ds(pl.multiple_of(group_ref[j] * group, group), group)
        turned = merged_ref[...].astype(F32).T.astype(BF16)
        y_one = y_one + dot_on(turned, w_out[rows, :], 1, 0)
    grad_y_ref[...] = y_one
    gain, bias = norm_ref[2:3, :], norm_ref[3:4, :]
    normed, unit, inv_rows = norm_rows(y_one, gain, bias)
    h_two_ref[...] = normed.astype(BF16)

    output_sum = jnp.zeros((BLOCK, D), F32)
    grad_sum = jnp.zeros((BLOCK, D), F32)
    for j in range(4):
        for move in arriving[1 + j]:
            move.wait()
        if j == 0:
            for move in arriving[5]:
                move.wait()
        columns = slice(j * D, (j + 1) * D)
        up = dot_on(h_two_ref[...], w_up[j], 1, 0)
        grad_hidden = dot_on(cot_ref[...], w_down[columns, :], 1, 1)
        normal = 0.5 + 0.5 * erf_of(up * 0.7071067811865476)
        density = jnp.exp(-0.5 * up * up) * 0.3989422804014327
        hidden = (up * normal).astype(BF16)
        grad_up = (grad_hidden * (normal + up * density)).astype(BF16)
        hidden_ref[:, columns] = hidden
        grad_up_ref[:, columns] = grad_up
        output_sum = output_sum + dot_on(hidden, w_down[columns, :], 1, 0)
        grad_sum = grad_sum + dot_on(grad_up, w_up[j], 1, 1)
    y_one = grad_y_ref[...]
    output_ref[...] = (y_one + output_sum).astype(BF16)
    normed, unit, inv_rows = norm_rows(y_one, gain, bias)
    sum_ref[...] = jnp.zeros_like(sum_ref)
    sum_ref[2:3, :] = jnp.sum(grad_sum * unit, axis=0, keepdims=True)
    sum_ref[3:4, :] = jnp.sum(grad_sum, axis=0, keepdims=True)
    grad_y = cot_ref[...].astype(F32) + norm_back(grad_sum, unit, inv_rows, gain)
    grad_y_ref[...] = grad_y
    grad_z = grad_y.astype(BF16)
    grad_z_ref[...] = grad_z
    for j, part_ref in enumerate(part_refs):
        rows = pl.ds(pl.multiple_of(group_ref[j] * group, group), group)
        part_ref[...] = dot_on(w_out[rows, :], grad_z, 1, 1).astype(BF16)


def middle(starts, groups, merged, tokens, cotangent, marks, pieces, shard):
    smem = pl.BlockSpec(memory_space=pltpu.SMEM)
    vmem = pl.BlockSpec(memory_space=pltpu.VMEM)
    anywhere = pl.BlockSpec(memory_space=pl.ANY)
    rows = tokens.shape[0]
    number = starts.shape[0]
    pair = sum(piece.shape[0] for piece in pieces) // (9 * number)

    def shape(columns, dtype, height=rows):
        return jax.ShapeDtypeStruct((height, columns), dtype)

    return pl.pallas_call(
        partial(middle_kernel, len(pieces), pair, shard),
        out_shape=(
            shape(D, BF16),
            shape(D, F32),
            shape(D, BF16),
            shape(D, BF16),
            shape(4 * D, BF16),
            shape(4 * D, BF16),
        )
        + (shape(rows, BF16, D // 4),) * 4
        + (shape(D, F32, 8),) * 2,
        in_specs=[smem, smem] + [vmem] * 7 + [anywhere] * len(pieces),
        out_specs=(vmem,) * 12,
        scratch_shapes=[
            pltpu.VMEM((D, D), BF16),
            pltpu.VMEM((4, D, D), BF16),
            pltpu.VMEM((4 * D, D), BF16),
            pltpu.SemaphoreType.DMA((6, number)),
        ],
        compiler_params=pltpu.CompilerParams(vmem_limit_bytes=59 << 20),
        cost_estimate=pl.CostEstimate(
            flops=12 * 1000 * 1000 * 1000, bytes_accessed=24 << 20, transcendentals=3 << 20
        ),
        name="middle",
    )(starts, groups, *merged, tokens, cotangent, marks, *pieces)


def put_halves(core, rows, keep_ref, give_ref, place, columns, values):
    for i in range(values.shape[0] // (2 * rows)):
        for which in range(2):
            first = (2 * i + which) * rows
            piece = values[first : first + rows].astype(BF16)
            start = place + i * rows
            if not isinstance(start, int):
                start = pl.multiple_of(start, rows)
            target = pl.ds(start, rows)

            @pl.when(core == which)
            def _(piece=piece, target=target):
                keep_ref[target, columns] = piece

            @pl.when(core != which)
            def _(piece=piece, target=target):
                give_ref[target, columns] = piece


def down_kernel(line, core_ref, hidden_ref, cot_ref, keep_ref, give_ref):
    block = dot_on(hidden_ref[...], cot_ref[...], 0, 0)
    put_halves(core_ref[0], 4 * line, keep_ref, give_ref, 0, slice(0, D), block)


def wide_kernel(line, *refs):
    core_ref, group_ref, h_two_ref, grad_up_ref, grad_z_ref = refs[:5]
    merged_refs, (keep_ref, give_ref) = refs[5:9], refs[9:]
    core, step = core_ref[0], pl.program_id(0)
    columns = slice(0, D)

    @pl.when(step < 4)
    def _():
        block = dot_on(h_two_ref[...], grad_up_ref[...], 0, 0)
        put_halves(core, line, keep_ref, give_ref, 0, columns, block)

    @pl.when(step == 4)
    def _():
        group = D // 4
        for j, merged_ref in enumerate(merged_refs):
            block = dot_on(merged_ref[...], grad_z_ref[...], 1, 0)
            place = group_ref[j] * (group // 2)
            put_halves(core, line, keep_ref, give_ref, place, columns, block)


def halves_of_down(line, core, hidden, cotangent):
    rows = cotangent.shape[0]
    half = pl.BlockSpec((D // 2, D), lambda j: (j, 0))
    return pl.pallas_call(
        partial(down_kernel, line),
        grid=(4,),
        out_shape=(jax.ShapeDtypeStruct((2 * D, D), BF16),) * 2,
        in_specs=[
            pl.BlockSpec(memory_space=pltpu.SMEM),
            pl.BlockSpec((rows, D), lambda j: (0, j)),
            pl.BlockSpec((rows, D), lambda j: (0, 0)),
        ],
        out_specs=(half, half),
        compiler_params=pltpu.CompilerParams(vmem_limit_bytes=56 << 20),
        cost_estimate=pl.CostEstimate(
            flops=3 * 10**9, bytes_accessed=10 << 20, transcendentals=0
        ),
        name="grad_down",
    )(core, hidden, cotangent)


def halves_of_wide(line, core, groups, h_two, grad_up, grad_z, merged):
    rows = h_two.shape[0]
    smem = pl.BlockSpec(memory_space=pltpu.SMEM)
    whole = pl.BlockSpec((rows, D), lambda j: (0, 0))
    half = pl.BlockSpec((D // 2, D), lambda j: (0, j))
    return pl.pallas_call(
        partial(wide_kernel, line),
        grid=(5,),
        out_shape=(jax.ShapeDtypeStruct((D // 2, 5 * D), BF16),) * 2,
        in_specs=[smem, smem, whole]
        + [pl.BlockSpec((rows, D), lambda j: (0, jnp.minimum(j, 3))), whole]
        + [pl.BlockSpec((D // 4, rows), lambda j: (0, 0))] * 4,
        out_specs=(half, half),
        compiler_params=pltpu.CompilerParams(vmem_limit_bytes=56 << 20),
        cost_estimate=pl.CostEstimate(
            flops=4 * 10**9, bytes_accessed=12 << 20, transcendentals=0
        ),
        name="grad_wide",
    )(core, groups, h_two, grad_up, grad_z, *merged)


def scene_lists(same):
    number = same.shape[-1]
    slot = jnp.arange(number)
    counts = jnp.sum(same, axis=-1).astype(jnp.int32)
    earlier = slot[None, :] < slot[:, None]
    place = jnp.sum(same[:, :, None, :] & earlier, axis=-1)
    hits = same[:, :, None, :] & (place[:, :, None, :] == slot[:, None])
    lists = jnp.sum(jnp.where(hits, slot, 0), axis=-1)
    return counts, lists.astype(jnp.int32)


def halve(value, axis, bit, send):
    give = lax.dynamic_index_in_dim(value, 1 - bit, axis, keepdims=False)
    return value, send(give)


def settle(pending, axis, bit):
    value, taken = pending
    keep = lax.dynamic_index_in_dim(value, bit, axis, keepdims=False)
    return (keep.astype(F32) + taken.astype(F32)).astype(BF16)


def ring_sources(count):
    order = ring_order(count)
    table = [[order[(order.index(c) - r) % count] for r in range(count)] for c in range(count)]
    return jnp.array(table, jnp.int32)[lax.axis_index("ctx")]


def give_over_seq(value):
    count = lax.axis_size("seq")
    me = lax.axis_index("seq")
    while True:
        count //= 2
        pairs = [(i, i ^ count) for i in range(lax.axis_size("seq"))]
        pending = halve(
            value.reshape((2, count) + value.shape[1:]),
            0,
            (me // count) % 2,
            lambda give: lax.ppermute(give, "seq", pairs),
        )
        if count == 1:
            return pending
        value = settle(pending, 0, (me // count) % 2)


def sum_over_seq(pending):
    value = settle(pending, 0, lax.axis_index("seq") % 2)
    return value.reshape(value.shape[1:])


def gather_bit(value, bit, send):
    other = send(value)
    first = jnp.where(bit == 0, value, other)
    return jnp.concatenate([first, jnp.where(bit == 0, other, value)], axis=0)


def gather_seq(value):
    count, reach = lax.axis_size("seq"), 1
    me = lax.axis_index("seq")
    while reach < count:
        pairs = [(i, i ^ reach) for i in range(count)]
        value = gather_bit(
            value[None], (me // reach) % 2, lambda v: lax.ppermute(v, "seq", pairs)
        ).reshape((2 * reach,) + value.shape[1:])
        reach *= 2
    return value


def swap_seq(value, mask=1):
    return lax.ppermute(value, "seq", [(i, i ^ mask) for i in range(lax.axis_size("seq"))])


def in_order(blocks, sources, shard):
    count = len(blocks)
    full = jnp.zeros((count,) + blocks[0].shape, BF16)
    for r in range(count):
        full = lax.dynamic_update_index_in_dim(full, blocks[r], sources[r], 0)
    cuts = []
    for half in range(2):
        part = full[half * (count // 2) : (half + 1) * (count // 2)]
        cut = [part[:, i * shard : (i + 1) * shard] for i in range(5)] + [part[:, 5 * shard :]]
        cuts += [c.reshape(-1, D) for c in cut]
    return jnp.concatenate(cuts, axis=0)


def join_halves(pieces, places, number):
    def woven(first, second):
        rows = first.shape[0] // 9
        cuts = [i * rows for i in range(1, 6)]
        both = zip(jnp.split(first, cuts), jnp.split(second, cuts))
        return jnp.concatenate([part for pair in both for part in pair], axis=0)

    joined, kept = [], []
    for base in range(0, len(pieces), number):
        for i in (0, 1):
            joined.append(woven(*jnp.split(pieces[base + i], 2)))
            kept.append(((0,),) + places[base + i][1:])
        for i in (2, 4):
            joined.append(woven(pieces[base + i], pieces[base + i + 1]))
            kept.append(((0,),) + places[base + i][1:])
    return joined, kept


def gather_ctx(value):
    count = lax.axis_size("ctx")
    sources = ring_sources(count)
    whole = jnp.zeros((count,) + value.shape, value.dtype)
    whole = lax.dynamic_update_index_in_dim(whole, value, sources[0], 0)
    for r in range(1, count):
        whole = lax.dynamic_update_index_in_dim(whole, ring_send(value, r), sources[r], 0)
    return whole


def sum_over_core(pending):
    keep, taken = pending
    return (keep.astype(F32) + taken.astype(F32)).astype(BF16)


def give_over_x(value):
    return halve(value, 0, lax.axis_index("head") // 2, lambda give: swap_head(give, 2))


def sum_over_x(pending):
    return settle(pending, 0, lax.axis_index("head") // 2)


def send_term(value, r):
    source = ring_sources(lax.axis_size("ctx"))[r]
    return ring_send(lax.dynamic_index_in_dim(value, source, 0, keepdims=False), -r)


def sum_terms(value, terms):
    source = ring_sources(lax.axis_size("ctx"))[0]
    total = lax.dynamic_index_in_dim(value, source, 0, keepdims=False).astype(F32)
    for term in terms:
        total = total + term.astype(F32)
    return total


def sum_over_ctx(value):
    count = lax.axis_size("ctx")
    sources = ring_sources(count)
    total = lax.dynamic_index_in_dim(value, sources[0], 0, keepdims=False).astype(F32)
    for r in range(1, count):
        give = lax.dynamic_index_in_dim(value, sources[r], 0, keepdims=False)
        total = total + ring_send(give, -r).astype(F32)
    return total


def tie(*values):
    return lax.optimization_barrier(values)


def body(
    tokens,
    segment_ids,
    w_qkv,
    w_out,
    w_up,
    w_down,
    gain_one,
    bias_one,
    gain_two,
    bias_two,
    cotangent,
):
    heads_ax = lax.axis_size("head")
    ctx_ax = lax.axis_size("ctx")
    seq_ax = lax.axis_size("seq")
    me_head = lax.axis_index("head")
    tok_rows = tokens.shape[0]
    group = D // heads_ax
    shard = w_qkv.shape[0]

    order = [me_head ^ j for j in range(heads_ax)]
    sources = ring_sources(ctx_ax)
    wide = 3 * group + LANES

    padding = tok_rows - jnp.sum(segment_ids >= 0)
    about = jnp.stack([segment_ids[0], padding // 16, padding % 16]).astype(BF16)
    extra = jnp.stack([gain_one, bias_one, gain_two, bias_two], axis=1)
    extra = jnp.concatenate([extra, jnp.broadcast_to(about[None, :], (shard, 3))], axis=1)
    extra = jnp.pad(extra, ((0, 0), (0, HDIM - 7)))
    by_head = w_qkv.reshape(shard, heads_ax, 3, 3, HDIM)
    beside = jnp.zeros((shard, heads_ax, 2, HDIM), BF16)
    beside = jnp.concatenate(
        [jnp.broadcast_to(extra[:, None, None], (shard, heads_ax, 1, HDIM)), beside], axis=2
    )
    packed = jnp.concatenate(
        [
            by_head[:, :, :, 1:].reshape(shard, heads_ax, 3 * LANES),
            jnp.stack([by_head[:, :, :, 0], beside], axis=3).reshape(shard, heads_ax, 3 * LANES),
        ],
        axis=2,
    )
    packed = jnp.swapaxes(packed, 0, 1)
    got = tie(
        *[lax.dynamic_index_in_dim(packed, o, 0, keepdims=False) for o in order]
    )
    got = [swap_head(piece, j) if j else piece for j, piece in enumerate(got)]
    w_rest = jnp.concatenate(
        [w_out] + [w_up[:, i * D : (i + 1) * D] for i in range(4)] + [w_down], axis=0
    )
    w_rest, *got = tie(w_rest, *got)
    mine = jnp.zeros((heads_ax, shard, D), BF16)
    for j in range(heads_ax):
        mine = lax.dynamic_update_index_in_dim(mine, got[j], order[j], 0)
    ring_mine = [mine] + [ring_send(mine, i) for i in range(1, ctx_ax)]

    rest = [w_rest]
    near, ahead, behind = swap_head(tokens, 2), ring_send(tokens, 1), ring_send(w_rest, 1)
    near, ahead, behind, *ring_mine = tie(near, ahead, behind, *ring_mine)
    rest.append(behind)
    packed = jnp.zeros((ctx_ax,) + mine.shape, BF16)
    for r in range(ctx_ax):
        packed = lax.dynamic_update_index_in_dim(packed, ring_mine[r], sources[r], 0)

    def weights_here(packed):
        weights = jnp.swapaxes(gather_seq(packed[None]), 1, 2).reshape(D, D)
        first = 3 * LANES + HDIM + 4
        about_all = weights[::shard, first : first + 3].astype(jnp.int32)
        about_all = lax.dynamic_index_in_dim(
            about_all.reshape(seq_ax, heads_ax, ctx_ax, 3),
            lax.axis_index("seq"),
            0,
            keepdims=False,
        )
        pick_head = jnp.stack(order)[:, None] == jnp.arange(heads_ax)[None, :]
        pick_ctx = sources[:, None] == jnp.arange(ctx_ax)[None, :]
        pick = pick_ctx[:, None, None, :] & pick_head[None, :, :, None]
        slot_about = jnp.sum(jnp.where(pick[..., None], about_all[None, None], 0), axis=(2, 3))
        slot_ids = slot_about[:, :, 0]
        slot_valid = (tok_rows - (slot_about[:, :, 1] * 16 + slot_about[:, :, 2])).reshape(-1)
        counts, lists = scene_lists(slot_ids[0][None, :, None] == slot_ids[:, None, :])
        return weights, counts, lists, slot_valid

    planes, key_vals, queries, acc = [], [], None, None
    block = tokens
    ready = None
    for r in range(ctx_ax + 1):
        if r < ctx_ax:
            travelers = [swap_head(block, 1), swap_head(near, 1)]
        else:
            travelers = []
        if r + 1 < ctx_ax:
            travelers.append(swap_head(ahead, 2))
        if r + 2 < ctx_ax:
            travelers.append(ring_send(ahead, 1))
            travelers.append(ring_send(rest[-1], 1))
        count = len(travelers)
        if r == ctx_ax - 2:
            line = in_order(rest, sources, shard)
            middle_row = line.shape[0] // 2
            travelers += [swap_head(line[:middle_row], 2), swap_seq(line)]
        if r == ctx_ax - 1:
            travelers += [swap_head(line[middle_row:], 2), swap_seq(x_first), swap_head(line, 1)]
        if r == ctx_ax:
            travelers += [swap_seq(x_second), swap_head(y_line, 1), swap_head(x_first, 1)]
        results = []
        if ready is not None:
            results = list(
                attend_forward(
                    r - 1,
                    r == ctx_ax,
                    counts,
                    lists,
                    slot_valid,
                    ready,
                    weights,
                    queries,
                    acc,
                    key_vals,
                )
            )
        tied = list(tie(*travelers, *results))
        extra, tied = tied[count : len(travelers)], tied[:count] + tied[len(travelers) :]
        if r == 0:
            weights, counts, lists, slot_valid = weights_here(packed)
        if r == ctx_ax - 2:
            x_first, y_line = extra
        if r == ctx_ax - 1:
            x_second, xy_first, core_line = extra
        if r == ctx_ax:
            xy_second, core_y, core_x_first = extra
            results = tied
            break
        planes.append([block, tied.pop(0), near, tied.pop(0)])
        ready = planes[-1]
        if r + 1 < ctx_ax:
            block, near = ahead, tied.pop(0)
        if r + 2 < ctx_ax:
            ahead = tied.pop(0)
            rest.append(tied.pop(0))
        if results:
            key_vals.append(tied.pop(0))
            if r == 1:
                queries = tied.pop(0)
            acc = tied.pop(0)
    key_vals.append(results[0])
    attended, exact, lse = results[1:]
    owns = [line, y_line, x_first, x_second, xy_first, xy_second]
    cores = [core_line, core_y, core_x_first]
    cores += [swap_head(v, 1) for v in (x_second, xy_first, xy_second)]
    offs = [((0, 1), 0, 0), ((0, 1), 0, 1), ((0,), 1, 0), ((1,), 1, 0), ((0,), 1, 1), ((1,), 1, 1)]
    me_x, me_core, me_seq = me_head // 2, me_head % 2, lax.axis_index("seq")
    pieces, places = [], []
    for core, arrays in enumerate((owns, cores)):
        for array, (halves, x, y) in zip(arrays, offs):
            pieces.append(array)
            places.append((halves, (me_x ^ x) * 2 + (me_core ^ core), y))
    reach = 2
    while reach < seq_ax:
        pieces += [swap_seq(array, reach) for array in pieces]
        places += [(halves, place, y ^ reach) for halves, place, y in places]
        reach *= 2
    if (ctx_ax // 2 * shard) % 8:
        pieces, places = join_halves(pieces, places, len(offs))
    starts = [
        ((me_seq ^ y) * heads_ax + place) * ctx_ax + half * (ctx_ax // 2)
        for halves, place, y in places
        for half in halves
    ]
    starts = jnp.stack(starts).astype(jnp.int32)

    merged = []
    for j in range(heads_ax):
        part = attended[:, :, j * tok_rows : (j + 1) * tok_rows].reshape(group, tok_rows)
        merged.append(swap_head(part, j) if j else part)

    marks = weights[:, 3 * LANES : 4 * LANES]
    groups = jnp.stack(order).astype(jnp.int32)
    output, grad_y_one, grad_z, h_two, hidden, grad_up, *rest_out = middle(
        starts, groups, merged, tokens, cotangent, marks, pieces, shard
    )
    grad_merged, sums_two, norms = rest_out[:4], rest_out[4], rest_out[5]

    grad_parts = [swap_head(p, j) if j else p for j, p in enumerate(grad_merged)]
    line = ctx_ax * shard
    outer = (seq_ax, 2, ctx_ax)
    me_bit = (me_head % 2)[None].astype(jnp.int32)
    keep, give = halves_of_down(line, me_bit, hidden, cotangent)
    shape = outer + (4 * shard, D)
    down_sum = (keep.reshape(shape), swap_head(give.reshape(shape), 1))
    h_two, keep, *_ = tie(h_two, down_sum[0])
    keep, give = halves_of_wide(line, me_bit, groups, h_two, grad_up, grad_z, merged)
    shape = outer + (shard, 5 * D)
    keep, give, *tied = tie(keep, give, *down_sum, *grad_parts)
    down_sum, grad_parts = sum_over_core(tied[:2]), tied[2:]
    grad_local = jnp.concatenate(grad_parts, axis=1).reshape(3, HDIM, heads_ax * tok_rows)
    wide_sum = (keep.reshape(shape), swap_head(give.reshape(shape), 1))
    down_sum = give_over_seq(down_sum)

    carry, traveling, near_half, far_half = (sums_two,), None, None, None
    for r in reversed(range(ctx_ax)):
        step = ctx_ax - 1 - r
        travelers = []
        if step >= 1:
            travelers.append(swap_head(far_half, 2))
        if step >= 2:
            travelers.append(ring_send(traveling, -1))
        count = len(travelers)
        if step == 0:
            travelers += [down_sum, wide_sum]
        if step == 1:
            travelers += [give_over_x(down_sum), give_over_seq(wide_sum)]
        if step == 2:
            travelers += [give_over_x(wide_sum)] + [send_term(down_sum, i) for i in (1, 2, 3)]
        if step == 3:
            travelers += [send_term(wide_sum, i) for i in (1, 2, 3)]
        keep, give, dw, fourth, sums = attend_backward(
            r,
            counts,
            lists,
            slot_valid,
            queries,
            key_vals[r],
            exact,
            lse,
            grad_local,
            weights,
            planes[r],
            carry,
            r == 0,
        )
        if r == 0:
            keep, give, dw, *travelers = tie(keep, give, dw, *travelers)
        else:
            keep, give, fourth, dw, sums, *travelers = tie(
                keep, give, fourth, dw, sums, *travelers
            )
        extra = travelers[count:]
        if step >= 1:
            moved = near_half.astype(F32) + travelers[0].astype(F32)
            if step >= 2:
                moved = moved + travelers[1].astype(F32)
            traveling = moved.astype(BF16)
        if step == 0:
            down_sum = sum_over_seq(extra[0])
            wide_sum = sum_over_core(extra[1])
        if step == 1:
            down_sum, wide_sum = sum_over_x(extra[0]), sum_over_seq(extra[1])
        if step == 2:
            wide_sum, down_terms = sum_over_x(extra[0]), list(extra[1:])
        if step == 3:
            wide_terms = list(extra)
        taken = swap_head(give, 1)
        near_half = (keep[0].astype(F32) + taken[0].astype(F32)).astype(BF16)
        far_half = (keep[1].astype(F32) + taken[1].astype(F32)).astype(BF16)
        if r:
            tied = [near_half, far_half, fourth, dw, sums, down_sum, wide_sum]
            tied += [traveling] if step >= 1 else []
            near_half, far_half, fourth, dw, sums, down_sum, wide_sum, *tied = tie(*tied)
            if step >= 1:
                traveling = tied[0]
        carry = (sums, fourth, dw)
    near_half, far_half, traveling = tie(near_half, far_half, traveling)
    dw_mine = give_over_seq(dw.reshape(seq_ax, heads_ax, ctx_ax, shard, wide))
    taken, carried, *dw_mine = tie(
        swap_head(far_half, 2), ring_send(traveling, -1), *dw_mine
    )
    dw_mine = sum_over_seq(dw_mine)
    grad_h_one = near_half.astype(F32) + taken.astype(F32) + carried.astype(F32)
    down_sum, wide_sum = sum_terms(down_sum, down_terms), sum_terms(wide_sum, wide_terms)
    up_sum, out_sum = wide_sum[:, : 4 * D], wide_sum[:, 4 * D :]
    dw_mine = sum_over_ctx(jnp.swapaxes(dw_mine, 0, 1)).astype(BF16)
    groups = []
    for j in range(heads_ax):
        part = lax.dynamic_index_in_dim(dw_mine, order[j], 0, keepdims=False)
        groups.append(swap_head(part, j) if j else part)
    groups = jnp.stack(groups)
    groups = jnp.stack(
        [lax.dynamic_index_in_dim(groups, o, 0, keepdims=False) for o in order]
    ).astype(F32)
    grad_w_qkv = jnp.swapaxes(groups[:, :, : 3 * group], 0, 1).reshape(shard, 3 * D)
    norm_sums = jnp.sum(groups[:, :, 3 * group : 3 * group + 4], axis=0)

    g_one = norms[0]
    ignored, unit_one, inv_one = norm_rows(tokens.astype(F32), g_one, norms[1])
    grad_tokens = (grad_y_one + norm_back(grad_h_one, unit_one, inv_one, g_one)).astype(BF16)
    return (
        output,
        grad_tokens,
        grad_w_qkv,
        out_sum,
        up_sum,
        down_sum,
        norm_sums[:, 0],
        norm_sums[:, 1],
        norm_sums[:, 2],
        norm_sums[:, 3],
    )


def solution(mesh):
    rows = P(ALL_AXES, None)
    vector = P(ALL_AXES)
    return jax.shard_map(
        body,
        mesh=mesh,
        in_specs=(rows, vector, rows, rows, rows, rows, vector, vector, vector, vector, rows),
        out_specs=(rows, rows, rows, rows, rows, rows, vector, vector, vector, vector),
        check_vma=False,
    )
```
